32 devices in a mesh: dp: 8 (over z, x), seq: 4 (over y, core).
Axes of the slice: x: 2, y: 2, z: 4, core: 2. Of those that a mesh axis runs over, the one named last changes fastest.
Arguments:
- tokens: bfloat16 [16384, 1024], P(('dp', 'seq')), may hold values from -6 to 6
- time_embed: bfloat16 [32, 1024], P(('dp', 'seq')), may hold values from -6 to 6
- lengths: int32 [32], P('dp'), may hold values from 0 to 475, as said below
- cotangent: bfloat16 [16384, 1024], P(('dp', 'seq')), may hold values from -6 to 6
- w_query: bfloat16 [1024, 1024], P('seq'), may hold values from -0.1875 to 0.1875
- w_key: bfloat16 [1024, 1024], P('seq'), may hold values from -0.1875 to 0.1875
- w_value: bfloat16 [1024, 1024], P('seq'), may hold values from -0.1875 to 0.1875
- w_out: bfloat16 [1024, 1024], P('seq'), may hold values from -0.75 to 0.75
- w_time: bfloat16 [1024, 1024], P('seq'), may hold values from -0.1875 to 0.1875
- w_in: bfloat16 [4096, 1024], P('seq'), may hold values from -0.1875 to 0.1875
- w_down: bfloat16 [4096, 1024], P('seq'), may hold values from -0.09375 to 0.09375
- b_query: bfloat16 [1024], replicated, may hold values from -3 to 3
- b_value: bfloat16 [1024], replicated, may hold values from -3 to 3
- b_out: bfloat16 [1024], replicated, may hold values from -3 to 3
- b_time: bfloat16 [1024], replicated, may hold values from -3 to 3
- b_in: bfloat16 [4096], replicated, may hold values from -3 to 3
- b_down: bfloat16 [1024], replicated, may hold values from -2 to 2
- gain_one: bfloat16 [1024], replicated, may hold values from 0.25 to 1.75
- shift_one: bfloat16 [1024], replicated, may hold values from -2 to 2
- gain_two: bfloat16 [1024], replicated, may hold values from 0.25 to 1.75
- shift_two: bfloat16 [1024], replicated, may hold values from -2 to 2
Outputs:
- layer_out: bfloat16 [16384, 1024], P(('dp', 'seq'))
- grad_tokens: bfloat16 [16384, 1024], P(('dp', 'seq'))
- grad_w_query: float32 [1024, 1024], P('seq')
- grad_w_key: float32 [1024, 1024], P('seq')
- grad_w_value: float32 [1024, 1024], P('seq')
- grad_w_out: float32 [1024, 1024], P('seq')
- grad_w_time: float32 [1024, 1024], P('seq')
- grad_w_in: float32 [4096, 1024], P('seq')
- grad_w_down: float32 [4096, 1024], P('seq')
- grad_b_query: float32 [1024], replicated
- grad_b_value: float32 [1024], replicated
- grad_b_out: float32 [1024], replicated
- grad_b_time: float32 [1024], replicated
- grad_b_in: float32 [4096], replicated
- grad_b_down: float32 [1024], replicated
- grad_gain_one: float32 [1024], replicated
- grad_shift_one: float32 [1024], replicated
- grad_gain_two: float32 [1024], replicated
- grad_shift_two: float32 [1024], replicated
The draws below stay inside these ranges and needn't reach their ends.
Inputs may be any that keep to these rules, and one draw needn't show every extreme that they name: Item i's valid slots are its first lengths[i] + 25; every draw has an item of length 475 and one of length 0.
All inputs are finite; a program needn't handle non-finite values.
Results may differ from the reference program's by a relative error of at most 0.02.
Values may be sent and summed in bfloat16 or wider, within the bound.
A program may use at most 256 MiB of HBM per device.

```python
import math
import jax
import jax.numpy as jnp
from jax import lax

D = 1024
HEADS = 16
HEAD_DIM = 64
FF = 4096
SLOTS = 512
BLOCK = 25
CTX_MAX = 475
ITEMS = 32
TOKENS = 16384


def draw_lengths(key, part):
    key_values = jax.random.fold_in(key, 11)
    key_chosen = jax.random.fold_in(key, 23)
    values = jax.random.randint(key_values, (ITEMS,), 0, CTX_MAX + 1)
    chosen = jax.random.permutation(key_chosen, ITEMS)
    values = values.at[chosen[0]].set(CTX_MAX)
    values = values.at[chosen[1]].set(0)
    return values.astype(jnp.int32)


def strengthened(result, own_key, source, target, parts, factor):
    owner, partner = [(jnp.arange(result.shape[axis_at]) // (result.shape[axis_at] // parts)).reshape([-1 if axis == axis_at else 1 for axis in range(result.ndim)]) for axis_at in (source, target)]
    chosen = jax.random.permutation(own_key, parts)[partner]
    strong = (owner == chosen) | (owner == (partner + parts // 2) % parts)
    return jnp.where(strong, factor * result, result)


def steps_of(own_key, dims, pieces, low, high):
    level, own = 1.0, jax.random.fold_in(own_key, 6)
    for axis_at, parts in pieces:
        draws = jnp.exp(jax.random.uniform(jax.random.fold_in(own, axis_at), (parts,), jnp.float32, low / len(pieces), high / len(pieces)))
        level = level * jnp.repeat(draws, dims[axis_at] // parts).reshape([-1 if axis == axis_at else 1 for axis in range(len(dims))])
    return level


def bell_draw(rng, shape, scale, limit, cuts=(), dtype=jnp.bfloat16):
    drawn = jax.random.normal(rng, shape, jnp.float32) * scale
    if len(cuts) > 0:
        drawn = steps_of(rng, shape, cuts, -0.22, 0.18) * drawn
    return jnp.clip(drawn, min=-limit, max=limit).astype(dtype)


def bell_draw_with(rng, shape, deviation, bound, cuts, heavy, dtype=jnp.bfloat16):
    entries = deviation * jax.random.normal(rng, shape, jnp.float32)
    if cuts:
        entries = entries * steps_of(rng, shape, cuts, -0.22, 0.18)
    return jnp.clip(strengthened(entries, jax.random.fold_in(rng, 3), *heavy), -bound, bound).astype(dtype)


def setup_inputs(seed: int = 0) -> dict:
    key_list = jax.random.split(jax.random.key(seed), 22)
    return {
        "tokens": bell_draw(key_list[0], (TOKENS, D), 1.0, 6.0, ((0, 32),)),
        "time_embed": bell_draw(key_list[1], (ITEMS, D), 1.0, 6.0, ((0, 32),)),
        "lengths": draw_lengths(jax.random.fold_in(key_list[21], 71), 0),
        "cotangent": bell_draw_with(key_list[3], (TOKENS, D), 1.0, 6.0, ((0, 32),), (0, 1, 32, 2.75)),
        "w_query": bell_draw(key_list[4], (D, D), D ** -0.5, 0.1875, ((0, 4),)),
        "w_key": bell_draw(key_list[5], (D, D), D ** -0.5, 0.1875, ((0, 4),)),
        "w_value": bell_draw(key_list[6], (D, D), D ** -0.5, 0.1875, ((0, 4),)),
        "w_out": bell_draw(key_list[7], (D, D), (D // 16) ** -0.5, 0.75, ((0, 4),)),
        "w_time": bell_draw(key_list[8], (D, D), D ** -0.5, 0.1875, ((0, 4),)),
        "w_in": bell_draw(key_list[9], (FF, D), D ** -0.5, 0.1875, ((0, 4),)),
        "w_down": bell_draw(key_list[10], (FF, D), FF ** -0.5, 0.09375, ((0, 4),)),
        "b_query": bell_draw(key_list[11], (D,), 0.5, 3.0),
        "b_value": bell_draw(key_list[12], (D,), 0.5, 3.0),
        "b_out": bell_draw(key_list[13], (D,), 0.5, 3.0),
        "b_time": bell_draw(key_list[14], (D,), 0.5, 3.0),
        "b_in": bell_draw(key_list[15], (FF,), 0.5, 3.0),
        "b_down": bell_draw(key_list[16], (D,), 0.3, 2.0),
        "gain_one": jnp.clip(1.0 + 0.15 * jax.random.normal(key_list[17], (D,), jnp.float32), 0.25, 1.75).astype(jnp.bfloat16),
        "shift_one": bell_draw(key_list[18], (D,), 0.3, 2.0),
        "gain_two": jnp.clip(1.0 + 0.15 * jax.random.normal(key_list[19], (D,), jnp.float32), 0.25, 1.75).astype(jnp.bfloat16),
        "shift_two": bell_draw(key_list[20], (D,), 0.3, 2.0),
    }


@jax.custom_vjp
def low(v):
    return lax.optimization_barrier(v.astype(jnp.bfloat16)).astype(jnp.float32)

@jax.custom_vjp
def low_back(v):
    return v

def low_keep(v):
    return (low(v), None)

def low_pass(kept, grad):
    return (grad,)

def back_keep(v):
    return (v, None)

def back_low(kept, grad):
    return (low(grad),)
low.defvjp(low_keep, low_pass)
low_back.defvjp(back_keep, back_low)
highest = lax.Precision.HIGHEST
norm_eps = 1e-05
neg_large = -1e+30

def product(left, right):
    return jnp.dot(left, right, precision=highest, preferred_element_type=jnp.float32)

def layer_norm(values, gain, shift):
    center = values - lax.optimization_barrier(jnp.mean(values, axis=-1, keepdims=True))
    spread = lax.rsqrt(lax.optimization_barrier(jnp.mean(center * center, axis=-1, keepdims=True)) + norm_eps)
    return center * spread * gain + shift

def attend_item(packed):
    queries, key_rows, value_rows, key_valid = packed
    query_heads = queries.reshape(SLOTS, HEADS, HEAD_DIM)
    key_heads = key_rows.reshape(SLOTS, HEADS, HEAD_DIM)
    value_heads = value_rows.reshape(SLOTS, HEADS, HEAD_DIM)
    scores = jnp.einsum('qhd,khd->hqk', query_heads, key_heads, precision=highest) * HEAD_DIM ** (-0.5)
    scores = low_back(scores)
    masked = jnp.where(key_valid[None, None, :], scores, neg_large)
    shifted = masked - lax.optimization_barrier(jnp.max(masked, axis=-1, keepdims=True))
    exp_scores = jnp.exp(shifted)
    soft_weights = low(exp_scores / lax.optimization_barrier(jnp.sum(exp_scores, axis=-1, keepdims=True)))
    mixed_heads = jnp.einsum('hqk,khd->qhd', soft_weights, value_heads, precision=highest)
    return mixed_heads.reshape(SLOTS, HEADS * HEAD_DIM)

def forward_block(params, packed):
    w_query, w_key, w_value, w_out, w_time, w_in, w_down, b_query, b_value, b_out, b_time, b_in, b_down, gain_one, shift_one, gain_two, shift_two = params
    token_rows, time_rows, item_lengths = packed
    per_block = time_rows.shape[0]
    time_proj = low_back(product(time_rows, w_time) + b_time)
    resid = (token_rows.reshape(per_block, SLOTS, D) + time_proj[:, None, :]).reshape(per_block * SLOTS, D)
    resid_low = low(resid)
    queries = low_back(low(product(resid_low, w_query) + b_query))
    key_rows = low_back(low(product(resid_low, w_key)))
    value_rows = low_back(low(product(resid_low, w_value) + b_value))
    slot_index = lax.broadcasted_iota(jnp.int32, (per_block, SLOTS), 1)
    key_valid = slot_index < item_lengths[:, None].astype(jnp.int32) + BLOCK
    mixed_rows = lax.map(jax.checkpoint(attend_item), (queries.reshape(per_block, SLOTS, D), key_rows.reshape(per_block, SLOTS, D), value_rows.reshape(per_block, SLOTS, D), key_valid))
    mixed_rows = low_back(low(mixed_rows.reshape(per_block * SLOTS, D)))
    attn_out = low_back(product(mixed_rows, w_out) + b_out)
    first_norm = layer_norm(resid + attn_out, gain_one, shift_one)
    first_low = low(first_norm)
    hidden_pre = low_back(product(first_low, w_in.T) + b_in)
    hidden_low = low(jax.nn.gelu(hidden_pre, approximate=False))
    ffn_out = low_back(product(hidden_low, w_down) + b_down)
    second_norm = layer_norm(first_norm + ffn_out, gain_two, shift_two)
    return second_norm * key_valid.reshape(per_block * SLOTS, 1).astype(jnp.float32)

def forward_all(params, token_rows, time_rows, item_lengths):
    per_block = math.gcd(ITEMS, 8)
    blocks = ITEMS // per_block
    packed = (token_rows.reshape(blocks, per_block * SLOTS, D), time_rows.reshape(blocks, per_block, D), item_lengths.reshape(blocks, per_block))
    block_step = jax.checkpoint(forward_block)

    def run_block(item):
        return block_step(params, item)
    outputs = lax.map(run_block, packed)
    return outputs.reshape(ITEMS * SLOTS, D)

def reference(tokens, time_embed, lengths, cotangent, w_query, w_key, w_value, w_out, w_time, w_in, w_down, b_query, b_value, b_out, b_time, b_in, b_down, gain_one, shift_one, gain_two, shift_two):
    params = (w_query.astype(jnp.float32), w_key.astype(jnp.float32), w_value.astype(jnp.float32), w_out.astype(jnp.float32), w_time.astype(jnp.float32), w_in.astype(jnp.float32), w_down.astype(jnp.float32), b_query.astype(jnp.float32), b_value.astype(jnp.float32), b_out.astype(jnp.float32), b_time.astype(jnp.float32), b_in.astype(jnp.float32), b_down.astype(jnp.float32), gain_one.astype(jnp.float32), shift_one.astype(jnp.float32), gain_two.astype(jnp.float32), shift_two.astype(jnp.float32))
    time_rows = time_embed.astype(jnp.float32)

    def run_forward(param_set, token_rows):
        return forward_all(param_set, token_rows, time_rows, lengths)
    outputs, pullback = jax.vjp(run_forward, params, tokens.astype(jnp.float32))
    grad_params, grad_rows = pullback(cotangent.astype(jnp.float32))
    grad_w_query, grad_w_key, grad_w_value, grad_w_out, grad_w_time, grad_w_in, grad_w_down, grad_b_query, grad_b_value, grad_b_out, grad_b_time, grad_b_in, grad_b_down, grad_gain_one, grad_shift_one, grad_gain_two, grad_shift_two = grad_params
    return (outputs.astype(jnp.bfloat16), grad_rows.astype(jnp.bfloat16), grad_w_query, grad_w_key, grad_w_value, grad_w_out, grad_w_time, grad_w_in, grad_w_down, grad_b_query, grad_b_value, grad_b_out, grad_b_time, grad_b_in, grad_b_down, grad_gain_one, grad_shift_one, grad_gain_two, grad_shift_two)
```

```python
import jax
import jax.numpy as jnp
from jax import lax
from jax.sharding import PartitionSpec as P

HEAD_DIM = 64
BLOCK = 25


norm_eps = 1e-05
neg_large = -1e30


def layer_norm(values, gain, shift):
    center = values - jnp.mean(values, axis=-1, keepdims=True)
    spread = lax.rsqrt(jnp.mean(center * center, axis=-1, keepdims=True) + norm_eps)
    return center * spread * gain + shift


def exact_gelu(values):
    return jax.nn.gelu(values, approximate=False)


def split_heads(rows):
    return rows.reshape(rows.shape[0], rows.shape[1] // HEAD_DIM, HEAD_DIM)


def item_scores(queries, keys, key_valid):
    scores = jnp.einsum(
        "qhd,khd->hqk", split_heads(queries), split_heads(keys), preferred_element_type=jnp.float32
    ) * HEAD_DIM ** (-0.5)
    return jnp.where(key_valid[None, None, :], scores, neg_large)


def attend_forward(queries, keys, values, key_valid):
    masked = item_scores(queries, keys, key_valid)
    row_max = jnp.max(masked, axis=-1, keepdims=True)
    exp_scores = jnp.exp(masked - row_max)
    row_total = jnp.sum(exp_scores, axis=-1, keepdims=True)
    soft = (exp_scores / row_total).astype(jnp.bfloat16)
    mixed = jnp.einsum(
        "hqk,khd->qhd", soft, split_heads(values), preferred_element_type=jnp.float32
    )
    log_total = row_max[:, :, 0] + jnp.log(row_total[:, :, 0])
    return mixed.reshape(queries.shape).astype(jnp.bfloat16), log_total


def attend_backward(queries, keys, values, key_valid, log_total, grad_mixed):
    masked = item_scores(queries, keys, key_valid)
    soft = jnp.exp(masked - log_total[:, :, None])
    grad_heads = split_heads(grad_mixed)
    grad_value = jnp.einsum(
        "hqk,qhd->khd", soft.astype(jnp.bfloat16), grad_heads, preferred_element_type=jnp.float32
    )
    grad_soft = jnp.einsum(
        "qhd,khd->hqk", grad_heads, split_heads(values), preferred_element_type=jnp.float32
    )
    grad_scores = soft * (grad_soft - jnp.sum(soft * grad_soft, axis=-1, keepdims=True))
    scores_low = grad_scores.astype(jnp.bfloat16)
    scale = HEAD_DIM ** (-0.5)
    grad_query = scale * jnp.einsum(
        "hqk,khd->qhd", scores_low, split_heads(keys), preferred_element_type=jnp.float32
    )
    grad_key = scale * jnp.einsum(
        "hqk,qhd->khd", scores_low, split_heads(queries), preferred_element_type=jnp.float32
    )
    return tuple(
        grad.reshape(queries.shape).astype(jnp.bfloat16)
        for grad in (grad_query, grad_key, grad_value)
    )


def per_item(fn, item_count, slot_count, *arrays):
    if item_count == 1:
        return fn(*[a[0] for a in arrays])
    outs = lax.map(lambda packed: fn(*packed), arrays)
    return outs


def local(
    tokens,
    time_embed,
    lengths,
    cotangent,
    w_query,
    w_key,
    w_value,
    w_out,
    w_time,
    w_in,
    w_down,
    b_query,
    b_value,
    b_out,
    b_time,
    b_in,
    b_down,
    gain_one,
    shift_one,
    gain_two,
    shift_two,
):
    f32, bf16 = jnp.float32, jnp.bfloat16
    seq_rank = lax.axis_index("seq")
    item_count = time_embed.shape[0]
    token_count = tokens.shape[0]
    slot_count = token_count // item_count
    width = tokens.shape[1]
    rows = w_time.shape[0]

    def mm(a, b, dims):
        return lax.dot_general(a, b, (dims, ((), ())), preferred_element_type=f32)

    def gather(a):
        return lax.all_gather(a, "seq", axis=0, tiled=True)

    def scatter_sum(a):
        return lax.psum_scatter(a, "seq", scatter_dimension=0, tiled=True)

    full_time, full_query, full_key, full_value, full_out = (
        gather(w_time),
        gather(w_query),
        gather(w_key),
        gather(w_value),
        gather(w_out),
    )
    own_lengths = lax.dynamic_slice_in_dim(lengths, seq_rank * item_count, item_count, 0)
    slot_index = lax.broadcasted_iota(jnp.int32, (item_count, slot_count), 1)
    own_valid = slot_index < own_lengths[:, None] + BLOCK
    row_keep = own_valid.reshape(token_count, 1).astype(f32)
    time_proj = mm(time_embed, full_time, ((1,), (0,))) + b_time.astype(f32)
    resid = (tokens.reshape(item_count, slot_count, width) + time_proj[:, None, :]).reshape(
        token_count, width
    )
    resid_low = resid.astype(bf16)
    query_rows = (mm(resid_low, full_query, ((1,), (0,))) + b_query.astype(f32)).astype(bf16)
    key_rows = mm(resid_low, full_key, ((1,), (0,))).astype(bf16)
    value_rows = (mm(resid_low, full_value, ((1,), (0,))) + b_value.astype(f32)).astype(bf16)

    def split_items(a):
        return a.reshape(item_count, slot_count, -1)

    qkv = [split_items(a) for a in (query_rows, key_rows, value_rows)]
    mixed, log_total = per_item(attend_forward, item_count, slot_count, *qkv, own_valid)
    mixed_rows = mixed.reshape(token_count, width)
    attn_out = mm(mixed_rows, full_out, ((1,), (0,))) + b_out.astype(f32)
    first_norm, first_pull = jax.vjp(
        layer_norm, resid + attn_out, gain_one.astype(f32), shift_one.astype(f32)
    )
    first_group = gather(first_norm.astype(bf16))
    bias_in = lax.dynamic_slice_in_dim(b_in, seq_rank * w_in.shape[0], w_in.shape[0], 0)
    hidden_pre = mm(first_group, w_in, ((1,), (1,))) + bias_in.astype(f32)
    hidden, gelu_pull = jax.vjp(exact_gelu, hidden_pre)
    hidden_low = hidden.astype(bf16)
    ffn_part = mm(hidden_low, w_down, ((1,), (0,))).astype(bf16)
    ffn_out = scatter_sum(ffn_part).astype(f32) + b_down.astype(f32)
    second_norm, second_pull = jax.vjp(
        layer_norm, first_norm + ffn_out, gain_two.astype(f32), shift_two.astype(f32)
    )
    layer_out = (second_norm * row_keep).astype(bf16)
    grad_second_in, grad_gain_two, grad_shift_two = second_pull(cotangent.astype(f32) * row_keep)
    grad_ffn = grad_second_in.astype(bf16)
    grad_group = gather(grad_ffn)
    grad_hidden = mm(grad_group, w_down, ((1,), (1,)))
    grad_pre = gelu_pull(grad_hidden)[0].astype(bf16)
    back_part = mm(grad_pre, w_in, ((1,), (0,))).astype(bf16)
    grad_first = grad_second_in + scatter_sum(back_part).astype(f32)
    term_in = mm(grad_pre, first_group, ((0,), (0,))).astype(bf16)
    term_down = mm(hidden_low, grad_group, ((0,), (0,))).astype(bf16)
    sum_ffn = lax.psum(jnp.concatenate([term_in, term_down], axis=0), "dp").astype(f32)
    grad_first_in, grad_gain_one, grad_shift_one = first_pull(grad_first)
    grad_attn = grad_first_in.astype(bf16)
    grad_mixed = mm(grad_attn, full_out, ((1,), (1,))).astype(bf16)
    if item_count == 1:
        extra = (log_total[None], split_items(grad_mixed))
    else:
        extra = (log_total, split_items(grad_mixed))
    grad_query, grad_key, grad_value = (
        a.reshape(token_count, width)
        for a in per_item(attend_backward, item_count, slot_count, *qkv, own_valid, *extra)
    )
    grad_resid = (
        grad_first_in
        + mm(grad_query, full_query, ((1,), (1,)))
        + mm(grad_key, full_key, ((1,), (1,)))
        + mm(grad_value, full_value, ((1,), (1,)))
    )
    grad_tokens = grad_resid.astype(bf16)
    grad_time = jnp.sum(grad_resid.reshape(item_count, slot_count, width), axis=1).astype(bf16)
    terms = [
        mm(resid_low, grad_query, ((0,), (0,))),
        mm(resid_low, grad_key, ((0,), (0,))),
        mm(resid_low, grad_value, ((0,), (0,))),
        mm(mixed_rows, grad_attn, ((0,), (0,))),
    ]
    group = w_out.shape[0]
    stacked = jnp.stack([t.astype(bf16).reshape(-1, group, width) for t in terms], axis=1)
    share = scatter_sum(stacked.reshape(-1, width))
    sum_attn = lax.psum(share, "dp").astype(f32)
    small = jnp.concatenate(
        [
            jnp.stack(
                [
                    jnp.sum(grad_query, axis=0, dtype=f32),
                    jnp.sum(grad_value, axis=0, dtype=f32),
                    jnp.sum(grad_attn, axis=0, dtype=f32),
                    jnp.sum(grad_ffn, axis=0, dtype=f32),
                    grad_gain_one,
                    grad_shift_one,
                    grad_gain_two,
                    grad_shift_two,
                ]
            ).astype(bf16),
            jnp.sum(grad_pre, axis=0, dtype=f32).reshape(-1, width).astype(bf16),
            time_embed,
            grad_time,
        ],
        axis=0,
    )
    every = lax.all_gather(small, ("dp", "seq"), axis=0)
    vectors = jnp.sum(every[:, :8], axis=0, dtype=f32)
    hidden_rows = every.shape[1] - 8 - 2 * item_count
    in_parts = every[:, 8 : 8 + hidden_rows].reshape(-1, b_in.shape[0])
    grad_b_in = jnp.sum(in_parts, axis=0, dtype=f32)
    time_rows = every[:, 8 + hidden_rows : 8 + hidden_rows + item_count].reshape(-1, width)
    time_grads = every[:, 8 + hidden_rows + item_count :].reshape(-1, width)
    own_columns = lax.dynamic_slice_in_dim(time_rows, seq_rank * rows, rows, 1)
    grad_w_time = mm(own_columns, time_grads, ((0,), (0,)))
    grad_b_time = jnp.sum(time_grads, axis=0, dtype=f32)
    return (
        layer_out,
        grad_tokens,
        sum_attn[:group],
        sum_attn[group : 2 * group],
        sum_attn[2 * group : 3 * group],
        sum_attn[3 * group :],
        grad_w_time,
        sum_ffn[: w_in.shape[0]],
        sum_ffn[w_in.shape[0] :],
        vectors[0],
        vectors[1],
        vectors[2],
        grad_b_time,
        grad_b_in,
        vectors[3],
        vectors[4],
        vectors[5],
        vectors[6],
        vectors[7],
    )


def solution(mesh):
    in_specs = (
        P(("dp", "seq"), None),
        P(("dp", "seq"), None),
        P("dp"),
        P(("dp", "seq"), None),
        P("seq", None),
        P("seq", None),
        P("seq", None),
        P("seq", None),
        P("seq", None),
        P("seq", None),
        P("seq", None),
        P(),
        P(),
        P(),
        P(),
        P(),
        P(),
        P(),
        P(),
        P(),
        P(),
    )
    out_specs = (
        P(("dp", "seq"), None),
        P(("dp", "seq"), None),
        P("seq", None),
        P("seq", None),
        P("seq", None),
        P("seq", None),
        P("seq", None),
        P("seq", None),
        P("seq", None),
        P(),
        P(),
        P(),
        P(),
        P(),
        P(),
        P(),
        P(),
        P(),
        P(),
    )
    return jax.shard_map(local, mesh=mesh, in_specs=in_specs, out_specs=out_specs, check_vma=False)
```

```python
import functools

import jax
import jax.numpy as jnp
from jax import lax
from jax.experimental import pallas as pl
from jax.experimental.pallas import tpu as pltpu
from jax.sharding import PartitionSpec as P

HEAD_DIM = 64
BLOCK = 25
MESH = pl.DeviceIdType.MESH


norm_eps = 1e-05
neg_large = -1e30


def layer_norm(values, gain, shift):
    center = values - jnp.mean(values, axis=-1, keepdims=True)
    spread = lax.rsqrt(jnp.mean(center * center, axis=-1, keepdims=True) + norm_eps)
    return center * spread * gain + shift


def exact_gelu(values):
    return jax.nn.gelu(values, approximate=False)


def _gather_kernel(sizes, *refs):
    n = len(sizes)
    ins, outs = refs[:n], refs[n : 2 * n]
    own_sem, c_send, c_recv, y_send, y_recv, x_send, x_recv, f_send, f_recv, g_send, g_recv = refs[2 * n :]
    dp, me = lax.axis_index("dp"), lax.axis_index("seq")
    half = lax.rem(dp, 2)
    core, across, side = (dp, me ^ 1), (dp, me ^ 2), (dp ^ 1, me)
    barrier = pltpu.get_barrier_semaphore()
    for peer in (core, across, side):
        pl.semaphore_signal(barrier, inc=1, device_id=peer, device_id_type=MESH)
    pl.semaphore_wait(barrier, 3)

    def remote(src, dst, send, recv, peer):
        return pltpu.make_async_remote_copy(
            src_ref=src, dst_ref=dst, send_sem=send, recv_sem=recv, device_id=peer, device_id_type=MESH
        )

    chunks = []
    for a, rows in enumerate(sizes):
        step = min(rows // 2, 256)
        chunks += [(a, rows, off, step) for off in range(0, rows // 2, step)]

    def region(ref, rows, shard, part, off, step):
        start = pl.multiple_of(shard * rows + part * (rows // 2) + off, 16)
        return ref.at[pl.ds(start, step), :]

    waits = []
    crossing = []
    for j, (a, rows, off, step) in enumerate(chunks):
        src = region(ins[a], rows, 0, half, off, step)
        copy = remote(src, region(outs[a], rows, me, half, off, step), y_send.at[j], y_recv.at[j], across)
        copy.start()
        crossing.append(copy)
    core_copies = []
    for a, rows in enumerate(sizes):
        home = outs[a].at[pl.ds(pl.multiple_of(me * rows, 16), rows), :]
        copy = remote(ins[a], home, c_send.at[a], c_recv.at[a], core)
        copy.start()
        core_copies.append(copy)
        keep = pltpu.make_async_copy(ins[a], home, own_sem.at[a])
        keep.start()
        waits.append(keep)
    sides, firsts, seconds = [], [], []
    for j in range(len(chunks) + 1):
        if j < len(chunks):
            a, rows, off, step = chunks[j]
            crossing[j].wait_recv()
            got = region(outs[a], rows, me ^ 2, half, off, step)
            copy = remote(got, got, x_send.at[j], x_recv.at[j], side)
            copy.start()
            sides.append(copy)
            copy = remote(got, got, f_send.at[j], f_recv.at[j], core)
            copy.start()
            firsts.append(copy)
        if j >= 1:
            a, rows, off, step = chunks[j - 1]
            sides[j - 1].wait_recv()
            got = region(outs[a], rows, me ^ 2, 1 - half, off, step)
            copy = remote(got, got, g_send.at[j - 1], g_recv.at[j - 1], core)
            copy.start()
            seconds.append(copy)
    for copy in waits:
        copy.wait()
    for copy in crossing + sides:
        copy.wait_send()
    for copy in core_copies + firsts + seconds:
        copy.wait()


def gather_weights(arrays):
    sizes = tuple(a.shape[0] for a in arrays)
    n = len(arrays)
    m = sum(max(1, r // 512) for r in sizes)
    dma = pltpu.SemaphoreType.DMA
    return pl.pallas_call(
        functools.partial(_gather_kernel, sizes),
        out_shape=[jax.ShapeDtypeStruct((4 * a.shape[0], a.shape[1]), a.dtype) for a in arrays],
        in_specs=[pl.BlockSpec(memory_space=pltpu.VMEM)] * n,
        out_specs=[pl.BlockSpec(memory_space=pl.ANY)] * n,
        scratch_shapes=[dma((n,))] * 3 + [dma((m,))] * 8,
        compiler_params=pltpu.CompilerParams(
            collective_id=0, has_side_effects=True, vmem_limit_bytes=32 << 20
        ),
        name="gather_weights",
    )(*arrays)


def _row_loop(rows, step, body):
    def run(i, carry):
        body(pl.ds(pl.multiple_of(i * step, step), step))
        return carry

    lax.fori_loop(0, rows // step, run, 0)


def _reduce_kernel(dp_n, slab, terms, vec, rec, out, vec_out, rec_out, *scr):
    (own, core_in, y_in, x_in, z_in, res, v_core, v_y, v_x, v_z, v_sum) = scr[:11]
    (load_sem, c_s, c_r, y_s, y_r, x_s, x_r, z_s, z_r, zg_s, zg_r, xg_s, xg_r, out_sem, vs, vr, ws, wr) = scr[11:]
    f32, bf16 = jnp.float32, jnp.bfloat16
    count = out.shape[0] // slab
    nz = dp_n // 2
    dp, me = lax.axis_index("dp"), lax.axis_index("seq")
    x, z, y, c = lax.rem(dp, 2), lax.div(dp, 2), lax.div(me, 2), lax.rem(me, 2)
    core, across, side = (dp, me ^ 1), (dp, me ^ 2), (dp ^ 1, me)
    others = [(lax.rem(z + o, nz) * 2 + x, me) for o in range(1, nz)]
    barrier = pltpu.get_barrier_semaphore()
    for peer in [core, across, side] + others:
        pl.semaphore_signal(barrier, inc=1, device_id=peer, device_id_type=MESH)
    pl.semaphore_wait(barrier, 3 + len(others))

    def remote(src, dst, send, recv, peer):
        copy = pltpu.make_async_remote_copy(
            src_ref=src, dst_ref=dst, send_sem=send, recv_sem=recv, device_id=peer, device_id_type=MESH
        )
        copy.start()
        return copy

    hs = slab // 2
    ps = hs // nz
    rs = min(ps, 32)
    loads, core_c, y_c, x_c, z_c, zg_c, xg_c, outs = [], [], [], [], [], [], [], []

    for k in range(count):
        rows = pl.ds(k * slab, slab)
        core_c.append(remote(terms.at[:, 1 - c, rows, :], core_in.at[k], c_s.at[k], c_r.at[k], core))
        load = pltpu.make_async_copy(terms.at[:, c, rows, :], own.at[k], load_sem.at[k])
        load.start()
        loads.append(load)

    small = [remote(vec, v_core, vs.at[0], vr.at[0], core)]
    rec_out[dp, me] = rec[...]
    small_rec = [remote(rec_out.at[dp, me], rec_out.at[dp, me], ws.at[0], wr.at[0], core)]

    def stage_core(k):
        loads[k].wait()
        core_c[k].wait_recv()

        def add(r):
            for p in range(2):
                own[k, p, r] = (own[k, p, r].astype(f32) + core_in[k, p, r].astype(f32)).astype(bf16)

        _row_loop(slab, 16, add)
        y_c.append(remote(own.at[k, 1 - y], y_in.at[k], y_s.at[k], y_r.at[k], across))

    def stage_y(k):
        y_c[k].wait_recv()

        def add(r):
            own[k, y, r] = (own[k, y, r].astype(f32) + y_in[k, r].astype(f32)).astype(bf16)

        _row_loop(slab, 32, add)
        give = pl.ds(pl.multiple_of((1 - x) * hs, 16), hs)
        x_c.append(remote(own.at[k, y, give], x_in.at[k], x_s.at[k], x_r.at[k], side))

    def stage_x(k):
        x_c[k].wait_recv()

        def add(r):
            at = pl.ds(pl.multiple_of(x * hs + r.start, 16), r.size)
            own[k, y, at] = (own[k, y, at].astype(f32) + x_in[k, r].astype(f32)).astype(bf16)

        _row_loop(hs, rs, add)
        copies = []
        for o in range(1, nz):
            piece = pl.ds(pl.multiple_of(x * hs + lax.rem(z + o, nz) * ps, 16), ps)
            copies.append(
                remote(own.at[k, y, piece], z_in.at[k, o], z_s.at[k, o], z_r.at[k, o], others[o - 1])
            )
        z_c.append(copies)

    def stage_z(k):
        for copy in z_c[k]:
            copy.wait_recv()

        def add(r):
            at = pl.ds(pl.multiple_of(x * hs + z * ps + r.start, 16), r.size)
            total = own[k, y, at].astype(f32)
            for o in range(1, nz):
                total += z_in[k, o, r].astype(f32)
            res[k, at] = total.astype(bf16)

        _row_loop(ps, rs, add)
        mine = res.at[k, pl.ds(pl.multiple_of(x * hs + z * ps, 16), ps)]
        zg_c.append(
            [remote(mine, mine, zg_s.at[k, o], zg_r.at[k, o], others[o - 1]) for o in range(1, nz)]
        )

    def stage_zg(k):
        for copy in zg_c[k]:
            copy.wait_recv()
        mine = res.at[k, pl.ds(pl.multiple_of(x * hs, 16), hs)]
        xg_c.append(remote(mine, mine, xg_s.at[k], xg_r.at[k], side))

    def stage_xg(k):
        xg_c[k].wait_recv()
        copy = pltpu.make_async_copy(res.at[k], out.at[pl.ds(k * slab, slab), :], out_sem.at[k])
        copy.start()
        outs.append(copy)

    def small_stage(t):
        if t == 0:
            small[0].wait_recv()
            v_sum[0] = vec[...] + v_core[...]
            small.append(remote(v_sum.at[0], v_y, vs.at[1], vr.at[1], across))
            small_rec[0].wait_recv()
            pair = rec_out.at[dp, pl.ds(y * 2, 2)]
            small_rec.append(remote(pair, pair, ws.at[1], wr.at[1], across))
        elif t == 1:
            small[1].wait_recv()
            v_sum[1] = v_sum[0] + v_y[...]
            small.append(remote(v_sum.at[1], v_x, vs.at[2], vr.at[2], side))
            small_rec[1].wait_recv()
            quad = rec_out.at[dp]
            small_rec.append(remote(quad, quad, ws.at[2], wr.at[2], side))
        elif t == 2:
            small[2].wait_recv()
            v_sum[2] = v_sum[1] + v_x[...]
            small_rec[2].wait_recv()
            pair = rec_out.at[pl.ds(z * 2, 2)]
            for o in range(1, nz):
                small.append(remote(v_sum.at[2], v_z.at[o], vs.at[2 + o], vr.at[2 + o], others[o - 1]))
                small_rec.append(remote(pair, pair, ws.at[2 + o], wr.at[2 + o], others[o - 1]))
        elif t == 3:
            total = v_sum[2]
            for o in range(1, nz):
                small[2 + o].wait_recv()
                small_rec[2 + o].wait_recv()
                total = total + v_z[o]
            vec_out[...] = total

    stages = [stage_y, stage_x, stage_z, stage_zg, stage_xg]
    started = 0
    for t in range(max(count, 4) + len(stages)):
        for _ in range(2):
            if started < count:
                stage_core(started)
                started += 1
        for d, stage in enumerate(stages):
            if 0 <= t - d < count:
                stage(t - d)
        small_stage(t)
    for copy in core_c + y_c + x_c + xg_c + small + small_rec:
        copy.wait_send()
    for copies in z_c + zg_c:
        for copy in copies:
            copy.wait_send()
    for copy in outs:
        copy.wait()


def reduce_gradients(dp_n, terms, vec, rec):
    rows, width = terms.shape[2:]
    slab = max(256, 16 * dp_n)
    count, nz = rows // slab, dp_n // 2
    items = rec.shape[0]
    bf16, f32 = jnp.bfloat16, jnp.float32
    dma, vmem = pltpu.SemaphoreType.DMA, pltpu.VMEM
    v_shape = vec.shape
    return pl.pallas_call(
        functools.partial(_reduce_kernel, dp_n, slab),
        out_shape=[
            jax.ShapeDtypeStruct((rows, width), bf16),
            jax.ShapeDtypeStruct(v_shape, f32),
            jax.ShapeDtypeStruct((dp_n, 4) + rec.shape, f32),
        ],
        in_specs=[
            pl.BlockSpec(memory_space=pl.ANY),
            pl.BlockSpec(memory_space=pltpu.VMEM),
            pl.BlockSpec(memory_space=pltpu.VMEM),
        ],
        out_specs=[
            pl.BlockSpec(memory_space=pl.ANY),
            pl.BlockSpec(memory_space=pltpu.VMEM),
            pl.BlockSpec(memory_space=pltpu.VMEM),
        ],
        scratch_shapes=[
            vmem((count, 2, slab, width), bf16),
            vmem((count, 2, slab, width), bf16),
            vmem((count, slab, width), bf16),
            vmem((count, slab // 2, width), bf16),
            vmem((count, nz, slab // 2 // nz, width), bf16),
            vmem((count, slab, width), bf16),
            vmem(v_shape, f32),
            vmem(v_shape, f32),
            vmem(v_shape, f32),
            vmem((nz,) + v_shape, f32),
            vmem((3,) + v_shape, f32),
        ]
        + [dma((count,))] * 7
        + [dma((count, nz))] * 4
        + [dma((count,))] * 3
        + [dma((2 + nz,))] * 4,
        compiler_params=pltpu.CompilerParams(
            collective_id=1, has_side_effects=True, vmem_limit_bytes=60 << 20
        ),
        name="reduce_gradients",
    )(terms, vec, rec)


def split_heads(rows):
    return rows.reshape(rows.shape[0], rows.shape[1] // HEAD_DIM, HEAD_DIM)


def item_scores(queries, keys, key_valid):
    scores = jnp.einsum(
        "qhd,khd->hqk", split_heads(queries), split_heads(keys), preferred_element_type=jnp.float32
    ) * HEAD_DIM ** (-0.5)
    return jnp.where(key_valid[None, None, :], scores, neg_large)


def attend_forward(queries, keys, values, key_valid):
    masked = item_scores(queries, keys, key_valid)
    row_max = jnp.max(masked, axis=-1, keepdims=True)
    exp_scores = jnp.exp(masked - row_max)
    row_total = jnp.sum(exp_scores, axis=-1, keepdims=True)
    soft = (exp_scores / row_total).astype(jnp.bfloat16)
    mixed = jnp.einsum(
        "hqk,khd->qhd", soft, split_heads(values), preferred_element_type=jnp.float32
    )
    log_total = row_max[:, :, 0] + jnp.log(row_total[:, :, 0])
    return mixed.reshape(queries.shape).astype(jnp.bfloat16), log_total


def attend_backward(queries, keys, values, key_valid, log_total, grad_mixed):
    masked = item_scores(queries, keys, key_valid)
    soft = jnp.exp(masked - log_total[:, :, None])
    grad_heads = split_heads(grad_mixed)
    grad_value = jnp.einsum(
        "hqk,qhd->khd", soft.astype(jnp.bfloat16), grad_heads, preferred_element_type=jnp.float32
    )
    grad_soft = jnp.einsum(
        "qhd,khd->hqk", grad_heads, split_heads(values), preferred_element_type=jnp.float32
    )
    grad_scores = soft * (grad_soft - jnp.sum(soft * grad_soft, axis=-1, keepdims=True))
    scores_low = grad_scores.astype(jnp.bfloat16)
    scale = HEAD_DIM ** (-0.5)
    grad_query = scale * jnp.einsum(
        "hqk,khd->qhd", scores_low, split_heads(keys), preferred_element_type=jnp.float32
    )
    grad_key = scale * jnp.einsum(
        "hqk,qhd->khd", scores_low, split_heads(queries), preferred_element_type=jnp.float32
    )
    return tuple(
        grad.reshape(queries.shape).astype(jnp.bfloat16)
        for grad in (grad_query, grad_key, grad_value)
    )


def per_item(fn, item_count, slot_count, *arrays):
    if item_count == 1:
        return fn(*[a[0] for a in arrays])
    outs = lax.map(lambda packed: fn(*packed), arrays)
    return outs


def local(
    dp_n,
    tokens,
    time_embed,
    lengths,
    cotangent,
    w_query,
    w_key,
    w_value,
    w_out,
    w_time,
    w_in,
    w_down,
    b_query,
    b_value,
    b_out,
    b_time,
    b_in,
    b_down,
    gain_one,
    shift_one,
    gain_two,
    shift_two,
):
    f32, bf16 = jnp.float32, jnp.bfloat16
    seq_rank = lax.axis_index("seq")
    item_count = time_embed.shape[0]
    token_count = tokens.shape[0]
    slot_count = token_count // item_count
    width = tokens.shape[1]
    rows = w_time.shape[0]

    def mm(a, b, dims):
        return lax.dot_general(a, b, (dims, ((), ())), preferred_element_type=f32)

    full_time, full_query, full_key, full_value, full_out, full_in, full_down = gather_weights(
        [w_time, w_query, w_key, w_value, w_out, w_in, w_down]
    )
    own_lengths = lax.dynamic_slice_in_dim(lengths, seq_rank * item_count, item_count, 0)
    slot_index = lax.broadcasted_iota(jnp.int32, (item_count, slot_count), 1)
    own_valid = slot_index < own_lengths[:, None] + BLOCK
    row_keep = own_valid.reshape(token_count, 1).astype(f32)
    time_proj = mm(time_embed, full_time, ((1,), (0,))) + b_time.astype(f32)
    resid = (tokens.reshape(item_count, slot_count, width) + time_proj[:, None, :]).reshape(
        token_count, width
    )
    resid_low = resid.astype(bf16)
    query_rows = (mm(resid_low, full_query, ((1,), (0,))) + b_query.astype(f32)).astype(bf16)
    key_rows = mm(resid_low, full_key, ((1,), (0,))).astype(bf16)
    value_rows = (mm(resid_low, full_value, ((1,), (0,))) + b_value.astype(f32)).astype(bf16)

    def split_items(a):
        return a.reshape(item_count, slot_count, -1)

    qkv = [split_items(a) for a in (query_rows, key_rows, value_rows)]
    mixed, log_total = per_item(attend_forward, item_count, slot_count, *qkv, own_valid)
    mixed_rows = mixed.reshape(token_count, width)
    attn_out = mm(mixed_rows, full_out, ((1,), (0,))) + b_out.astype(f32)
    first_norm, first_pull = jax.vjp(
        layer_norm, resid + attn_out, gain_one.astype(f32), shift_one.astype(f32)
    )
    first_low = first_norm.astype(bf16)
    hidden_pre = mm(first_low, full_in, ((1,), (1,))) + b_in.astype(f32)
    hidden, gelu_pull = jax.vjp(exact_gelu, hidden_pre)
    hidden_low = hidden.astype(bf16)
    ffn_out = mm(hidden_low, full_down, ((1,), (0,))) + b_down.astype(f32)
    second_norm, second_pull = jax.vjp(
        layer_norm, first_norm + ffn_out, gain_two.astype(f32), shift_two.astype(f32)
    )
    layer_out = (second_norm * row_keep).astype(bf16)
    grad_second_in, grad_gain_two, grad_shift_two = second_pull(cotangent.astype(f32) * row_keep)
    grad_ffn = grad_second_in.astype(bf16)
    grad_hidden = mm(grad_ffn, full_down, ((1,), (1,)))
    grad_pre = gelu_pull(grad_hidden)[0].astype(bf16)
    grad_first = grad_second_in + mm(grad_pre, full_in, ((1,), (0,)))
    term_in = mm(grad_pre, first_low, ((0,), (0,))).astype(bf16)
    term_down = mm(hidden_low, grad_ffn, ((0,), (0,))).astype(bf16)
    grad_first_in, grad_gain_one, grad_shift_one = first_pull(grad_first)
    grad_attn = grad_first_in.astype(bf16)
    grad_mixed = mm(grad_attn, full_out, ((1,), (1,))).astype(bf16)
    if item_count == 1:
        extra = (log_total[None], split_items(grad_mixed))
    else:
        extra = (log_total, split_items(grad_mixed))
    grad_query, grad_key, grad_value = (
        a.reshape(token_count, width)
        for a in per_item(attend_backward, item_count, slot_count, *qkv, own_valid, *extra)
    )
    grad_resid = (
        grad_first_in
        + mm(grad_query, full_query, ((1,), (1,)))
        + mm(grad_key, full_key, ((1,), (1,)))
        + mm(grad_value, full_value, ((1,), (1,)))
    )
    grad_tokens = grad_resid.astype(bf16)
    grad_time = jnp.sum(grad_resid.reshape(item_count, slot_count, width), axis=1).astype(bf16)
    parts = [
        mm(resid_low, grad_query, ((0,), (0,))).astype(bf16),
        mm(resid_low, grad_key, ((0,), (0,))).astype(bf16),
        mm(resid_low, grad_value, ((0,), (0,))).astype(bf16),
        mm(mixed_rows, grad_attn, ((0,), (0,))).astype(bf16),
        term_in,
        term_down,
    ]
    terms = jnp.concatenate([t.reshape(2, 2, -1, width) for t in parts], axis=2)
    vec = jnp.stack(
        [
            jnp.sum(grad_query, axis=0, dtype=f32),
            jnp.sum(grad_value, axis=0, dtype=f32),
            jnp.sum(grad_attn, axis=0, dtype=f32),
            jnp.sum(grad_ffn, axis=0, dtype=f32),
            grad_gain_one,
            grad_shift_one,
            grad_gain_two,
            grad_shift_two,
        ]
    )
    vec = jnp.concatenate([vec, jnp.sum(grad_pre, axis=0, dtype=f32).reshape(-1, width)], axis=0)
    vec = jnp.pad(vec, ((0, -vec.shape[0] % 8), (0, 0)))
    rec = jnp.stack([time_embed, grad_time], axis=1).astype(f32).reshape(item_count, -1, 128)
    sums, vectors, every = reduce_gradients(dp_n, terms, vec, rec)
    every = every.reshape(-1, 2, width)
    time_rows, time_grads = every[:, 0].astype(bf16), every[:, 1].astype(bf16)
    own_columns = lax.dynamic_slice_in_dim(time_rows, seq_rank * rows, rows, 1)
    grad_w_time = mm(own_columns, time_grads, ((0,), (0,)))
    grad_b_time = jnp.sum(time_grads, axis=0, dtype=f32)
    grad_b_in = vectors[8 : 8 + b_in.shape[0] // width].reshape(-1)
    sums = sums.astype(f32)
    ends = [0]
    for t in parts:
        ends.append(ends[-1] + t.shape[0] // 4)
    shares = [sums[lo:hi] for lo, hi in zip(ends[:-1], ends[1:])]
    return (
        layer_out,
        grad_tokens,
        *shares[:4],
        grad_w_time,
        *shares[4:],
        vectors[0],
        vectors[1],
        vectors[2],
        grad_b_time,
        grad_b_in,
        vectors[3],
        vectors[4],
        vectors[5],
        vectors[6],
        vectors[7],
    )


def solution(mesh):
    in_specs = (
        P(("dp", "seq"), None),
        P(("dp", "seq"), None),
        P("dp"),
        P(("dp", "seq"), None),
        P("seq", None),
        P("seq", None),
        P("seq", None),
        P("seq", None),
        P("seq", None),
        P("seq", None),
        P("seq", None),
        P(),
        P(),
        P(),
        P(),
        P(),
        P(),
        P(),
        P(),
        P(),
        P(),
    )
    out_specs = (
        P(("dp", "seq"), None),
        P(("dp", "seq"), None),
        P("seq", None),
        P("seq", None),
        P("seq", None),
        P("seq", None),
        P("seq", None),
        P("seq", None),
        P("seq", None),
        P(),
        P(),
        P(),
        P(),
        P(),
        P(),
        P(),
        P(),
        P(),
        P(),
    )
    return jax.shard_map(functools.partial(local, mesh.shape["dp"]), mesh=mesh, in_specs=in_specs, out_specs=out_specs, check_vma=False)
```

```python
import functools

import jax
import jax.numpy as jnp
from jax import lax
from jax.experimental import pallas as pl
from jax.experimental.pallas import tpu as pltpu
from jax.sharding import PartitionSpec as P

HEAD_DIM = 64
BLOCK = 25
MESH = pl.DeviceIdType.MESH


norm_eps = 1e-05
neg_large = -1e30


def layer_norm(values, gain, shift):
    center = values - jnp.mean(values, axis=-1, keepdims=True)
    spread = lax.rsqrt(jnp.mean(center * center, axis=-1, keepdims=True) + norm_eps)
    return center * spread * gain + shift


def gelu_parts(values):
    half = 0.5 + 0.5 * lax.erf(values * 0.5**0.5)
    density = jnp.exp(-0.5 * values * values) * (0.5 / jnp.pi) ** 0.5
    return values * half, half + values * density


def _gather_kernel(sizes, *refs):
    n = len(sizes)
    given, outs, ins = refs[:n], refs[n : 2 * n], refs[2 * n : 3 * n]
    load_sem, own_sem, c_send, c_recv, y_send, y_recv, x_send, x_recv, f_send, f_recv, g_send, g_recv = refs[3 * n :]
    dp, me = lax.axis_index("dp"), lax.axis_index("seq")
    half = lax.rem(dp, 2)
    loads = [pltpu.make_async_copy(given[a], ins[a], load_sem.at[a]) for a in range(n)]
    for load in loads:
        load.start()
    core, across, side = (dp, me ^ 1), (dp, me ^ 2), (dp ^ 1, me)
    barrier = pltpu.get_barrier_semaphore()
    for peer in (core, across, side):
        pl.semaphore_signal(barrier, inc=1, device_id=peer, device_id_type=MESH)
    pl.semaphore_wait(barrier, 3)

    def remote(src, dst, send, recv, peer):
        return pltpu.make_async_remote_copy(
            src_ref=src, dst_ref=dst, send_sem=send, recv_sem=recv, device_id=peer, device_id_type=MESH
        )

    chunks = []
    for a, rows in enumerate(sizes):
        step = min(rows // 2, 256)
        chunks += [(a, rows, off, step) for off in range(0, rows // 2, step)]

    def region(ref, rows, shard, part, off, step):
        start = pl.multiple_of(shard * rows + part * (rows // 2) + off, 16)
        return ref.at[pl.ds(start, step), :]

    waits = []
    crossing = []
    for j, (a, rows, off, step) in enumerate(chunks):
        if off == 0:
            loads[a].wait()
        src = region(ins[a], rows, 0, half, off, step)
        copy = remote(src, region(outs[a], rows, me, half, off, step), y_send.at[j], y_recv.at[j], across)
        copy.start()
        crossing.append(copy)
    core_copies = []
    for a, rows in enumerate(sizes):
        home = outs[a].at[pl.ds(pl.multiple_of(me * rows, 16), rows), :]
        copy = remote(ins[a], home, c_send.at[a], c_recv.at[a], core)
        copy.start()
        core_copies.append(copy)
        keep = pltpu.make_async_copy(ins[a], home, own_sem.at[a])
        keep.start()
        waits.append(keep)
    sides, firsts, seconds = [], [], []
    for j in range(len(chunks) + 1):
        if j < len(chunks):
            a, rows, off, step = chunks[j]
            crossing[j].wait_recv()
            got = region(outs[a], rows, me ^ 2, half, off, step)
            copy = remote(got, got, x_send.at[j], x_recv.at[j], side)
            copy.start()
            sides.append(copy)
            copy = remote(got, got, f_send.at[j], f_recv.at[j], core)
            copy.start()
            firsts.append(copy)
        if j >= 1:
            a, rows, off, step = chunks[j - 1]
            sides[j - 1].wait_recv()
            got = region(outs[a], rows, me ^ 2, 1 - half, off, step)
            copy = remote(got, got, g_send.at[j - 1], g_recv.at[j - 1], core)
            copy.start()
            seconds.append(copy)
    for copy in waits:
        copy.wait()
    for copy in crossing + sides:
        copy.wait_send()
    for copy in core_copies + firsts + seconds:
        copy.wait()


def gather_weights(arrays):
    sizes = tuple(a.shape[0] for a in arrays)
    n = len(arrays)
    m = sum(max(1, r // 512) for r in sizes)
    dma = pltpu.SemaphoreType.DMA
    return pl.pallas_call(
        functools.partial(_gather_kernel, sizes),
        out_shape=[jax.ShapeDtypeStruct((4 * a.shape[0], a.shape[1]), a.dtype) for a in arrays],
        in_specs=[pl.BlockSpec(memory_space=pl.ANY)] * n,
        out_specs=[pl.BlockSpec(memory_space=pl.ANY)] * n,
        scratch_shapes=[pltpu.VMEM(a.shape, a.dtype) for a in arrays] + [dma((n,))] * 4 + [dma((m,))] * 8,
        compiler_params=pltpu.CompilerParams(
            collective_id=0, has_side_effects=True, vmem_limit_bytes=32 << 20
        ),
        name="gather_weights",
    )(*arrays)


def _row_loop(rows, step, body):
    def run(i, carry):
        body(pl.ds(pl.multiple_of(i * step, step), step))
        return carry

    lax.fori_loop(0, rows // step, run, 0)


def _reduce_kernel(dp_n, slab, heights, *refs):
    terms, (vec, rec, out, vec_out, rec_out), scr = refs[: len(heights)], refs[len(heights) : len(heights) + 5], refs[len(heights) + 5 :]
    (own, core_in, y_in, x_in, z_in, res, v_core, v_y, v_x, v_z, v_sum) = scr[:11]
    (load_sem, c_s, c_r, y_s, y_r, x_s, x_r, z_s, z_r, zg_s, zg_r, xg_s, xg_r, out_sem, vs, vr, ws, wr) = scr[11:]
    f32, bf16 = jnp.float32, jnp.bfloat16
    count = out.shape[0] // slab
    nz = dp_n // 2
    dp, me = lax.axis_index("dp"), lax.axis_index("seq")
    x, z, y, c = lax.rem(dp, 2), lax.div(dp, 2), lax.div(me, 2), lax.rem(me, 2)
    core, across, side = (dp, me ^ 1), (dp, me ^ 2), (dp ^ 1, me)
    others = [(lax.rem(z + o, nz) * 2 + x, me) for o in range(1, nz)]
    barrier = pltpu.get_barrier_semaphore()
    for peer in [core, across, side] + others:
        pl.semaphore_signal(barrier, inc=1, device_id=peer, device_id_type=MESH)
    pl.semaphore_wait(barrier, 3 + len(others))

    def remote(src, dst, send, recv, peer):
        copy = pltpu.make_async_remote_copy(
            src_ref=src, dst_ref=dst, send_sem=send, recv_sem=recv, device_id=peer, device_id_type=MESH
        )
        copy.start()
        return copy

    hs = slab // 2
    ps = hs // nz
    rs = min(ps, 32)
    loads, core_c, y_c, x_c, z_c, zg_c, xg_c, outs = [], [], [], [], [], [], [], []

    bases = [sum(heights[:i]) for i in range(len(heights))]
    pieces = [[] for _ in range(count)]
    for term, base, height in zip(terms, bases, heights):
        step = min(height, slab)
        for off in range(0, height, step):
            pieces[(base + off) // slab].append((term, off, (base + off) % slab, step))
    for k in range(count):
        group = [[], []]
        for i, (term, off, at, step) in enumerate(pieces[k]):
            rows, place = pl.ds(off, step), pl.ds(at, step)
            copy = remote(term.at[:, 1 - c, rows, :], core_in.at[k, :, place, :], c_s.at[k, i], c_r.at[k, i], core)
            load = pltpu.make_async_copy(term.at[:, c, rows, :], own.at[k, :, place, :], load_sem.at[k, i])
            load.start()
            group[0].append(copy)
            group[1].append(load)
        core_c.append(group[0])
        loads.append(group[1])

    small = [remote(vec, v_core, vs.at[0], vr.at[0], core)]
    rec_out[dp, me] = rec[...]
    small_rec = [remote(rec_out.at[dp, me], rec_out.at[dp, me], ws.at[0], wr.at[0], core)]

    def stage_core(k):
        for load in loads[k]:
            load.wait()
        for copy in core_c[k]:
            copy.wait_recv()

        def add(r):
            for p in range(2):
                own[k, p, r] = (own[k, p, r].astype(f32) + core_in[k, p, r].astype(f32)).astype(bf16)

        _row_loop(slab, 16, add)
        y_c.append(remote(own.at[k, 1 - y], y_in.at[k], y_s.at[k], y_r.at[k], across))

    def stage_y(k):
        y_c[k].wait_recv()

        def add(r):
            own[k, y, r] = (own[k, y, r].astype(f32) + y_in[k, r].astype(f32)).astype(bf16)

        _row_loop(slab, 32, add)
        give = pl.ds(pl.multiple_of((1 - x) * hs, 16), hs)
        x_c.append(remote(own.at[k, y, give], x_in.at[k], x_s.at[k], x_r.at[k], side))

    def stage_x(k):
        x_c[k].wait_recv()

        def add(r):
            at = pl.ds(pl.multiple_of(x * hs + r.start, 16), r.size)
            own[k, y, at] = (own[k, y, at].astype(f32) + x_in[k, r].astype(f32)).astype(bf16)

        _row_loop(hs, rs, add)
        copies = []
        for o in range(1, nz):
            piece = pl.ds(pl.multiple_of(x * hs + lax.rem(z + o, nz) * ps, 16), ps)
            copies.append(
                remote(own.at[k, y, piece], z_in.at[k, o], z_s.at[k, o], z_r.at[k, o], others[o - 1])
            )
        z_c.append(copies)

    def stage_z(k):
        for copy in z_c[k]:
            copy.wait_recv()

        def add(r):
            at = pl.ds(pl.multiple_of(x * hs + z * ps + r.start, 16), r.size)
            total = own[k, y, at].astype(f32)
            for o in range(1, nz):
                total += z_in[k, o, r].astype(f32)
            res[k, at] = total.astype(bf16)

        _row_loop(ps, rs, add)
        mine = res.at[k, pl.ds(pl.multiple_of(x * hs + z * ps, 16), ps)]
        zg_c.append(
            [remote(mine, mine, zg_s.at[k, o], zg_r.at[k, o], others[o - 1]) for o in range(1, nz)]
        )

    def stage_zg(k):
        for copy in zg_c[k]:
            copy.wait_recv()
        mine = res.at[k, pl.ds(pl.multiple_of(x * hs, 16), hs)]
        xg_c.append(remote(mine, mine, xg_s.at[k], xg_r.at[k], side))

    def stage_xg(k):
        xg_c[k].wait_recv()
        copy = pltpu.make_async_copy(res.at[k], out.at[pl.ds(k * slab, slab), :], out_sem.at[k])
        copy.start()
        outs.append(copy)

    def small_stage(t):
        if t == 0:
            small[0].wait_recv()
            v_sum[0] = vec[...] + v_core[...]
            small.append(remote(v_sum.at[0], v_y, vs.at[1], vr.at[1], across))
            small_rec[0].wait_recv()
            pair = rec_out.at[dp, pl.ds(y * 2, 2)]
            small_rec.append(remote(pair, pair, ws.at[1], wr.at[1], across))
        elif t == 1:
            small[1].wait_recv()
            v_sum[1] = v_sum[0] + v_y[...]
            small.append(remote(v_sum.at[1], v_x, vs.at[2], vr.at[2], side))
            small_rec[1].wait_recv()
            quad = rec_out.at[dp]
            small_rec.append(remote(quad, quad, ws.at[2], wr.at[2], side))
        elif t == 2:
            small[2].wait_recv()
            v_sum[2] = v_sum[1] + v_x[...]
            small_rec[2].wait_recv()
            pair = rec_out.at[pl.ds(z * 2, 2)]
            for o in range(1, nz):
                small.append(remote(v_sum.at[2], v_z.at[o], vs.at[2 + o], vr.at[2 + o], others[o - 1]))
                small_rec.append(remote(pair, pair, ws.at[2 + o], wr.at[2 + o], others[o - 1]))
        elif t == 3:
            total = v_sum[2]
            for o in range(1, nz):
                small[2 + o].wait_recv()
                small_rec[2 + o].wait_recv()
                total = total + v_z[o]
            vec_out[...] = total

    stages = [stage_y, stage_x, stage_z, stage_zg, stage_xg]
    started = 0
    for t in range(max(count, 4) + len(stages)):
        for _ in range(2):
            if started < count:
                stage_core(started)
                started += 1
        for d, stage in enumerate(stages):
            if 0 <= t - d < count:
                stage(t - d)
        small_stage(t)
    for copy in y_c + x_c + xg_c + small + small_rec:
        copy.wait_send()
    for copies in core_c + z_c + zg_c:
        for copy in copies:
            copy.wait_send()
    for copy in outs:
        copy.wait()


def reduce_gradients(dp_n, terms, vec, rec):
    width = terms[0].shape[-1]
    heights = tuple(t.shape[2] for t in terms)
    rows = sum(heights)
    slab = max(256, 16 * dp_n)
    count, nz = rows // slab, dp_n // 2
    most = max(1, slab // min(heights))
    items = rec.shape[0]
    bf16, f32 = jnp.bfloat16, jnp.float32
    dma, vmem = pltpu.SemaphoreType.DMA, pltpu.VMEM
    v_shape = vec.shape
    return pl.pallas_call(
        functools.partial(_reduce_kernel, dp_n, slab, heights),
        out_shape=[
            jax.ShapeDtypeStruct((rows, width), bf16),
            jax.ShapeDtypeStruct(v_shape, f32),
            jax.ShapeDtypeStruct((dp_n, 4) + rec.shape, f32),
        ],
        in_specs=[pl.BlockSpec(memory_space=pl.ANY)] * len(terms) + [pl.BlockSpec(memory_space=pltpu.VMEM)] * 2,
        out_specs=[
            pl.BlockSpec(memory_space=pl.ANY),
            pl.BlockSpec(memory_space=pltpu.VMEM),
            pl.BlockSpec(memory_space=pltpu.VMEM),
        ],
        scratch_shapes=[
            vmem((count, 2, slab, width), bf16),
            vmem((count, 2, slab, width), bf16),
            vmem((count, slab, width), bf16),
            vmem((count, slab // 2, width), bf16),
            vmem((count, nz, slab // 2 // nz, width), bf16),
            vmem((count, slab, width), bf16),
            vmem(v_shape, f32),
            vmem(v_shape, f32),
            vmem(v_shape, f32),
            vmem((nz,) + v_shape, f32),
            vmem((3,) + v_shape, f32),
        ]
        + [dma((count, most))] * 3
        + [dma((count,))] * 4
        + [dma((count, nz))] * 4
        + [dma((count,))] * 3
        + [dma((2 + nz,))] * 4,
        compiler_params=pltpu.CompilerParams(
            collective_id=1, has_side_effects=True, vmem_limit_bytes=60 << 20
        ),
        name="reduce_gradients",
    )(*terms, vec, rec)


def split_heads(rows):
    return rows.reshape(rows.shape[0], rows.shape[1] // HEAD_DIM, HEAD_DIM)


def item_scores(queries, keys, key_valid):
    scores = jnp.einsum(
        "qhd,khd->hqk", split_heads(queries), split_heads(keys), preferred_element_type=jnp.float32
    ) * HEAD_DIM ** (-0.5)
    return jnp.where(key_valid[None, None, :], scores, neg_large)


def attend_forward(queries, keys, values, key_valid):
    masked = item_scores(queries, keys, key_valid)
    row_max = jnp.max(masked, axis=-1, keepdims=True)
    exp_scores = jnp.exp(masked - row_max)
    row_total = jnp.sum(exp_scores, axis=-1, keepdims=True)
    soft = (exp_scores / row_total).astype(jnp.bfloat16)
    mixed = jnp.einsum(
        "hqk,khd->qhd", soft, split_heads(values), preferred_element_type=jnp.float32
    )
    log_total = row_max[:, :, 0] + jnp.log(row_total[:, :, 0])
    return mixed.reshape(queries.shape).astype(jnp.bfloat16), log_total


def attend_backward(queries, keys, values, key_valid, log_total, grad_mixed):
    masked = item_scores(queries, keys, key_valid)
    soft = jnp.exp(masked - log_total[:, :, None])
    grad_heads = split_heads(grad_mixed)
    grad_value = jnp.einsum(
        "hqk,qhd->khd", soft.astype(jnp.bfloat16), grad_heads, preferred_element_type=jnp.float32
    )
    grad_soft = jnp.einsum(
        "qhd,khd->hqk", grad_heads, split_heads(values), preferred_element_type=jnp.float32
    )
    grad_scores = soft * (grad_soft - jnp.sum(soft * grad_soft, axis=-1, keepdims=True))
    scores_low = grad_scores.astype(jnp.bfloat16)
    scale = HEAD_DIM ** (-0.5)
    grad_query = scale * jnp.einsum(
        "hqk,khd->qhd", scores_low, split_heads(keys), preferred_element_type=jnp.float32
    )
    grad_key = scale * jnp.einsum(
        "hqk,qhd->khd", scores_low, split_heads(queries), preferred_element_type=jnp.float32
    )
    return tuple(
        grad.reshape(queries.shape).astype(jnp.bfloat16)
        for grad in (grad_query, grad_key, grad_value)
    )


def per_item(fn, item_count, slot_count, *arrays):
    if item_count == 1:
        return fn(*[a[0] for a in arrays])
    outs = lax.map(lambda packed: fn(*packed), arrays)
    return outs


def local(
    dp_n,
    tokens,
    time_embed,
    lengths,
    cotangent,
    w_query,
    w_key,
    w_value,
    w_out,
    w_time,
    w_in,
    w_down,
    b_query,
    b_value,
    b_out,
    b_time,
    b_in,
    b_down,
    gain_one,
    shift_one,
    gain_two,
    shift_two,
):
    f32, bf16 = jnp.float32, jnp.bfloat16
    seq_rank = lax.axis_index("seq")
    item_count = time_embed.shape[0]
    token_count = tokens.shape[0]
    slot_count = token_count // item_count
    width = tokens.shape[1]
    rows = w_time.shape[0]

    def mm(a, b, dims):
        return lax.dot_general(a, b, (dims, ((), ())), preferred_element_type=f32)

    full_time, full_query, full_key, full_value, full_out, full_in, full_down = gather_weights(
        [w_time, w_query, w_key, w_value, w_out, w_in, w_down]
    )
    own_lengths = lax.dynamic_slice_in_dim(lengths, seq_rank * item_count, item_count, 0)
    slot_index = lax.broadcasted_iota(jnp.int32, (item_count, slot_count), 1)
    own_valid = slot_index < own_lengths[:, None] + BLOCK
    row_keep = own_valid.reshape(token_count, 1).astype(f32)
    time_proj = mm(time_embed, full_time, ((1,), (0,))) + b_time.astype(f32)
    resid = (tokens.reshape(item_count, slot_count, width) + time_proj[:, None, :]).reshape(
        token_count, width
    )
    resid_low = resid.astype(bf16)
    query_rows = (mm(resid_low, full_query, ((1,), (0,))) + b_query.astype(f32)).astype(bf16)
    key_rows = mm(resid_low, full_key, ((1,), (0,))).astype(bf16)
    value_rows = (mm(resid_low, full_value, ((1,), (0,))) + b_value.astype(f32)).astype(bf16)

    def split_items(a):
        return a.reshape(item_count, slot_count, -1)

    qkv = [split_items(a) for a in (query_rows, key_rows, value_rows)]
    mixed, log_total = per_item(attend_forward, item_count, slot_count, *qkv, own_valid)
    mixed_rows = mixed.reshape(token_count, width)
    attn_out = mm(mixed_rows, full_out, ((1,), (0,))) + b_out.astype(f32)
    first_norm, first_pull = jax.vjp(
        layer_norm, resid + attn_out, gain_one.astype(f32), shift_one.astype(f32)
    )
    first_low = first_norm.astype(bf16)
    hidden_pre = mm(first_low, full_in, ((1,), (1,))) + b_in.astype(f32)
    hidden, gelu_slope = gelu_parts(hidden_pre)
    hidden_low = hidden.astype(bf16)
    ffn_out = mm(hidden_low, full_down, ((1,), (0,))) + b_down.astype(f32)
    second_norm, second_pull = jax.vjp(
        layer_norm, first_norm + ffn_out, gain_two.astype(f32), shift_two.astype(f32)
    )
    layer_out = (second_norm * row_keep).astype(bf16)
    grad_second_in, grad_gain_two, grad_shift_two = second_pull(cotangent.astype(f32) * row_keep)
    grad_ffn = grad_second_in.astype(bf16)
    grad_hidden = mm(grad_ffn, full_down, ((1,), (1,)))
    grad_pre = (grad_hidden * gelu_slope).astype(bf16)
    grad_first = grad_second_in + mm(grad_pre, full_in, ((1,), (0,)))
    term_in = mm(grad_pre, first_low, ((0,), (0,))).astype(bf16)
    term_down = mm(hidden_low, grad_ffn, ((0,), (0,))).astype(bf16)
    grad_first_in, grad_gain_one, grad_shift_one = first_pull(grad_first)
    grad_attn = grad_first_in.astype(bf16)
    grad_mixed = mm(grad_attn, full_out, ((1,), (1,))).astype(bf16)
    if item_count == 1:
        extra = (log_total[None], split_items(grad_mixed))
    else:
        extra = (log_total, split_items(grad_mixed))
    grad_query, grad_key, grad_value = (
        a.reshape(token_count, width)
        for a in per_item(attend_backward, item_count, slot_count, *qkv, own_valid, *extra)
    )
    grad_resid = (
        grad_first_in
        + mm(grad_query, full_query, ((1,), (1,)))
        + mm(grad_key, full_key, ((1,), (1,)))
        + mm(grad_value, full_value, ((1,), (1,)))
    )
    grad_tokens = grad_resid.astype(bf16)
    grad_time = jnp.sum(grad_resid.reshape(item_count, slot_count, width), axis=1).astype(bf16)
    parts = [
        mm(resid_low, grad_query, ((0,), (0,))).astype(bf16),
        mm(resid_low, grad_key, ((0,), (0,))).astype(bf16),
        mm(resid_low, grad_value, ((0,), (0,))).astype(bf16),
        mm(mixed_rows, grad_attn, ((0,), (0,))).astype(bf16),
        term_in,
        term_down,
    ]
    terms = [t.reshape(2, 2, -1, width) for t in parts]
    vec = jnp.stack(
        [
            jnp.sum(grad_query, axis=0, dtype=f32),
            jnp.sum(grad_value, axis=0, dtype=f32),
            jnp.sum(grad_attn, axis=0, dtype=f32),
            jnp.sum(grad_ffn, axis=0, dtype=f32),
            grad_gain_one,
            grad_shift_one,
            grad_gain_two,
            grad_shift_two,
        ]
    )
    vec = jnp.concatenate([vec, jnp.sum(grad_pre, axis=0, dtype=f32).reshape(-1, width)], axis=0)
    vec = jnp.pad(vec, ((0, -vec.shape[0] % 8), (0, 0)))
    rec = jnp.stack([time_embed, grad_time], axis=1).astype(f32).reshape(item_count, -1, 128)
    sums, vectors, every = reduce_gradients(dp_n, terms, vec, rec)
    every = every.reshape(-1, 2, width)
    time_rows, time_grads = every[:, 0].astype(bf16), every[:, 1].astype(bf16)
    own_columns = lax.dynamic_slice_in_dim(time_rows, seq_rank * rows, rows, 1)
    grad_w_time = mm(own_columns, time_grads, ((0,), (0,)))
    grad_b_time = jnp.sum(time_grads, axis=0, dtype=f32)
    grad_b_in = vectors[8 : 8 + b_in.shape[0] // width].reshape(-1)
    sums = sums.astype(f32)
    ends = [0]
    for t in parts:
        ends.append(ends[-1] + t.shape[0] // 4)
    shares = [sums[lo:hi] for lo, hi in zip(ends[:-1], ends[1:])]
    return (
        layer_out,
        grad_tokens,
        *shares[:4],
        grad_w_time,
        *shares[4:],
        vectors[0],
        vectors[1],
        vectors[2],
        grad_b_time,
        grad_b_in,
        vectors[3],
        vectors[4],
        vectors[5],
        vectors[6],
        vectors[7],
    )


def solution(mesh):
    in_specs = (
        P(("dp", "seq"), None),
        P(("dp", "seq"), None),
        P("dp"),
        P(("dp", "seq"), None),
        P("seq", None),
        P("seq", None),
        P("seq", None),
        P("seq", None),
        P("seq", None),
        P("seq", None),
        P("seq", None),
        P(),
        P(),
        P(),
        P(),
        P(),
        P(),
        P(),
        P(),
        P(),
        P(),
    )
    out_specs = (
        P(("dp", "seq"), None),
        P(("dp", "seq"), None),
        P("seq", None),
        P("seq", None),
        P("seq", None),
        P("seq", None),
        P("seq", None),
        P("seq", None),
        P("seq", None),
        P(),
        P(),
        P(),
        P(),
        P(),
        P(),
        P(),
        P(),
        P(),
        P(),
    )
    return jax.shard_map(functools.partial(local, mesh.shape["dp"]), mesh=mesh, in_specs=in_specs, out_specs=out_specs, check_vma=False)
```

```python
import functools

import jax
import jax.numpy as jnp
from jax import lax
from jax.experimental import pallas as pl
from jax.experimental.pallas import tpu as pltpu
from jax.sharding import PartitionSpec as P

HEAD_DIM = 64
BLOCK = 25
MESH = pl.DeviceIdType.MESH


norm_eps = 1e-05
neg_large = -1e30


def layer_norm(values, gain, shift):
    center = values - jnp.mean(values, axis=-1, keepdims=True)
    spread = lax.rsqrt(jnp.mean(center * center, axis=-1, keepdims=True) + norm_eps)
    return center * spread * gain + shift


def gelu_parts(values):
    half = 0.5 + 0.5 * lax.erf(values * 0.5**0.5)
    density = jnp.exp(-0.5 * values * values) * (0.5 / jnp.pi) ** 0.5
    return values * half, half + values * density


def _gather_kernel(sizes, *refs):
    n = len(sizes)
    given, outs, ins = refs[:n], refs[n : 2 * n], refs[2 * n : 3 * n]
    load_sem, own_sem, c_send, c_recv, y_send, y_recv, x_send, x_recv, f_send, f_recv, g_send, g_recv = refs[3 * n :]
    dp, me = lax.axis_index("dp"), lax.axis_index("seq")
    half = lax.rem(dp, 2)
    loads = [pltpu.make_async_copy(given[a], ins[a], load_sem.at[a]) for a in range(n)]
    for load in loads:
        load.start()
    core, across, side = (dp, me ^ 1), (dp, me ^ 2), (dp ^ 1, me)
    barrier = pltpu.get_barrier_semaphore()
    for peer in (core, across, side):
        pl.semaphore_signal(barrier, inc=1, device_id=peer, device_id_type=MESH)
    pl.semaphore_wait(barrier, 3)

    def remote(src, dst, send, recv, peer):
        return pltpu.make_async_remote_copy(
            src_ref=src, dst_ref=dst, send_sem=send, recv_sem=recv, device_id=peer, device_id_type=MESH
        )

    chunks = []
    for a, rows in enumerate(sizes):
        step = min(rows // 2, 256)
        chunks += [(a, rows, off, step) for off in range(0, rows // 2, step)]

    def region(ref, rows, shard, part, off, step):
        start = pl.multiple_of(shard * rows + part * (rows // 2) + off, 16)
        return ref.at[pl.ds(start, step), :]

    waits = []
    crossing = []
    for j, (a, rows, off, step) in enumerate(chunks):
        if off == 0:
            loads[a].wait()
        src = region(ins[a], rows, 0, half, off, step)
        copy = remote(src, region(outs[a], rows, me, half, off, step), y_send.at[j], y_recv.at[j], across)
        copy.start()
        crossing.append(copy)
    core_copies = []
    for a, rows in enumerate(sizes):
        home = outs[a].at[pl.ds(pl.multiple_of(me * rows, 16), rows), :]
        copy = remote(ins[a], home, c_send.at[a], c_recv.at[a], core)
        copy.start()
        core_copies.append(copy)
        keep = pltpu.make_async_copy(ins[a], home, own_sem.at[a])
        keep.start()
        waits.append(keep)
    sides, firsts, seconds = [], [], []
    for j in range(len(chunks) + 1):
        if j < len(chunks):
            a, rows, off, step = chunks[j]
            crossing[j].wait_recv()
            got = region(outs[a], rows, me ^ 2, half, off, step)
            copy = remote(got, got, x_send.at[j], x_recv.at[j], side)
            copy.start()
            sides.append(copy)
            copy = remote(got, got, f_send.at[j], f_recv.at[j], core)
            copy.start()
            firsts.append(copy)
        if j >= 1:
            a, rows, off, step = chunks[j - 1]
            sides[j - 1].wait_recv()
            got = region(outs[a], rows, me ^ 2, 1 - half, off, step)
            copy = remote(got, got, g_send.at[j - 1], g_recv.at[j - 1], core)
            copy.start()
            seconds.append(copy)
    for copy in waits:
        copy.wait()
    for copy in crossing + sides:
        copy.wait_send()
    for copy in core_copies + firsts + seconds:
        copy.wait()


def gather_weights(arrays):
    sizes = tuple(a.shape[0] for a in arrays)
    n = len(arrays)
    m = sum(max(1, r // 512) for r in sizes)
    dma = pltpu.SemaphoreType.DMA
    return pl.pallas_call(
        functools.partial(_gather_kernel, sizes),
        out_shape=[jax.ShapeDtypeStruct((4 * a.shape[0], a.shape[1]), a.dtype) for a in arrays],
        in_specs=[pl.BlockSpec(memory_space=pl.ANY)] * n,
        out_specs=[pl.BlockSpec(memory_space=pl.ANY)] * n,
        scratch_shapes=[pltpu.VMEM(a.shape, a.dtype) for a in arrays] + [dma((n,))] * 4 + [dma((m,))] * 8,
        compiler_params=pltpu.CompilerParams(
            collective_id=0, has_side_effects=True, vmem_limit_bytes=66_000_000
        ),
        name="gather_weights",
    )(*arrays)


def _row_loop(rows, step, body):
    def run(i, carry):
        body(pl.ds(pl.multiple_of(i * step, step), step))
        return carry

    lax.fori_loop(0, rows // step, run, 0)


def _backward_kernel(dp_n, slab, lag, heights, own_heights, *refs):
    n_terms = len(heights)
    terms = refs[:n_terms]
    (query, key, value, grad_mixed, w_query, w_key, w_value, log_total, keep, resid_t, grad_first, vec, embed) = refs[
        n_terms : n_terms + 13
    ]
    out, vec_out, rec_out, grad_tokens = refs[n_terms + 13 : n_terms + 17]
    (own, core_in, y_in, x_in, z_in, act, grads, weights, time_sum, v_own, v_core, v_y, v_x, v_z, v_sum) = refs[
        n_terms + 17 : n_terms + 32
    ]
    (load_sem, act_sem, w_sem, c_s, c_r, y_s, y_r, x_s, x_r, z_s, z_r, zg_s, zg_r, xg_s, xg_r, out_sem) = refs[
        n_terms + 32 : n_terms + 48
    ]
    vs, vr, ws, wr = refs[n_terms + 48 :]
    f32, bf16 = jnp.float32, jnp.bfloat16
    count = out.shape[0] // slab
    nz = dp_n // 2
    scale = HEAD_DIM**-0.5
    slots, width = query.shape
    pair = 2 * HEAD_DIM
    pairs = width // pair
    dp, me = lax.axis_index("dp"), lax.axis_index("seq")
    x, z, y, c = lax.rem(dp, 2), lax.div(dp, 2), lax.div(me, 2), lax.rem(me, 2)
    core, across, side = (dp, me ^ 1), (dp, me ^ 2), (dp ^ 1, me)
    others = [(lax.rem(z + o, nz) * 2 + x, me) for o in range(1, nz)]

    act_loads = [
        pltpu.make_async_copy(src, act.at[i], act_sem.at[i]) for i, src in enumerate((query, key, value, grad_mixed))
    ]
    w_loads = [pltpu.make_async_copy(src, weights.at[i], w_sem.at[i]) for i, src in enumerate((w_query, w_key, w_value))]
    for load in act_loads:
        load.start()
    barrier = pltpu.get_barrier_semaphore()
    for peer in [core, across, side] + others:
        pl.semaphore_signal(barrier, inc=1, device_id=peer, device_id_type=MESH)
    pl.semaphore_wait(barrier, 3 + len(others))

    def remote(src, dst, send, recv, peer):
        return pltpu.make_async_remote_copy(
            src_ref=src, dst_ref=dst, send_sem=send, recv_sem=recv, device_id=peer, device_id_type=MESH
        )

    hs = slab // 2
    ps = hs // nz
    rs = min(ps, 32)
    given = sum(heights)
    full = given // slab

    row = 0
    for term, height in zip(terms, heights):
        step = min(height, slab)
        for off in range(0, height, step):
            k, at = (row + off) // slab, (row + off) % slab
            rows, place = pl.ds(off, step), pl.ds(at, step)
            remote(term.at[:, 1 - c, rows, :], core_in.at[k, :, place, :], c_s.at[k], c_r.at[k], core).start()
            sem = load_sem.at[k] if k < full else load_sem.at[count]
            pltpu.make_async_copy(term.at[:, c, rows, :], own.at[k, :, place, :], sem).start()
        row += height
    for load in w_loads:
        load.start()

    def core_copy(k):
        return remote(core_in.at[k], core_in.at[k], c_s.at[k], c_r.at[k], core)

    def y_copy(k):
        return remote(own.at[k, 1 - y], y_in.at[k], y_s.at[k], y_r.at[k], across)

    def x_copy(k):
        give = pl.ds(pl.multiple_of((1 - x) * hs, 16), hs)
        return remote(own.at[k, y, give], x_in.at[k], x_s.at[k], x_r.at[k], side)

    def z_copy(k, o):
        piece = pl.ds(pl.multiple_of(x * hs + lax.rem(z + o, nz) * ps, 16), ps)
        return remote(own.at[k, y, piece], z_in.at[k, o], z_s.at[k, o], z_r.at[k, o], others[o - 1])

    def zg_copy(k, o):
        mine = own.at[k, 1 - y, pl.ds(pl.multiple_of(x * hs + z * ps, 16), ps)]
        return remote(mine, mine, zg_s.at[k, o], zg_r.at[k, o], others[o - 1])

    def xg_copy(k):
        mine = own.at[k, 1 - y, pl.ds(pl.multiple_of(x * hs, 16), hs)]
        return remote(mine, mine, xg_s.at[k], xg_r.at[k], side)

    def out_copy(k):
        rows = pl.ds(pl.multiple_of(k * slab, slab), slab)
        return pltpu.make_async_copy(own.at[k, 1 - y], out.at[rows, :], out_sem.at[k])

    def stage_core(k):
        @pl.when(k < full)
        def _():
            pltpu.make_async_copy(own.at[k], own.at[k], load_sem.at[k]).wait()

        core_copy(k).wait_recv()

        def add(r):
            for p in range(2):
                own[k, p, r] = (own[k, p, r].astype(f32) + core_in[k, p, r].astype(f32)).astype(bf16)

        _row_loop(slab, 16, add)
        y_copy(k).start()

    def stage_y(k):
        y_copy(k).wait()

        def add(r):
            own[k, y, r] = (own[k, y, r].astype(f32) + y_in[k, r].astype(f32)).astype(bf16)

        _row_loop(slab, 32, add)
        x_copy(k).start()

    def stage_x(k):
        x_copy(k).wait_recv()

        def add(r):
            at = pl.ds(pl.multiple_of(x * hs + r.start, 16), r.size)
            own[k, y, at] = (own[k, y, at].astype(f32) + x_in[k, r].astype(f32)).astype(bf16)

        _row_loop(hs, rs, add)
        for o in range(1, nz):
            z_copy(k, o).start()

    def stage_z(k):
        for o in range(1, nz):
            z_copy(k, o).wait_recv()

        def add(r):
            at = pl.ds(pl.multiple_of(x * hs + z * ps + r.start, 16), r.size)
            total = own[k, y, at].astype(f32)
            for o in range(1, nz):
                total += z_in[k, o, r].astype(f32)
            own[k, 1 - y, at] = total.astype(bf16)

        _row_loop(ps, rs, add)
        for o in range(1, nz):
            zg_copy(k, o).start()

    def stage_zg(k):
        for o in range(1, nz):
            zg_copy(k, o).wait_recv()
        xg_copy(k).start()

    def stage_xg(k):
        xg_copy(k).wait_recv()
        out_copy(k).start()

    def dot(a, b, dims):
        return lax.dot_general(a, b, (dims, ((), ())), preferred_element_type=f32)

    def head_pair(p):
        cols = pl.ds(pl.multiple_of(p * pair, pair), pair)
        q2, k2, v2, g2 = (act[i, :, cols] for i in range(4))
        first = lax.broadcasted_iota(jnp.int32, (1, pair), 1) < HEAD_DIM
        kept = keep[...] > 0
        found = []
        for h in range(2):
            mask = jnp.where(first == (h == 0), 1.0, 0.0)
            q_h = q2 * (mask * scale).astype(bf16)
            g_h = g2 * mask.astype(bf16)
            scores = dot(k2, q_h, ((1,), (1,)))
            soft = jnp.where(kept, jnp.exp(scores - log_total[pl.ds(2 * p + h, 1), :]), 0.0)
            grad_soft = dot(v2, g_h, ((1,), (1,)))
            inner = jnp.sum(soft * grad_soft, axis=0, keepdims=True)
            grad_scores = (soft * (grad_soft - inner)).astype(bf16)
            found.append(
                (
                    dot(k2, grad_scores, ((0,), (0,))),
                    dot(grad_scores, q2, ((1,), (0,))),
                    dot(soft.astype(bf16), g2, ((1,), (0,))),
                )
            )
        q_t = jnp.concatenate([found[0][0][:HEAD_DIM], found[1][0][HEAD_DIM:]], axis=0)
        grad_q = (q_t.T * scale).astype(bf16)
        grad_k = (jnp.where(first, found[0][1], found[1][1]) * scale).astype(bf16)
        grad_v = jnp.where(first, found[0][2], found[1][2]).astype(bf16)
        grads[0, :, cols] = grad_q
        grads[1, :, cols] = grad_k
        grads[2, :, cols] = grad_v
        v_own[0:1, cols] = jnp.sum(grad_q.astype(f32), axis=0, keepdims=True)
        v_own[1:2, cols] = jnp.sum(grad_v.astype(f32), axis=0, keepdims=True)

    def term(m):
        step = min(own_heights, slab)
        for cc, mine in ((1 - c, False), (c, True)):
            for p in range(2):
                left = resid_t[pl.ds(pl.multiple_of((p * 2 + cc) * own_heights, own_heights), own_heights), :]
                tile = dot(left, grads[m], ((1,), (0,))).astype(bf16)
                if not mine:
                    act[m, p * own_heights : (p + 1) * own_heights] = tile
                for off in range(0, own_heights, step):
                    start = given + m * own_heights + off
                    k, at = lax.div(start, slab), pl.multiple_of(lax.rem(start, slab), step)
                    if mine:
                        own[k, p, pl.ds(at, step)] = tile[off : off + step]
                    else:
                        src = act.at[m, pl.ds(p * own_heights + off, step), :]
                        dst = core_in.at[k, p, pl.ds(at, step), :]
                        remote(src, dst, c_s.at[k], c_r.at[k], core).start()

    blocks = 4
    block = slots // blocks

    def resid_rows(r):
        rows = pl.ds(pl.multiple_of(r * block, block), block)
        total = grad_first[rows, :]
        for m in range(3):
            total += dot(grads[m, rows, :], weights[m], ((1,), (1,)))
        grad_tokens[rows, :] = total.astype(bf16)
        time_sum[...] += jnp.sum(total, axis=0, keepdims=True)

    def v_copy(i):
        peers = [core, across, side] + others
        dst = (v_core, v_y, v_x)[i] if i < 3 else v_z.at[i - 2]
        return remote(v_own if i == 0 else v_sum.at[min(i, 3) - 1], dst, vs.at[i], vr.at[i], peers[i])

    def w_copy(i):
        peers = [core, across, side] + others
        part = (
            rec_out.at[dp, me],
            rec_out.at[dp, pl.ds(y * 2, 2)],
            rec_out.at[dp],
            rec_out.at[pl.ds(z * 2, 2)],
        )[min(i, 3)]
        return remote(part, part, ws.at[i], wr.at[i], peers[i])

    def small_stage(i):
        if i == 0:
            rounded = time_sum[...].astype(bf16).astype(f32)
            lanes = embed.shape[-1]
            lines = width // lanes
            rec_out[dp, me, 0, 0:lines, :] = embed[...]
            for j in range(lines):
                rec_out[dp, me, 0, lines + j : lines + j + 1, :] = rounded[:, j * lanes : (j + 1) * lanes]
            v_copy(0).start()
            w_copy(0).start()
        elif i <= 3:
            v_copy(i - 1).wait_recv()
            w_copy(i - 1).wait_recv()
            before = v_own[...] if i == 1 else v_sum[i - 2]
            v_sum[i - 1] = before + (v_core, v_y, v_x)[i - 1][...]
            for j in range(i, i + 1 if i < 3 else 2 + nz):
                v_copy(j).start()
                w_copy(j).start()
        else:
            total = v_sum[2]
            for o in range(1, nz):
                v_copy(2 + o).wait_recv()
                w_copy(2 + o).wait_recv()
                total = total + v_z[o]
            vec_out[...] = total

    stages = [stage_y, stage_x, stage_z, stage_zg, stage_xg]
    n_units = pairs + 3 + blocks
    base = 0 if slab <= own_heights else pairs + 4
    ticks = max(base + count + lag * (len(stages) - 1), n_units + 5)
    v_own[...] = vec[...]
    time_sum[...] = jnp.zeros_like(time_sum)
    for load in act_loads:
        load.wait()

    def tick(t, carry):
        @pl.when(t < pairs)
        def _():
            head_pair(t)

        @pl.when((t >= pairs) & (t < pairs + 3))
        def _():
            term(t - pairs)

        @pl.when(t == pairs + 3)
        def _():
            for load in w_loads:
                load.wait()

        @pl.when((t >= pairs + 3) & (t < n_units))
        def _():
            resid_rows(t - pairs - 3)

        if row > full * slab:

            @pl.when(t == base)
            def _():
                part = own.at[full, :, pl.ds(0, row - full * slab), :]
                pltpu.make_async_copy(part, part, load_sem.at[count]).wait()

        for i in range(2):
            k = 2 * (t - base) + i

            @pl.when((k >= 0) & (k < count))
            def _():
                stage_core(k)

        for d, stage in enumerate(stages):
            k = t - base - d * lag

            @pl.when((k >= 0) & (k < count))
            def _():
                stage(k)

        for i in range(5):

            @pl.when(t == n_units + i)
            def _():
                small_stage(i)

        return carry

    lax.fori_loop(0, ticks, tick, 0)

    def finish(k, carry):
        core_copy(k).wait_send()
        x_copy(k).wait_send()
        for o in range(1, nz):
            z_copy(k, o).wait_send()
            zg_copy(k, o).wait_send()
        xg_copy(k).wait_send()
        out_copy(k).wait()
        return carry

    lax.fori_loop(0, count, finish, 0)
    for i in range(2 + nz):
        v_copy(i).wait_send()
        w_copy(i).wait_send()


def attend_and_reduce(dp_n, terms, acts, weights, log_total, keep, resid_t, grad_first, vec, embed):
    slots, width = acts[0].shape
    heights = tuple(t.shape[2] for t in terms)
    own_heights = width // 4
    rows = sum(heights) + 3 * own_heights
    slab = max(128, 16 * dp_n)
    count, nz = rows // slab, dp_n // 2
    bf16, f32 = jnp.bfloat16, jnp.float32
    dma, vmem = pltpu.SemaphoreType.DMA, pltpu.VMEM
    v_shape = vec.shape
    anywhere, inside = pl.BlockSpec(memory_space=pl.ANY), pl.BlockSpec(memory_space=pltpu.VMEM)
    rec_shape = (1, 2 * embed.shape[0], embed.shape[1])
    return pl.pallas_call(
        functools.partial(_backward_kernel, dp_n, slab, 1, heights, own_heights),
        out_shape=[
            jax.ShapeDtypeStruct((rows, width), bf16),
            jax.ShapeDtypeStruct(v_shape, f32),
            jax.ShapeDtypeStruct((dp_n, 4) + rec_shape, f32),
            jax.ShapeDtypeStruct((slots, width), bf16),
        ],
        in_specs=[anywhere] * (len(terms) + 7) + [inside] * 6,
        out_specs=[anywhere, inside, inside, inside],
        scratch_shapes=[
            vmem((count, 2, slab, width), bf16),
            vmem((count, 2, slab, width), bf16),
            vmem((count, slab, width), bf16),
            vmem((count, slab // 2, width), bf16),
            vmem((count, nz, slab // 2 // nz, width), bf16),
            vmem((4, slots, width), bf16),
            vmem((3, slots, width), bf16),
            vmem((3, width, width), bf16),
            vmem((1, width), f32),
            vmem(v_shape, f32),
            vmem(v_shape, f32),
            vmem(v_shape, f32),
            vmem(v_shape, f32),
            vmem((nz,) + v_shape, f32),
            vmem((3,) + v_shape, f32),
        ]
        + [dma((count + 1,)), dma((4,)), dma((3,))]
        + [dma((count,))] * 6
        + [dma((count, nz))] * 4
        + [dma((count,))] * 3
        + [dma((2 + nz,))] * 4,
        compiler_params=pltpu.CompilerParams(collective_id=1, has_side_effects=True, vmem_limit_bytes=66_000_000),
        name="attend_and_reduce",
    )(*terms, *acts, *weights, log_total, keep, resid_t, grad_first, vec, embed)


def split_heads(rows):
    return rows.reshape(rows.shape[0], rows.shape[1] // HEAD_DIM, HEAD_DIM)


def item_scores(queries, keys, key_valid):
    scores = jnp.einsum(
        "qhd,khd->hqk", split_heads(queries), split_heads(keys), preferred_element_type=jnp.float32
    ) * HEAD_DIM ** (-0.5)
    return jnp.where(key_valid[None, None, :], scores, neg_large)


def attend_forward(queries, keys, values, key_valid):
    masked = item_scores(queries, keys, key_valid)
    row_max = jnp.max(masked, axis=-1, keepdims=True)
    exp_scores = jnp.exp(masked - row_max)
    row_total = jnp.sum(exp_scores, axis=-1, keepdims=True)
    soft = (exp_scores / row_total).astype(jnp.bfloat16)
    mixed = jnp.einsum(
        "hqk,khd->qhd", soft, split_heads(values), preferred_element_type=jnp.float32
    )
    log_total = row_max[:, :, 0] + jnp.log(row_total[:, :, 0])
    return mixed.reshape(queries.shape).astype(jnp.bfloat16), log_total


def per_item(fn, item_count, slot_count, *arrays):
    if item_count == 1:
        return fn(*[a[0] for a in arrays])
    outs = lax.map(lambda packed: fn(*packed), arrays)
    return outs


def local(
    dp_n,
    tokens,
    time_embed,
    lengths,
    cotangent,
    w_query,
    w_key,
    w_value,
    w_out,
    w_time,
    w_in,
    w_down,
    b_query,
    b_value,
    b_out,
    b_time,
    b_in,
    b_down,
    gain_one,
    shift_one,
    gain_two,
    shift_two,
):
    f32, bf16 = jnp.float32, jnp.bfloat16
    seq_rank = lax.axis_index("seq")
    item_count = time_embed.shape[0]
    token_count = tokens.shape[0]
    slot_count = token_count // item_count
    width = tokens.shape[1]
    rows = w_time.shape[0]

    def mm(a, b, dims):
        return lax.dot_general(a, b, (dims, ((), ())), preferred_element_type=f32)

    full_time, full_query, full_key, full_value, full_out, full_in, full_down = gather_weights(
        [w_time, w_query, w_key, w_value, w_out, w_in, w_down]
    )
    own_lengths = lax.dynamic_slice_in_dim(lengths, seq_rank * item_count, item_count, 0)
    slot_index = lax.broadcasted_iota(jnp.int32, (item_count, slot_count), 1)
    own_valid = slot_index < own_lengths[:, None] + BLOCK
    row_keep = own_valid.reshape(token_count, 1).astype(f32)
    time_proj = mm(time_embed, full_time, ((1,), (0,))) + b_time.astype(f32)
    resid = (tokens.reshape(item_count, slot_count, width) + time_proj[:, None, :]).reshape(
        token_count, width
    )
    resid_low = resid.astype(bf16)
    query_rows = (mm(resid_low, full_query, ((1,), (0,))) + b_query.astype(f32)).astype(bf16)
    key_rows = mm(resid_low, full_key, ((1,), (0,))).astype(bf16)
    value_rows = (mm(resid_low, full_value, ((1,), (0,))) + b_value.astype(f32)).astype(bf16)

    def split_items(a):
        return a.reshape(item_count, slot_count, -1)

    qkv = [split_items(a) for a in (query_rows, key_rows, value_rows)]
    mixed, log_total = per_item(attend_forward, item_count, slot_count, *qkv, own_valid)
    mixed_rows = mixed.reshape(token_count, width)
    attn_out = mm(mixed_rows, full_out, ((1,), (0,))) + b_out.astype(f32)
    first_norm, first_pull = jax.vjp(
        layer_norm, resid + attn_out, gain_one.astype(f32), shift_one.astype(f32)
    )
    first_low = first_norm.astype(bf16)
    hidden_pre = mm(first_low, full_in, ((1,), (1,))) + b_in.astype(f32)
    hidden, gelu_slope = gelu_parts(hidden_pre)
    hidden_low = hidden.astype(bf16)
    ffn_out = mm(hidden_low, full_down, ((1,), (0,))) + b_down.astype(f32)
    second_norm, second_pull = jax.vjp(
        layer_norm, first_norm + ffn_out, gain_two.astype(f32), shift_two.astype(f32)
    )
    layer_out = (second_norm * row_keep).astype(bf16)
    grad_second_in, grad_gain_two, grad_shift_two = second_pull(cotangent.astype(f32) * row_keep)
    grad_ffn = grad_second_in.astype(bf16)
    grad_hidden = mm(grad_ffn, full_down, ((1,), (1,)))
    grad_pre = (grad_hidden * gelu_slope).astype(bf16)
    grad_first = grad_second_in + mm(grad_pre, full_in, ((1,), (0,)))
    term_in = mm(grad_pre, first_low, ((0,), (0,))).astype(bf16)
    term_down = mm(hidden_low, grad_ffn, ((0,), (0,))).astype(bf16)
    grad_first_in, grad_gain_one, grad_shift_one = first_pull(grad_first)
    grad_attn = grad_first_in.astype(bf16)
    grad_mixed = mm(grad_attn, full_out, ((1,), (1,))).astype(bf16)
    terms = [
        term_down,
        term_in,
        mm(mixed_rows, grad_attn, ((0,), (0,))).astype(bf16),
    ]
    zero = jnp.zeros((width,), f32)
    vec = jnp.stack(
        [
            zero,
            zero,
            jnp.sum(grad_attn, axis=0, dtype=f32),
            jnp.sum(grad_ffn, axis=0, dtype=f32),
            grad_gain_one,
            grad_shift_one,
            grad_gain_two,
            grad_shift_two,
        ]
    )
    vec = jnp.concatenate([vec, jnp.sum(grad_pre, axis=0, dtype=f32).reshape(-1, width)], axis=0)
    vec = jnp.pad(vec, ((0, -vec.shape[0] % 8), (0, 0)))
    sums, vectors, every, grad_tokens = attend_and_reduce(
        dp_n,
        [t.reshape(2, 2, -1, width) for t in terms],
        [query_rows, key_rows, value_rows, grad_mixed],
        [full_query, full_key, full_value],
        log_total,
        row_keep,
        resid_low.T,
        grad_first_in,
        vec,
        time_embed.astype(f32).reshape(-1, 128),
    )
    every = every.reshape(-1, 2, width)
    time_rows, time_grads = every[:, 0].astype(bf16), every[:, 1].astype(bf16)
    own_columns = lax.dynamic_slice_in_dim(time_rows, seq_rank * rows, rows, 1)
    grad_w_time = mm(own_columns, time_grads, ((0,), (0,)))
    grad_b_time = jnp.sum(time_grads, axis=0, dtype=f32)
    grad_b_in = vectors[8 : 8 + b_in.shape[0] // width].reshape(-1)
    sums = sums.astype(f32)
    down_rows, in_rows = (t.shape[0] // 4 for t in terms[:2])
    ends = [0, down_rows, down_rows + in_rows]
    ends += [ends[-1] + rows * i for i in range(1, 5)]
    share_down, share_in, share_out, share_q, share_k, share_v = (
        sums[lo:hi] for lo, hi in zip(ends[:-1], ends[1:])
    )
    return (
        layer_out,
        grad_tokens,
        share_q,
        share_k,
        share_v,
        share_out,
        grad_w_time,
        share_in,
        share_down,
        vectors[0],
        vectors[1],
        vectors[2],
        grad_b_time,
        grad_b_in,
        vectors[3],
        vectors[4],
        vectors[5],
        vectors[6],
        vectors[7],
    )


def solution(mesh):
    in_specs = (
        P(("dp", "seq"), None),
        P(("dp", "seq"), None),
        P("dp"),
        P(("dp", "seq"), None),
        P("seq", None),
        P("seq", None),
        P("seq", None),
        P("seq", None),
        P("seq", None),
        P("seq", None),
        P("seq", None),
        P(),
        P(),
        P(),
        P(),
        P(),
        P(),
        P(),
        P(),
        P(),
        P(),
    )
    out_specs = (
        P(("dp", "seq"), None),
        P(("dp", "seq"), None),
        P("seq", None),
        P("seq", None),
        P("seq", None),
        P("seq", None),
        P("seq", None),
        P("seq", None),
        P("seq", None),
        P(),
        P(),
        P(),
        P(),
        P(),
        P(),
        P(),
        P(),
        P(),
        P(),
    )
    return jax.shard_map(functools.partial(local, mesh.shape["dp"]), mesh=mesh, in_specs=in_specs, out_specs=out_specs, check_vma=False)
```

```python
import functools

import jax
import jax.numpy as jnp
from jax import lax
from jax.experimental import pallas as pl
from jax.experimental.pallas import tpu as pltpu
from jax.sharding import PartitionSpec as P

HEAD_DIM = 64
BLOCK = 25
MESH = pl.DeviceIdType.MESH


norm_eps = 1e-05
neg_large = -1e30


def layer_norm(values, gain, shift):
    center = values - jnp.mean(values, axis=-1, keepdims=True)
    spread = lax.rsqrt(jnp.mean(center * center, axis=-1, keepdims=True) + norm_eps)
    return center * spread * gain + shift


def gelu_parts(values):
    half = 0.5 + 0.5 * lax.erf(values * 0.5**0.5)
    density = jnp.exp(-0.5 * values * values) * (0.5 / jnp.pi) ** 0.5
    return values * half, half + values * density


def _gather_kernel(sizes, *refs):
    n = len(sizes)
    given, outs, ins = refs[:n], refs[n : 2 * n], refs[2 * n : 3 * n]
    load_sem, own_sem, c_send, c_recv, y_send, y_recv, x_send, x_recv, f_send, f_recv, g_send, g_recv = refs[3 * n :]
    dp, me = lax.axis_index("dp"), lax.axis_index("seq")
    half = lax.rem(dp, 2)
    loads = [pltpu.make_async_copy(given[a], ins[a], load_sem.at[a]) for a in range(n)]
    for load in loads:
        load.start()
    core, across, side = (dp, me ^ 1), (dp, me ^ 2), (dp ^ 1, me)
    barrier = pltpu.get_barrier_semaphore()
    for peer in (core, across, side):
        pl.semaphore_signal(barrier, inc=1, device_id=peer, device_id_type=MESH)
    pl.semaphore_wait(barrier, 3)

    def remote(src, dst, send, recv, peer):
        return pltpu.make_async_remote_copy(
            src_ref=src, dst_ref=dst, send_sem=send, recv_sem=recv, device_id=peer, device_id_type=MESH
        )

    chunks = []
    for a, rows in enumerate(sizes):
        step = min(rows // 2, 256)
        chunks += [(a, rows, off, step) for off in range(0, rows // 2, step)]

    def region(ref, rows, shard, part, off, step):
        start = pl.multiple_of(shard * rows + part * (rows // 2) + off, 16)
        return ref.at[pl.ds(start, step), :]

    waits = []
    crossing = []
    for j, (a, rows, off, step) in enumerate(chunks):
        if off == 0:
            loads[a].wait()
        src = region(ins[a], rows, 0, half, off, step)
        copy = remote(src, region(outs[a], rows, me, half, off, step), y_send.at[j], y_recv.at[j], across)
        copy.start()
        crossing.append(copy)
    core_copies = []
    for a, rows in enumerate(sizes):
        home = outs[a].at[pl.ds(pl.multiple_of(me * rows, 16), rows), :]
        copy = remote(ins[a], home, c_send.at[a], c_recv.at[a], core)
        copy.start()
        core_copies.append(copy)
        keep = pltpu.make_async_copy(ins[a], home, own_sem.at[a])
        keep.start()
        waits.append(keep)
    sides, firsts, seconds = [], [], []
    for j in range(len(chunks) + 1):
        if j < len(chunks):
            a, rows, off, step = chunks[j]
            crossing[j].wait_recv()
            got = region(outs[a], rows, me ^ 2, half, off, step)
            copy = remote(got, got, x_send.at[j], x_recv.at[j], side)
            copy.start()
            sides.append(copy)
            copy = remote(got, got, f_send.at[j], f_recv.at[j], core)
            copy.start()
            firsts.append(copy)
        if j >= 1:
            a, rows, off, step = chunks[j - 1]
            sides[j - 1].wait_recv()
            got = region(outs[a], rows, me ^ 2, 1 - half, off, step)
            copy = remote(got, got, g_send.at[j - 1], g_recv.at[j - 1], core)
            copy.start()
            seconds.append(copy)
    for copy in waits:
        copy.wait()
    for copy in crossing + sides:
        copy.wait_send()
    for copy in core_copies + firsts + seconds:
        copy.wait()


def gather_weights(arrays):
    sizes = tuple(a.shape[0] for a in arrays)
    n = len(arrays)
    m = sum(max(1, r // 512) for r in sizes)
    dma = pltpu.SemaphoreType.DMA
    return pl.pallas_call(
        functools.partial(_gather_kernel, sizes),
        out_shape=[jax.ShapeDtypeStruct((4 * a.shape[0], a.shape[1]), a.dtype) for a in arrays],
        in_specs=[pl.BlockSpec(memory_space=pl.ANY)] * n,
        out_specs=[pl.BlockSpec(memory_space=pl.ANY)] * n,
        scratch_shapes=[pltpu.VMEM(a.shape, a.dtype) for a in arrays] + [dma((n,))] * 4 + [dma((m,))] * 8,
        compiler_params=pltpu.CompilerParams(
            collective_id=0, has_side_effects=True, vmem_limit_bytes=66_000_000
        ),
        name="gather_weights",
    )(*arrays)


def _row_loop(rows, step, body):
    def run(i, carry):
        body(pl.ds(pl.multiple_of(i * step, step), step))
        return carry

    lax.fori_loop(0, rows // step, run, 0)


def _backward_kernel(dp_n, slab, lag, heights, own_heights, *refs):
    n_terms = len(heights)
    terms = refs[:n_terms]
    (query, key, value, grad_mixed, w_query, w_key, w_value, log_total, keep, resid_t, grad_first, vec, embed) = refs[
        n_terms : n_terms + 13
    ]
    out, vec_out, rec_out, grad_tokens = refs[n_terms + 13 : n_terms + 17]
    (own, core_in, y_in, x_in, z_in, act, grads, weights, time_sum, v_own, v_core, v_y, v_x, v_z, v_sum) = refs[
        n_terms + 17 : n_terms + 32
    ]
    (load_sem, act_sem, w_sem, c_s, c_r, y_s, y_r, x_s, x_r, z_s, z_r, zg_s, zg_r, xg_s, xg_r, out_sem) = refs[
        n_terms + 32 : n_terms + 48
    ]
    vs, vr, ws, wr = refs[n_terms + 48 :]
    f32, bf16 = jnp.float32, jnp.bfloat16
    count = out.shape[0] // slab
    nz = dp_n // 2
    scale = HEAD_DIM**-0.5
    slots, width = query.shape
    pair = 2 * HEAD_DIM
    pairs = width // pair
    dp, me = lax.axis_index("dp"), lax.axis_index("seq")
    x, z, y, c = lax.rem(dp, 2), lax.div(dp, 2), lax.div(me, 2), lax.rem(me, 2)
    core, across, side = (dp, me ^ 1), (dp, me ^ 2), (dp ^ 1, me)
    others = [(lax.rem(z + o, nz) * 2 + x, me) for o in range(1, nz)]

    act_loads = [
        pltpu.make_async_copy(src, act.at[i], act_sem.at[i]) for i, src in enumerate((query, key, value, grad_mixed))
    ]
    w_loads = [pltpu.make_async_copy(src, weights.at[i], w_sem.at[i]) for i, src in enumerate((w_query, w_key, w_value))]
    for load in act_loads:
        load.start()
    barrier = pltpu.get_barrier_semaphore()
    for peer in [core, across, side] + others:
        pl.semaphore_signal(barrier, inc=1, device_id=peer, device_id_type=MESH)
    pl.semaphore_wait(barrier, 3 + len(others))

    def remote(src, dst, send, recv, peer):
        return pltpu.make_async_remote_copy(
            src_ref=src, dst_ref=dst, send_sem=send, recv_sem=recv, device_id=peer, device_id_type=MESH
        )

    hs = slab // 2
    ps = hs // nz
    rs = min(ps, 32)
    given = sum(heights)
    full = given // slab

    row = 0
    ahead = 5
    issues = []
    for term, height in zip(terms, heights):
        step = min(height, slab)
        for off in range(0, height, step):
            issues.append((term, off, (row + off) // slab, (row + off) % slab, step))
        row += height

    def issue(term, off, k, at, step):
        rows, place = pl.ds(off, step), pl.ds(at, step)
        remote(term.at[:, 1 - c, rows, :], core_in.at[k, :, place, :], c_s.at[k], c_r.at[k], core).start()
        sem = load_sem.at[k] if not isinstance(k, int) or k < full else load_sem.at[count]
        pltpu.make_async_copy(term.at[:, c, rows, :], own.at[k, :, place, :], sem).start()

    upfront = slab > own_heights
    for k, entry in enumerate(issues):
        if upfront or k < ahead:
            issue(*entry)

    def issue_later(k):
        start = 0
        for term, height in zip(terms, heights):
            first, last = start // slab, (start + height) // slab

            @pl.when((k >= first) & (k < last))
            def _():
                off = pl.multiple_of((k - first) * slab, slab)
                issue(term, off, k, 0, slab)

            start += height

    for load in w_loads:
        load.start()

    def core_copy(k):
        return remote(core_in.at[k], core_in.at[k], c_s.at[k], c_r.at[k], core)

    def y_copy(k):
        return remote(own.at[k, 1 - y], y_in.at[k], y_s.at[k], y_r.at[k], across)

    def x_copy(k):
        give = pl.ds(pl.multiple_of((1 - x) * hs, 16), hs)
        return remote(own.at[k, y, give], x_in.at[k], x_s.at[k], x_r.at[k], side)

    def z_copy(k, o):
        piece = pl.ds(pl.multiple_of(x * hs + lax.rem(z + o, nz) * ps, 16), ps)
        return remote(own.at[k, y, piece], z_in.at[k, o], z_s.at[k, o], z_r.at[k, o], others[o - 1])

    def zg_copy(k, o):
        mine = own.at[k, 1 - y, pl.ds(pl.multiple_of(x * hs + z * ps, 16), ps)]
        return remote(mine, mine, zg_s.at[k, o], zg_r.at[k, o], others[o - 1])

    def xg_copy(k):
        mine = own.at[k, 1 - y, pl.ds(pl.multiple_of(x * hs, 16), hs)]
        return remote(mine, mine, xg_s.at[k], xg_r.at[k], side)

    def out_copy(k):
        rows = pl.ds(pl.multiple_of(k * slab, slab), slab)
        return pltpu.make_async_copy(own.at[k, 1 - y], out.at[rows, :], out_sem.at[k])

    def stage_core(k):
        @pl.when(k < full)
        def _():
            pltpu.make_async_copy(own.at[k], own.at[k], load_sem.at[k]).wait()

        core_copy(k).wait_recv()

        def add(r):
            for p in range(2):
                own[k, p, r] = (own[k, p, r].astype(f32) + core_in[k, p, r].astype(f32)).astype(bf16)

        _row_loop(slab, 16, add)
        y_copy(k).start()

    def stage_y(k):
        y_copy(k).wait()

        def add(r):
            own[k, y, r] = (own[k, y, r].astype(f32) + y_in[k, r].astype(f32)).astype(bf16)

        _row_loop(slab, 32, add)
        x_copy(k).start()

    def stage_x(k):
        x_copy(k).wait_recv()

        def add(r):
            at = pl.ds(pl.multiple_of(x * hs + r.start, 16), r.size)
            own[k, y, at] = (own[k, y, at].astype(f32) + x_in[k, r].astype(f32)).astype(bf16)

        _row_loop(hs, rs, add)
        for o in range(1, nz):
            z_copy(k, o).start()

    def stage_z(k):
        for o in range(1, nz):
            z_copy(k, o).wait_recv()

        def add(r):
            at = pl.ds(pl.multiple_of(x * hs + z * ps + r.start, 16), r.size)
            total = own[k, y, at].astype(f32)
            for o in range(1, nz):
                total += z_in[k, o, r].astype(f32)
            own[k, 1 - y, at] = total.astype(bf16)

        _row_loop(ps, rs, add)
        for o in range(1, nz):
            zg_copy(k, o).start()

    def stage_zg(k):
        for o in range(1, nz):
            zg_copy(k, o).wait_recv()
        xg_copy(k).start()

    def stage_xg(k):
        xg_copy(k).wait_recv()
        out_copy(k).start()

    def dot(a, b, dims):
        return lax.dot_general(a, b, (dims, ((), ())), preferred_element_type=f32)

    def head_pair(p):
        cols = pl.ds(pl.multiple_of(p * pair, pair), pair)
        q2, k2, v2, g2 = (act[i, :, cols] for i in range(4))
        first = lax.broadcasted_iota(jnp.int32, (1, pair), 1) < HEAD_DIM
        kept = keep[...] > 0
        found = []
        for h in range(2):
            mask = jnp.where(first == (h == 0), 1.0, 0.0)
            q_h = q2 * (mask * scale).astype(bf16)
            g_h = g2 * mask.astype(bf16)
            scores = dot(k2, q_h, ((1,), (1,)))
            soft = jnp.where(kept, jnp.exp(scores - log_total[pl.ds(2 * p + h, 1), :]), 0.0)
            grad_soft = dot(v2, g_h, ((1,), (1,)))
            inner = jnp.sum(soft * grad_soft, axis=0, keepdims=True)
            grad_scores = (soft * (grad_soft - inner)).astype(bf16)
            found.append(
                (
                    dot(k2, grad_scores, ((0,), (0,))),
                    dot(grad_scores, q2, ((1,), (0,))),
                    dot(soft.astype(bf16), g2, ((1,), (0,))),
                )
            )
        q_t = jnp.concatenate([found[0][0][:HEAD_DIM], found[1][0][HEAD_DIM:]], axis=0)
        grad_q = (q_t.T * scale).astype(bf16)
        grad_k = (jnp.where(first, found[0][1], found[1][1]) * scale).astype(bf16)
        grad_v = jnp.where(first, found[0][2], found[1][2]).astype(bf16)
        grads[0, :, cols] = grad_q
        grads[1, :, cols] = grad_k
        grads[2, :, cols] = grad_v
        v_own[0:1, cols] = jnp.sum(grad_q.astype(f32), axis=0, keepdims=True)
        v_own[1:2, cols] = jnp.sum(grad_v.astype(f32), axis=0, keepdims=True)

    def term(m):
        step = min(own_heights, slab)
        for cc, mine in ((1 - c, False), (c, True)):
            for p in range(2):
                left = resid_t[pl.ds(pl.multiple_of((p * 2 + cc) * own_heights, own_heights), own_heights), :]
                tile = dot(left, grads[m], ((1,), (0,))).astype(bf16)
                if not mine:
                    act[m, p * own_heights : (p + 1) * own_heights] = tile
                for off in range(0, own_heights, step):
                    start = given + m * own_heights + off
                    k, at = lax.div(start, slab), pl.multiple_of(lax.rem(start, slab), step)
                    if mine:
                        own[k, p, pl.ds(at, step)] = tile[off : off + step]
                    else:
                        src = act.at[m, pl.ds(p * own_heights + off, step), :]
                        dst = core_in.at[k, p, pl.ds(at, step), :]
                        remote(src, dst, c_s.at[k], c_r.at[k], core).start()

    blocks = 4
    block = slots // blocks

    def resid_rows(r):
        rows = pl.ds(pl.multiple_of(r * block, block), block)
        total = grad_first[rows, :]
        for m in range(3):
            total += dot(grads[m, rows, :], weights[m], ((1,), (1,)))
        grad_tokens[rows, :] = total.astype(bf16)
        time_sum[...] += jnp.sum(total, axis=0, keepdims=True)

    v_half = v_core.shape[0]
    v_mine = pl.ds(pl.multiple_of(c * v_half, v_half), v_half)
    v_given = pl.ds(pl.multiple_of((1 - c) * v_half, v_half), v_half)

    def v_copy(i):
        peers = [core, across, side] + others + [core]
        if i == 0:
            src, dst = v_own.at[v_given], v_core
        elif i == 2 + nz:
            src = dst = vec_out.at[v_mine]
        else:
            src, dst = v_sum.at[min(i, 3) - 1], v_z.at[i - 2] if i > 2 else (v_y, v_x)[i - 1]
        return remote(src, dst, vs.at[i], vr.at[i], peers[i])

    def v_stage(i):
        if i == 0:
            v_copy(0).start()
        elif i <= 3:
            v_copy(i - 1).wait_recv()
            before = v_own[v_mine] if i == 1 else v_sum[i - 2]
            v_sum[i - 1] = before + (v_core, v_y, v_x)[i - 1][...]
            for j in range(i, i + 1 if i < 3 else 2 + nz):
                v_copy(j).start()
        elif i == 4:
            total = v_sum[2]
            for o in range(1, nz):
                v_copy(2 + o).wait_recv()
                total = total + v_z[o]
            vec_out[v_mine] = total
            v_copy(2 + nz).start()
        else:
            v_copy(2 + nz).wait_recv()

    def w_copy(q, i):
        peers = [across, side] + others + [core]
        if i == 0:
            part = rec_out.at[q, dp, y, c]
        elif i == 1:
            part = rec_out.at[q, dp, :, c]
        elif i < 1 + nz:
            part = rec_out.at[q, pl.ds(z * 2, 2), :, c]
        else:
            part = rec_out.at[q, :, :, c]
        return remote(part, part, ws.at[q, i], wr.at[q, i], peers[i])

    def w_stage(q, i):
        if i == 0:
            if q == 0:
                rec_out[0, dp, y, c] = embed[...]
            else:
                rounded = time_sum[...].astype(bf16).astype(f32)
                lanes = embed.shape[-1]
                for j in range(width // lanes):
                    rec_out[1, dp, y, c, j : j + 1, :] = rounded[:, j * lanes : (j + 1) * lanes]
            w_copy(q, 0).start()
        elif i < 3:
            w_copy(q, i - 1).wait_recv()
            for j in range(i, i + 1 if i == 1 else 1 + nz):
                w_copy(q, j).start()
        elif i == 3:
            for o in range(1, nz):
                w_copy(q, 1 + o).wait_recv()
            w_copy(q, 1 + nz).start()
        else:
            w_copy(q, 1 + nz).wait_recv()

    stages = [stage_y, stage_x, stage_z, stage_zg, stage_xg]
    n_units = pairs + 3 + blocks
    base = 0 if slab <= own_heights else pairs + 4
    small = [(pairs + at, functools.partial(v_stage, i)) for i, at in enumerate((0, 2, 5, 7, 9, 10))]
    for q, first in ((0, 0), (1, n_units)):
        small += [(first + at, functools.partial(w_stage, q, i)) for i, at in enumerate((0, 3, 5, 7, 8))]
    ticks = max([base + count + lag * (len(stages) - 1)] + [at + 1 for at, _ in small])
    v_own[...] = vec[...]
    time_sum[...] = jnp.zeros_like(time_sum)
    for load in act_loads:
        load.wait()

    def tick(t, carry):
        @pl.when(t < pairs)
        def _():
            head_pair(t)

        @pl.when((t >= pairs) & (t < pairs + 3))
        def _():
            term(t - pairs)

        @pl.when(t == pairs + 3)
        def _():
            for load in w_loads:
                load.wait()

        @pl.when((t >= pairs + 3) & (t < n_units))
        def _():
            resid_rows(t - pairs - 3)

        if row > full * slab:

            @pl.when(t == base)
            def _():
                part = own.at[full, :, pl.ds(0, row - full * slab), :]
                pltpu.make_async_copy(part, part, load_sem.at[count]).wait()

        if not upfront:
            issue_later(t - base + ahead)

        for i in range(3):
            k = t - base + i

            @pl.when((k < count) & ((t == base) | ((t > base) & (i == 2))))
            def _():
                stage_core(k)

        for d, stage in enumerate(stages):
            k = t - base - d * lag

            @pl.when((k >= 0) & (k < count))
            def _():
                stage(k)

        for at, run in small:
            pl.when(t == at)(run)

        return carry

    lax.fori_loop(0, ticks, tick, 0)

    def finish(k, carry):
        core_copy(k).wait_send()
        x_copy(k).wait_send()
        for o in range(1, nz):
            z_copy(k, o).wait_send()
            zg_copy(k, o).wait_send()
        xg_copy(k).wait_send()
        out_copy(k).wait()
        return carry

    lax.fori_loop(0, count, finish, 0)
    for i in range(3 + nz):
        v_copy(i).wait_send()
    for i in range(2 + nz):
        for q in range(2):
            w_copy(q, i).wait_send()


def attend_and_reduce(dp_n, terms, acts, weights, log_total, keep, resid_t, grad_first, vec, embed):
    slots, width = acts[0].shape
    heights = tuple(t.shape[2] for t in terms)
    own_heights = width // 4
    rows = sum(heights) + 3 * own_heights
    slab = max(128, 16 * dp_n)
    count, nz = rows // slab, dp_n // 2
    bf16, f32 = jnp.bfloat16, jnp.float32
    dma, vmem = pltpu.SemaphoreType.DMA, pltpu.VMEM
    v_shape = vec.shape
    anywhere, inside = pl.BlockSpec(memory_space=pl.ANY), pl.BlockSpec(memory_space=pltpu.VMEM)
    half_shape = (v_shape[0] // 2, width)
    return pl.pallas_call(
        functools.partial(_backward_kernel, dp_n, slab, 1, heights, own_heights),
        out_shape=[
            jax.ShapeDtypeStruct((rows, width), bf16),
            jax.ShapeDtypeStruct(v_shape, f32),
            jax.ShapeDtypeStruct((2, dp_n, 2, 2) + embed.shape, f32),
            jax.ShapeDtypeStruct((slots, width), bf16),
        ],
        in_specs=[anywhere] * (len(terms) + 7) + [inside] * 6,
        out_specs=[anywhere, inside, inside, inside],
        scratch_shapes=[
            vmem((count, 2, slab, width), bf16),
            vmem((count, 2, slab, width), bf16),
            vmem((count, slab, width), bf16),
            vmem((count, slab // 2, width), bf16),
            vmem((count, nz, slab // 2 // nz, width), bf16),
            vmem((4, slots, width), bf16),
            vmem((3, slots, width), bf16),
            vmem((3, width, width), bf16),
            vmem((1, width), f32),
            vmem(v_shape, f32),
            vmem(half_shape, f32),
            vmem(half_shape, f32),
            vmem(half_shape, f32),
            vmem((nz,) + half_shape, f32),
            vmem((3,) + half_shape, f32),
        ]
        + [dma((count + 1,)), dma((4,)), dma((3,))]
        + [dma((count,))] * 6
        + [dma((count, nz))] * 4
        + [dma((count,))] * 3
        + [dma((3 + nz,))] * 2
        + [dma((2, 2 + nz))] * 2,
        compiler_params=pltpu.CompilerParams(collective_id=1, has_side_effects=True, vmem_limit_bytes=66_000_000),
        name="attend_and_reduce",
    )(*terms, *acts, *weights, log_total, keep, resid_t, grad_first, vec, embed)


def split_heads(rows):
    return rows.reshape(rows.shape[0], rows.shape[1] // HEAD_DIM, HEAD_DIM)


def item_scores(queries, keys, key_valid):
    scores = jnp.einsum(
        "qhd,khd->hqk", split_heads(queries), split_heads(keys), preferred_element_type=jnp.float32
    ) * HEAD_DIM ** (-0.5)
    return jnp.where(key_valid[None, None, :], scores, neg_large)


def attend_forward(queries, keys, values, key_valid):
    masked = item_scores(queries, keys, key_valid)
    row_max = jnp.max(masked, axis=-1, keepdims=True)
    exp_scores = jnp.exp(masked - row_max)
    row_total = jnp.sum(exp_scores, axis=-1, keepdims=True)
    soft = (exp_scores / row_total).astype(jnp.bfloat16)
    mixed = jnp.einsum(
        "hqk,khd->qhd", soft, split_heads(values), preferred_element_type=jnp.float32
    )
    log_total = row_max[:, :, 0] + jnp.log(row_total[:, :, 0])
    return mixed.reshape(queries.shape).astype(jnp.bfloat16), log_total


def per_item(fn, item_count, slot_count, *arrays):
    if item_count == 1:
        return fn(*[a[0] for a in arrays])
    outs = lax.map(lambda packed: fn(*packed), arrays)
    return outs


def local(
    dp_n,
    tokens,
    time_embed,
    lengths,
    cotangent,
    w_query,
    w_key,
    w_value,
    w_out,
    w_time,
    w_in,
    w_down,
    b_query,
    b_value,
    b_out,
    b_time,
    b_in,
    b_down,
    gain_one,
    shift_one,
    gain_two,
    shift_two,
):
    f32, bf16 = jnp.float32, jnp.bfloat16
    seq_rank = lax.axis_index("seq")
    item_count = time_embed.shape[0]
    token_count = tokens.shape[0]
    slot_count = token_count // item_count
    width = tokens.shape[1]
    rows = w_time.shape[0]

    def mm(a, b, dims):
        return lax.dot_general(a, b, (dims, ((), ())), preferred_element_type=f32)

    full_time, full_query, full_key, full_value, full_out, full_in, full_down = gather_weights(
        [w_time, w_query, w_key, w_value, w_out, w_in, w_down]
    )
    own_lengths = lax.dynamic_slice_in_dim(lengths, seq_rank * item_count, item_count, 0)
    slot_index = lax.broadcasted_iota(jnp.int32, (item_count, slot_count), 1)
    own_valid = slot_index < own_lengths[:, None] + BLOCK
    row_keep = own_valid.reshape(token_count, 1).astype(f32)
    time_proj = mm(time_embed, full_time, ((1,), (0,))) + b_time.astype(f32)
    resid = (tokens.reshape(item_count, slot_count, width) + time_proj[:, None, :]).reshape(
        token_count, width
    )
    resid_low = resid.astype(bf16)
    query_rows = (mm(resid_low, full_query, ((1,), (0,))) + b_query.astype(f32)).astype(bf16)
    key_rows = mm(resid_low, full_key, ((1,), (0,))).astype(bf16)
    value_rows = (mm(resid_low, full_value, ((1,), (0,))) + b_value.astype(f32)).astype(bf16)

    def split_items(a):
        return a.reshape(item_count, slot_count, -1)

    qkv = [split_items(a) for a in (query_rows, key_rows, value_rows)]
    mixed, log_total = per_item(attend_forward, item_count, slot_count, *qkv, own_valid)
    mixed_rows = mixed.reshape(token_count, width)
    attn_out = mm(mixed_rows, full_out, ((1,), (0,))) + b_out.astype(f32)
    first_norm, first_pull = jax.vjp(
        layer_norm, resid + attn_out, gain_one.astype(f32), shift_one.astype(f32)
    )
    first_low = first_norm.astype(bf16)
    hidden_pre = mm(first_low, full_in, ((1,), (1,))) + b_in.astype(f32)
    hidden, gelu_slope = gelu_parts(hidden_pre)
    hidden_low = hidden.astype(bf16)
    ffn_out = mm(hidden_low, full_down, ((1,), (0,))) + b_down.astype(f32)
    second_norm, second_pull = jax.vjp(
        layer_norm, first_norm + ffn_out, gain_two.astype(f32), shift_two.astype(f32)
    )
    layer_out = (second_norm * row_keep).astype(bf16)
    grad_second_in, grad_gain_two, grad_shift_two = second_pull(cotangent.astype(f32) * row_keep)
    grad_ffn = grad_second_in.astype(bf16)
    grad_hidden = mm(grad_ffn, full_down, ((1,), (1,)))
    grad_pre = (grad_hidden * gelu_slope).astype(bf16)
    grad_first = grad_second_in + mm(grad_pre, full_in, ((1,), (0,)))
    term_in = mm(grad_pre, first_low, ((0,), (0,))).astype(bf16)
    term_down = mm(hidden_low, grad_ffn, ((0,), (0,))).astype(bf16)
    grad_first_in, grad_gain_one, grad_shift_one = first_pull(grad_first)
    grad_attn = grad_first_in.astype(bf16)
    grad_mixed = mm(grad_attn, full_out, ((1,), (1,))).astype(bf16)
    terms = [
        term_down,
        term_in,
        mm(mixed_rows, grad_attn, ((0,), (0,))).astype(bf16),
    ]
    zero = jnp.zeros((width,), f32)
    vec = jnp.stack(
        [
            zero,
            zero,
            jnp.sum(grad_attn, axis=0, dtype=f32),
            jnp.sum(grad_ffn, axis=0, dtype=f32),
            grad_gain_one,
            grad_shift_one,
            grad_gain_two,
            grad_shift_two,
        ]
    )
    vec = jnp.concatenate([vec, jnp.sum(grad_pre, axis=0, dtype=f32).reshape(-1, width)], axis=0)
    vec = jnp.pad(vec, ((0, -vec.shape[0] % 8), (0, 0)))
    sums, vectors, every, grad_tokens = attend_and_reduce(
        dp_n,
        [t.reshape(2, 2, -1, width) for t in terms],
        [query_rows, key_rows, value_rows, grad_mixed],
        [full_query, full_key, full_value],
        log_total,
        row_keep,
        resid_low.T,
        grad_first_in,
        vec,
        time_embed.astype(f32).reshape(-1, 128),
    )
    time_rows, time_grads = every.reshape(2, -1, width).astype(bf16)
    own_columns = lax.dynamic_slice_in_dim(time_rows, seq_rank * rows, rows, 1)
    grad_w_time = mm(own_columns, time_grads, ((0,), (0,)))
    grad_b_time = jnp.sum(time_grads, axis=0, dtype=f32)
    grad_b_in = vectors[8 : 8 + b_in.shape[0] // width].reshape(-1)
    sums = sums.astype(f32)
    down_rows, in_rows = (t.shape[0] // 4 for t in terms[:2])
    ends = [0, down_rows, down_rows + in_rows]
    ends += [ends[-1] + rows * i for i in range(1, 5)]
    share_down, share_in, share_out, share_q, share_k, share_v = (
        sums[lo:hi] for lo, hi in zip(ends[:-1], ends[1:])
    )
    return (
        layer_out,
        grad_tokens,
        share_q,
        share_k,
        share_v,
        share_out,
        grad_w_time,
        share_in,
        share_down,
        vectors[0],
        vectors[1],
        vectors[2],
        grad_b_time,
        grad_b_in,
        vectors[3],
        vectors[4],
        vectors[5],
        vectors[6],
        vectors[7],
    )


def solution(mesh):
    in_specs = (
        P(("dp", "seq"), None),
        P(("dp", "seq"), None),
        P("dp"),
        P(("dp", "seq"), None),
        P("seq", None),
        P("seq", None),
        P("seq", None),
        P("seq", None),
        P("seq", None),
        P("seq", None),
        P("seq", None),
        P(),
        P(),
        P(),
        P(),
        P(),
        P(),
        P(),
        P(),
        P(),
        P(),
    )
    out_specs = (
        P(("dp", "seq"), None),
        P(("dp", "seq"), None),
        P("seq", None),
        P("seq", None),
        P("seq", None),
        P("seq", None),
        P("seq", None),
        P("seq", None),
        P("seq", None),
        P(),
        P(),
        P(),
        P(),
        P(),
        P(),
        P(),
        P(),
        P(),
        P(),
    )
    return jax.shard_map(functools.partial(local, mesh.shape["dp"]), mesh=mesh, in_specs=in_specs, out_specs=out_specs, check_vma=False)
```

```python
import functools

import jax
import jax.numpy as jnp
from jax import lax
from jax.experimental import pallas as pl
from jax.experimental.pallas import tpu as pltpu
from jax.sharding import PartitionSpec as P

HEAD_DIM = 64
BLOCK = 25
MESH = pl.DeviceIdType.MESH


norm_eps = 1e-05
neg_large = -1e30


def layer_norm(values, gain, shift):
    center = values - jnp.mean(values, axis=-1, keepdims=True)
    spread = lax.rsqrt(jnp.mean(center * center, axis=-1, keepdims=True) + norm_eps)
    return center * spread * gain + shift


def gelu_parts(values):
    half = 0.5 + 0.5 * lax.erf(values * 0.5**0.5)
    density = jnp.exp(-0.5 * values * values) * (0.5 / jnp.pi) ** 0.5
    return values * half, half + values * density


def _forward_kernel(sizes, *refs):
    n = len(sizes)
    given, (tokens, embed, rows_in, bias_in, keep) = refs[:n], refs[n : n + 5]
    outs = refs[n + 5 : 2 * n + 5]
    (resid_out, query_out, key_out, value_out, mixed_out, pre_out, hidden_out, slope_out, ffn_out, log_total) = refs[
        2 * n + 5 : 2 * n + 15
    ]
    full = refs[2 * n + 15 : 3 * n + 15]
    act, pre, first_low, hidden, slope, total = refs[3 * n + 15 : 3 * n + 21]
    load_sem, save_sem, act_sem, c_send, c_recv, y_send, y_recv, x_send, x_recv, f_send, f_recv, g_send, g_recv = refs[
        3 * n + 21 :
    ]
    f32, bf16 = jnp.float32, jnp.bfloat16
    w_time, w_query, w_key, w_value, w_out, w_in, w_down = full
    slots, width = tokens.shape
    pair = 2 * HEAD_DIM
    scale = HEAD_DIM**-0.5
    dp, me = lax.axis_index("dp"), lax.axis_index("seq")
    half = lax.rem(dp, 2)

    def home(a, shard):
        return full[a].at[pl.ds(pl.multiple_of(shard * sizes[a], sizes[a]), sizes[a]), :]

    loads = [pltpu.make_async_copy(given[a], home(a, me), load_sem.at[a]) for a in range(n)]
    for load in loads:
        load.start()
    core, across, side = (dp, me ^ 1), (dp, me ^ 2), (dp ^ 1, me)
    barrier = pltpu.get_barrier_semaphore()
    for peer in (core, across, side):
        pl.semaphore_signal(barrier, inc=1, device_id=peer, device_id_type=MESH)
    pl.semaphore_wait(barrier, 3)

    def remote(src, send, recv, peer):
        return pltpu.make_async_remote_copy(
            src_ref=src, dst_ref=src, send_sem=send, recv_sem=recv, device_id=peer, device_id_type=MESH
        )

    chunks, of = [], [[] for _ in sizes]
    for a, rows in enumerate(sizes):
        step = min(rows // 2, 128)
        for off in range(0, rows // 2, step):
            of[a].append(len(chunks))
            chunks.append((a, rows, off, step))

    def region(j, shard, part):
        a, rows, off, step = chunks[j]
        start = pl.multiple_of(shard * rows + part * (rows // 2) + off, 16)
        return full[a].at[pl.ds(start, step), :]

    saves = []

    def crossing(j):
        return remote(region(j, me, half), y_send.at[j], y_recv.at[j], across)

    def core_copy(a):
        return remote(home(a, me), c_send.at[a], c_recv.at[a], core)

    def sideways(j):
        return remote(region(j, me ^ 2, half), x_send.at[j], x_recv.at[j], side)

    def first_half(j):
        return remote(region(j, me ^ 2, half), f_send.at[j], f_recv.at[j], core)

    def second_half(j):
        return remote(region(j, me ^ 2, 1 - half), g_send.at[j], g_recv.at[j], core)

    for j, (a, rows, off, _) in enumerate(chunks):
        if off == 0:
            loads[a].wait()
            core_copy(a).start()
        crossing(j).start()

    def step(j):
        crossing(j).wait_recv()
        sideways(j).start()
        first_half(j).start()

    def turn(j):
        sideways(j).wait_recv()
        second_half(j).start()

    def arrived(j):
        first_half(j).wait_recv()
        second_half(j).wait_recv()

    def save(src, dst, sem):
        copy = pltpu.make_async_copy(src, dst, sem)
        copy.start()
        saves.append(copy)

    def complete(a):
        for j in of[a]:
            arrived(j)
        core_copy(a).wait_recv()
        save(full[a], outs[a], save_sem.at[a])

    def dot(a, b, dims):
        return lax.dot_general(a, b, (dims, ((), ())), preferred_element_type=f32)

    def bias(i):
        return rows_in[i : i + 1, :]

    tile = 256

    def tiles(extent, size, body):
        def run(i, carry):
            body(pl.ds(pl.multiple_of(i * size, size), size))
            return carry

        lax.fori_loop(0, extent // size, run, 0)

    def project(weight, i, row):
        def body(cols):
            value = dot(act[0], weight[:, cols], ((1,), (0,)))
            if row is not None:
                value += rows_in[row : row + 1, cols]
            act[i, :, cols] = value.astype(bf16)

        tiles(width, tile, body)
        save(act.at[i], (resid_out, query_out, key_out, value_out)[i], act_sem.at[i])

    step(0)
    step(1)
    turn(0)
    complete(0)
    time_proj = dot(embed[...], w_time[...], ((1,), (0,)))[0:1] + bias(0)

    def enter(r):
        value = tokens[r, :].astype(f32) + time_proj
        pre[r, :] = value
        act[0, r, :] = value.astype(bf16)

    tiles(slots, 64, enter)
    save(act.at[0], resid_out, act_sem.at[0])
    for j, (weight, row) in enumerate(((w_query, 1), (w_key, None), (w_value, 2))):
        step(j + 2)
        turn(j + 1)
        complete(j + 1)
        project(weight, j + 1, row)

    first = lax.broadcasted_iota(jnp.int32, (1, pair), 1) < HEAD_DIM

    def head_pair(p):
        cols = pl.ds(pl.multiple_of(p * pair, pair), pair)
        q2, k2, v2 = (act[i, :, cols] for i in (1, 2, 3))
        kept = keep[...] > 0
        found = []
        for h in range(2):
            mask = jnp.where(first == (h == 0), scale, 0.0)
            scores = jnp.where(kept, dot(k2, q2 * mask.astype(bf16), ((1,), (1,))), neg_large)
            top = jnp.max(scores, axis=0, keepdims=True)
            weights = jnp.exp(scores - top)
            norm = jnp.sum(weights, axis=0, keepdims=True)
            soft = (weights * (1.0 / norm)).astype(bf16)
            log_total[pl.ds(2 * p + h, 1), :] = top + jnp.log(norm)
            found.append(dot(v2, soft, ((0,), (0,))))
        mixed = jnp.concatenate([found[0][:HEAD_DIM], found[1][HEAD_DIM:]], axis=0)
        act[4, :, cols] = mixed.T.astype(bf16)

    beside = {0: (None, 4), 1: (5, None), 3: (6, 5), 5: (7, 6), 7: (8, 7)}

    def attend(p, carry):
        for at, (enters, turns) in beside.items():

            @pl.when(p == at)
            def _():
                if enters is not None:
                    step(enters)
                if turns is not None:
                    turn(turns)

        head_pair(p)
        return carry

    lax.fori_loop(0, width // pair, attend, 0)
    save(act.at[4], mixed_out, act_sem.at[4])
    complete(4)

    def attn_out(cols):
        pre[:, cols] += dot(act[4], w_out[:, cols], ((1,), (0,))) + rows_in[3:4, cols]

    tiles(width, tile, attn_out)
    step(9)
    turn(8)
    save(pre, pre_out, act_sem.at[5])

    def norm_rows(r):
        first_low[r, :] = layer_norm(pre[r, :], bias(4), bias(5)).astype(bf16)

    tiles(slots, 32, norm_rows)

    def feed_up(start, size):
        rows = pl.ds(pl.multiple_of(start, size), size)
        value = dot(first_low[...], w_in[rows, :], ((1,), (1,))) + bias_in[:, rows]
        up, lean = gelu_parts(value)
        hidden[:, rows] = up.astype(bf16)
        slope[:, rows] = lean.astype(bf16)

    share = sizes[5]

    def up_shard(shard):
        def run(i, carry):
            feed_up(shard * share + i * tile, tile)
            return carry

        lax.fori_loop(0, share // tile, run, 0)

    def down_shards(shards, opening):
        def body(cols):
            value = rows_in[6:7, cols] if opening else total[:, cols]
            for shard in shards:
                rows = pl.ds(pl.multiple_of(shard * share, share), share)
                value = value + dot(hidden[:, rows], w_down[rows, cols], ((1,), (0,)))
            total[:, cols] = value

        tiles(width, tile, body)

    def up_arrived(which):
        def run(i, carry):
            shard = (me ^ 2) ^ lax.rem(i, 2)
            feed_up(shard * share + lax.div(i, 2) * (share // 2) + which * tile, tile)
            return carry

        lax.fori_loop(0, 4, run, 0)

    up_shard(me)
    step(10)
    turn(9)
    core_copy(5).wait_recv()
    up_shard(me ^ 1)
    step(11)
    turn(10)
    core_copy(6).wait_recv()
    down_shards((me, me ^ 1), True)
    for j in (5, 6):
        arrived(j)
    up_arrived(0)
    step(12)
    turn(11)
    for j in (7, 8):
        arrived(j)
    save(w_in, outs[5], save_sem.at[5])
    up_arrived(1)
    turn(12)
    save(hidden, hidden_out, act_sem.at[6])
    save(slope, slope_out, act_sem.at[7])
    for j in of[6]:
        arrived(j)
    save(w_down, outs[6], save_sem.at[6])
    down_shards((me ^ 2, me ^ 3), False)
    save(total, ffn_out, act_sem.at[8])
    for copy in saves:
        copy.wait()
    for a in range(n):
        core_copy(a).wait_send()
    for j in range(len(chunks)):
        for copy in (crossing, sideways, first_half, second_half):
            copy(j).wait_send()


def gather_and_forward(arrays, tokens, embed, rows_in, bias_in, keep):
    sizes = tuple(a.shape[0] for a in arrays)
    n = len(arrays)
    m = sum(max(1, r // 256) for r in sizes)
    slots, width = tokens.shape
    units = 4 * sizes[5]
    bf16, f32 = jnp.bfloat16, jnp.float32
    dma, vmem = pltpu.SemaphoreType.DMA, pltpu.VMEM
    anywhere, inside = pl.BlockSpec(memory_space=pl.ANY), pl.BlockSpec(memory_space=pltpu.VMEM)
    wide = jax.ShapeDtypeStruct((slots, width), bf16)
    return pl.pallas_call(
        functools.partial(_forward_kernel, sizes),
        out_shape=[jax.ShapeDtypeStruct((4 * a.shape[0], a.shape[1]), a.dtype) for a in arrays]
        + [wide] * 5
        + [jax.ShapeDtypeStruct((slots, width), f32)]
        + [jax.ShapeDtypeStruct((slots, units), bf16)] * 2
        + [jax.ShapeDtypeStruct((slots, width), f32), jax.ShapeDtypeStruct((width // HEAD_DIM, slots), f32)],
        in_specs=[anywhere] * n + [inside] * 5,
        out_specs=[anywhere] * (n + 9) + [inside],
        scratch_shapes=[vmem((4 * a.shape[0], a.shape[1]), a.dtype) for a in arrays]
        + [
            vmem((5, slots, width), bf16),
            vmem((slots, width), f32),
            vmem((slots, width), bf16),
            vmem((slots, units), bf16),
            vmem((slots, units), bf16),
            vmem((slots, width), f32),
        ]
        + [dma((n,)), dma((n,)), dma((9,))]
        + [dma((n,))] * 2
        + [dma((m,))] * 8,
        compiler_params=pltpu.CompilerParams(
            collective_id=0, has_side_effects=True, vmem_limit_bytes=66_000_000
        ),
        name="gather_and_forward",
    )(*arrays, tokens, embed, rows_in, bias_in, keep)


def _row_loop(rows, step, body):
    def run(i, carry):
        body(pl.ds(pl.multiple_of(i * step, step), step))
        return carry

    lax.fori_loop(0, rows // step, run, 0)


def _backward_kernel(dp_n, slab, lag, heights, own_heights, *refs):
    n_terms = len(heights)
    terms = refs[:n_terms]
    (query, key, value, grad_mixed, w_query, w_key, w_value, log_total, keep, resid_t, grad_first, vec, embed) = refs[
        n_terms : n_terms + 13
    ]
    out, vec_out, rec_out, grad_tokens = refs[n_terms + 13 : n_terms + 17]
    (own, core_in, y_in, x_in, z_in, act, grads, weights, time_sum, v_own, v_core, v_y, v_x, v_z, v_sum) = refs[
        n_terms + 17 : n_terms + 32
    ]
    (load_sem, act_sem, w_sem, c_s, c_r, y_s, y_r, x_s, x_r, z_s, z_r, zg_s, zg_r, xg_s, xg_r, out_sem) = refs[
        n_terms + 32 : n_terms + 48
    ]
    vs, vr, ws, wr = refs[n_terms + 48 :]
    f32, bf16 = jnp.float32, jnp.bfloat16
    count = out.shape[0] // slab
    nz = dp_n // 2
    scale = HEAD_DIM**-0.5
    slots, width = query.shape
    pair = 2 * HEAD_DIM
    pairs = width // pair
    dp, me = lax.axis_index("dp"), lax.axis_index("seq")
    x, z, y, c = lax.rem(dp, 2), lax.div(dp, 2), lax.div(me, 2), lax.rem(me, 2)
    core, across, side = (dp, me ^ 1), (dp, me ^ 2), (dp ^ 1, me)
    others = [(lax.rem(z + o, nz) * 2 + x, me) for o in range(1, nz)]

    act_loads = [
        pltpu.make_async_copy(src, act.at[i], act_sem.at[i]) for i, src in enumerate((query, key, value, grad_mixed))
    ]
    w_loads = [pltpu.make_async_copy(src, weights.at[i], w_sem.at[i]) for i, src in enumerate((w_query, w_key, w_value))]
    for load in act_loads:
        load.start()
    barrier = pltpu.get_barrier_semaphore()
    for peer in [core, across, side] + others:
        pl.semaphore_signal(barrier, inc=1, device_id=peer, device_id_type=MESH)
    pl.semaphore_wait(barrier, 3 + len(others))

    def remote(src, dst, send, recv, peer):
        return pltpu.make_async_remote_copy(
            src_ref=src, dst_ref=dst, send_sem=send, recv_sem=recv, device_id=peer, device_id_type=MESH
        )

    hs = slab // 2
    ps = hs // nz
    rs = min(ps, 32)
    given = sum(heights)
    full = given // slab

    row = 0
    ahead = 5
    issues = []
    for term, height in zip(terms, heights):
        step = min(height, slab)
        for off in range(0, height, step):
            issues.append((term, off, (row + off) // slab, (row + off) % slab, step))
        row += height

    def issue(term, off, k, at, step):
        rows, place = pl.ds(off, step), pl.ds(at, step)
        remote(term.at[:, 1 - c, rows, :], core_in.at[k, :, place, :], c_s.at[k], c_r.at[k], core).start()
        sem = load_sem.at[k] if not isinstance(k, int) or k < full else load_sem.at[count]
        pltpu.make_async_copy(term.at[:, c, rows, :], own.at[k, :, place, :], sem).start()

    upfront = slab > own_heights
    for k, entry in enumerate(issues):
        if upfront or k < ahead:
            issue(*entry)

    def issue_later(k):
        start = 0
        for term, height in zip(terms, heights):
            first, last = start // slab, (start + height) // slab

            @pl.when((k >= first) & (k < last))
            def _():
                off = pl.multiple_of((k - first) * slab, slab)
                issue(term, off, k, 0, slab)

            start += height

    for load in w_loads:
        load.start()

    def core_copy(k):
        return remote(core_in.at[k], core_in.at[k], c_s.at[k], c_r.at[k], core)

    def y_copy(k):
        return remote(own.at[k, 1 - y], y_in.at[k], y_s.at[k], y_r.at[k], across)

    def x_copy(k):
        give = pl.ds(pl.multiple_of((1 - x) * hs, 16), hs)
        return remote(own.at[k, y, give], x_in.at[k], x_s.at[k], x_r.at[k], side)

    def z_copy(k, o):
        piece = pl.ds(pl.multiple_of(x * hs + lax.rem(z + o, nz) * ps, 16), ps)
        return remote(own.at[k, y, piece], z_in.at[k, o], z_s.at[k, o], z_r.at[k, o], others[o - 1])

    def zg_copy(k, o):
        mine = own.at[k, 1 - y, pl.ds(pl.multiple_of(x * hs + z * ps, 16), ps)]
        return remote(mine, mine, zg_s.at[k, o], zg_r.at[k, o], others[o - 1])

    def xg_copy(k):
        mine = own.at[k, 1 - y, pl.ds(pl.multiple_of(x * hs, 16), hs)]
        return remote(mine, mine, xg_s.at[k], xg_r.at[k], side)

    def out_copy(k):
        rows = pl.ds(pl.multiple_of(k * slab, slab), slab)
        return pltpu.make_async_copy(own.at[k, 1 - y], out.at[rows, :], out_sem.at[k])

    def stage_core(k):
        @pl.when(k < full)
        def _():
            pltpu.make_async_copy(own.at[k], own.at[k], load_sem.at[k]).wait()

        core_copy(k).wait_recv()

        def add(r):
            for p in range(2):
                own[k, p, r] = (own[k, p, r].astype(f32) + core_in[k, p, r].astype(f32)).astype(bf16)

        _row_loop(slab, 16, add)
        y_copy(k).start()

    def stage_y(k):
        y_copy(k).wait()

        def add(r):
            own[k, y, r] = (own[k, y, r].astype(f32) + y_in[k, r].astype(f32)).astype(bf16)

        _row_loop(slab, 32, add)
        x_copy(k).start()

    def stage_x(k):
        x_copy(k).wait_recv()

        def add(r):
            at = pl.ds(pl.multiple_of(x * hs + r.start, 16), r.size)
            own[k, y, at] = (own[k, y, at].astype(f32) + x_in[k, r].astype(f32)).astype(bf16)

        _row_loop(hs, rs, add)
        for o in range(1, nz):
            z_copy(k, o).start()

    def stage_z(k):
        for o in range(1, nz):
            z_copy(k, o).wait_recv()

        def add(r):
            at = pl.ds(pl.multiple_of(x * hs + z * ps + r.start, 16), r.size)
            total = own[k, y, at].astype(f32)
            for o in range(1, nz):
                total += z_in[k, o, r].astype(f32)
            own[k, 1 - y, at] = total.astype(bf16)

        _row_loop(ps, rs, add)
        for o in range(1, nz):
            zg_copy(k, o).start()

    def stage_zg(k):
        for o in range(1, nz):
            zg_copy(k, o).wait_recv()
        xg_copy(k).start()

    def stage_xg(k):
        xg_copy(k).wait_recv()
        out_copy(k).start()

    def dot(a, b, dims):
        return lax.dot_general(a, b, (dims, ((), ())), preferred_element_type=f32)

    def head_pair(p):
        cols = pl.ds(pl.multiple_of(p * pair, pair), pair)
        q2, k2, v2, g2 = (act[i, :, cols] for i in range(4))
        first = lax.broadcasted_iota(jnp.int32, (1, pair), 1) < HEAD_DIM
        kept = keep[...] > 0
        found = []
        for h in range(2):
            mask = jnp.where(first == (h == 0), 1.0, 0.0)
            q_h = q2 * (mask * scale).astype(bf16)
            g_h = g2 * mask.astype(bf16)
            scores = dot(k2, q_h, ((1,), (1,)))
            soft = jnp.where(kept, jnp.exp(scores - log_total[pl.ds(2 * p + h, 1), :]), 0.0)
            grad_soft = dot(v2, g_h, ((1,), (1,)))
            inner = jnp.sum(soft * grad_soft, axis=0, keepdims=True)
            grad_scores = (soft * (grad_soft - inner)).astype(bf16)
            found.append(
                (
                    dot(k2, grad_scores, ((0,), (0,))),
                    dot(grad_scores, q2, ((1,), (0,))),
                    dot(soft.astype(bf16), g2, ((1,), (0,))),
                )
            )
        q_t = jnp.concatenate([found[0][0][:HEAD_DIM], found[1][0][HEAD_DIM:]], axis=0)
        grad_q = (q_t.T * scale).astype(bf16)
        grad_k = (jnp.where(first, found[0][1], found[1][1]) * scale).astype(bf16)
        grad_v = jnp.where(first, found[0][2], found[1][2]).astype(bf16)
        grads[0, :, cols] = grad_q
        grads[1, :, cols] = grad_k
        grads[2, :, cols] = grad_v
        v_own[0:1, cols] = jnp.sum(grad_q.astype(f32), axis=0, keepdims=True)
        v_own[1:2, cols] = jnp.sum(grad_v.astype(f32), axis=0, keepdims=True)

    def term(m):
        step = min(own_heights, slab)
        for cc, mine in ((1 - c, False), (c, True)):
            for p in range(2):
                left = resid_t[pl.ds(pl.multiple_of((p * 2 + cc) * own_heights, own_heights), own_heights), :]
                tile = dot(left, grads[m], ((1,), (0,))).astype(bf16)
                if not mine:
                    act[m, p * own_heights : (p + 1) * own_heights] = tile
                for off in range(0, own_heights, step):
                    start = given + m * own_heights + off
                    k, at = lax.div(start, slab), pl.multiple_of(lax.rem(start, slab), step)
                    if mine:
                        own[k, p, pl.ds(at, step)] = tile[off : off + step]
                    else:
                        src = act.at[m, pl.ds(p * own_heights + off, step), :]
                        dst = core_in.at[k, p, pl.ds(at, step), :]
                        remote(src, dst, c_s.at[k], c_r.at[k], core).start()

    blocks = 4
    block = slots // blocks

    def resid_rows(r):
        rows = pl.ds(pl.multiple_of(r * block, block), block)
        total = grad_first[rows, :]
        for m in range(3):
            total += dot(grads[m, rows, :], weights[m], ((1,), (1,)))
        grad_tokens[rows, :] = total.astype(bf16)
        time_sum[...] += jnp.sum(total, axis=0, keepdims=True)

    v_half = v_core.shape[0]
    v_mine = pl.ds(pl.multiple_of(c * v_half, v_half), v_half)
    v_given = pl.ds(pl.multiple_of((1 - c) * v_half, v_half), v_half)

    def v_copy(i):
        peers = [core, across, side] + others + [core]
        if i == 0:
            src, dst = v_own.at[v_given], v_core
        elif i == 2 + nz:
            src = dst = vec_out.at[v_mine]
        else:
            src, dst = v_sum.at[min(i, 3) - 1], v_z.at[i - 2] if i > 2 else (v_y, v_x)[i - 1]
        return remote(src, dst, vs.at[i], vr.at[i], peers[i])

    def v_stage(i):
        if i == 0:
            v_copy(0).start()
        elif i <= 3:
            v_copy(i - 1).wait_recv()
            before = v_own[v_mine] if i == 1 else v_sum[i - 2]
            v_sum[i - 1] = before + (v_core, v_y, v_x)[i - 1][...]
            for j in range(i, i + 1 if i < 3 else 2 + nz):
                v_copy(j).start()
        elif i == 4:
            total = v_sum[2]
            for o in range(1, nz):
                v_copy(2 + o).wait_recv()
                total = total + v_z[o]
            vec_out[v_mine] = total
            v_copy(2 + nz).start()
        else:
            v_copy(2 + nz).wait_recv()

    def w_copy(q, i):
        peers = [across, side] + others + [core]
        if i == 0:
            part = rec_out.at[q, dp, y, c]
        elif i == 1:
            part = rec_out.at[q, dp, :, c]
        elif i < 1 + nz:
            part = rec_out.at[q, pl.ds(z * 2, 2), :, c]
        else:
            part = rec_out.at[q, :, :, c]
        return remote(part, part, ws.at[q, i], wr.at[q, i], peers[i])

    def w_stage(q, i):
        if i == 0:
            if q == 0:
                rec_out[0, dp, y, c] = embed[...]
            else:
                rounded = time_sum[...].astype(bf16).astype(f32)
                lanes = embed.shape[-1]
                for j in range(width // lanes):
                    rec_out[1, dp, y, c, j : j + 1, :] = rounded[:, j * lanes : (j + 1) * lanes]
            w_copy(q, 0).start()
        elif i < 3:
            w_copy(q, i - 1).wait_recv()
            for j in range(i, i + 1 if i == 1 else 1 + nz):
                w_copy(q, j).start()
        elif i == 3:
            for o in range(1, nz):
                w_copy(q, 1 + o).wait_recv()
            w_copy(q, 1 + nz).start()
        else:
            w_copy(q, 1 + nz).wait_recv()

    stages = [stage_y, stage_x, stage_z, stage_zg, stage_xg]
    n_units = pairs + 3 + blocks
    base = 0 if slab <= own_heights else pairs + 4
    small = [(pairs + at, functools.partial(v_stage, i)) for i, at in enumerate((0, 2, 5, 7, 9, 10))]
    for q, first in ((0, 0), (1, n_units)):
        small += [(first + at, functools.partial(w_stage, q, i)) for i, at in enumerate((0, 3, 5, 7, 8))]
    ticks = max([base + count + lag * (len(stages) - 1)] + [at + 1 for at, _ in small])
    v_own[...] = vec[...]
    time_sum[...] = jnp.zeros_like(time_sum)
    for load in act_loads:
        load.wait()

    def tick(t, carry):
        @pl.when(t < pairs)
        def _():
            head_pair(t)

        @pl.when((t >= pairs) & (t < pairs + 3))
        def _():
            term(t - pairs)

        @pl.when(t == pairs + 3)
        def _():
            for load in w_loads:
                load.wait()

        @pl.when((t >= pairs + 3) & (t < n_units))
        def _():
            resid_rows(t - pairs - 3)

        if row > full * slab:

            @pl.when(t == base)
            def _():
                part = own.at[full, :, pl.ds(0, row - full * slab), :]
                pltpu.make_async_copy(part, part, load_sem.at[count]).wait()

        if not upfront:
            issue_later(t - base + ahead)

        for i in range(3):
            k = t - base + i

            @pl.when((k < count) & ((t == base) | ((t > base) & (i == 2))))
            def _():
                stage_core(k)

        for d, stage in enumerate(stages):
            k = t - base - d * lag

            @pl.when((k >= 0) & (k < count))
            def _():
                stage(k)

        for at, run in small:
            pl.when(t == at)(run)

        return carry

    lax.fori_loop(0, ticks, tick, 0)

    def finish(k, carry):
        core_copy(k).wait_send()
        x_copy(k).wait_send()
        for o in range(1, nz):
            z_copy(k, o).wait_send()
            zg_copy(k, o).wait_send()
        xg_copy(k).wait_send()
        out_copy(k).wait()
        return carry

    lax.fori_loop(0, count, finish, 0)
    for i in range(3 + nz):
        v_copy(i).wait_send()
    for i in range(2 + nz):
        for q in range(2):
            w_copy(q, i).wait_send()


def attend_and_reduce(dp_n, terms, acts, weights, log_total, keep, resid_t, grad_first, vec, embed):
    slots, width = acts[0].shape
    heights = tuple(t.shape[2] for t in terms)
    own_heights = width // 4
    rows = sum(heights) + 3 * own_heights
    slab = max(128, 16 * dp_n)
    count, nz = rows // slab, dp_n // 2
    bf16, f32 = jnp.bfloat16, jnp.float32
    dma, vmem = pltpu.SemaphoreType.DMA, pltpu.VMEM
    v_shape = vec.shape
    anywhere, inside = pl.BlockSpec(memory_space=pl.ANY), pl.BlockSpec(memory_space=pltpu.VMEM)
    half_shape = (v_shape[0] // 2, width)
    return pl.pallas_call(
        functools.partial(_backward_kernel, dp_n, slab, 1, heights, own_heights),
        out_shape=[
            jax.ShapeDtypeStruct((rows, width), bf16),
            jax.ShapeDtypeStruct(v_shape, f32),
            jax.ShapeDtypeStruct((2, dp_n, 2, 2) + embed.shape, f32),
            jax.ShapeDtypeStruct((slots, width), bf16),
        ],
        in_specs=[anywhere] * (len(terms) + 7) + [inside] * 6,
        out_specs=[anywhere, inside, inside, inside],
        scratch_shapes=[
            vmem((count, 2, slab, width), bf16),
            vmem((count, 2, slab, width), bf16),
            vmem((count, slab, width), bf16),
            vmem((count, slab // 2, width), bf16),
            vmem((count, nz, slab // 2 // nz, width), bf16),
            vmem((4, slots, width), bf16),
            vmem((3, slots, width), bf16),
            vmem((3, width, width), bf16),
            vmem((1, width), f32),
            vmem(v_shape, f32),
            vmem(half_shape, f32),
            vmem(half_shape, f32),
            vmem(half_shape, f32),
            vmem((nz,) + half_shape, f32),
            vmem((3,) + half_shape, f32),
        ]
        + [dma((count + 1,)), dma((4,)), dma((3,))]
        + [dma((count,))] * 6
        + [dma((count, nz))] * 4
        + [dma((count,))] * 3
        + [dma((3 + nz,))] * 2
        + [dma((2, 2 + nz))] * 2,
        compiler_params=pltpu.CompilerParams(collective_id=1, has_side_effects=True, vmem_limit_bytes=66_000_000),
        name="attend_and_reduce",
    )(*terms, *acts, *weights, log_total, keep, resid_t, grad_first, vec, embed)


def local(
    dp_n,
    tokens,
    time_embed,
    lengths,
    cotangent,
    w_query,
    w_key,
    w_value,
    w_out,
    w_time,
    w_in,
    w_down,
    b_query,
    b_value,
    b_out,
    b_time,
    b_in,
    b_down,
    gain_one,
    shift_one,
    gain_two,
    shift_two,
):
    f32, bf16 = jnp.float32, jnp.bfloat16
    seq_rank = lax.axis_index("seq")
    item_count = time_embed.shape[0]
    token_count = tokens.shape[0]
    slot_count = token_count // item_count
    width = tokens.shape[1]
    rows = w_time.shape[0]

    def mm(a, b, dims):
        return lax.dot_general(a, b, (dims, ((), ())), preferred_element_type=f32)

    own_lengths = lax.dynamic_slice_in_dim(lengths, seq_rank * item_count, item_count, 0)
    slot_index = lax.broadcasted_iota(jnp.int32, (item_count, slot_count), 1)
    own_valid = slot_index < own_lengths[:, None] + BLOCK
    row_keep = own_valid.reshape(token_count, 1).astype(f32)
    rows_in = jnp.stack([b_time, b_query, b_value, b_out, gain_one, shift_one, b_down, b_down]).astype(f32)
    (
        _,
        full_query,
        full_key,
        full_value,
        full_out,
        full_in,
        full_down,
        resid_low,
        query_rows,
        key_rows,
        value_rows,
        mixed_rows,
        first_in,
        hidden_low,
        gelu_slope,
        ffn_out,
        log_total,
    ) = gather_and_forward(
        [w_time, w_query, w_key, w_value, w_out, w_in, w_down],
        tokens,
        jnp.broadcast_to(time_embed, (16, width)),
        rows_in,
        b_in.astype(f32).reshape(1, -1),
        row_keep,
    )
    first_norm, first_pull = jax.vjp(
        layer_norm, first_in, gain_one.astype(f32), shift_one.astype(f32)
    )
    first_low = first_norm.astype(bf16)
    second_norm, second_pull = jax.vjp(
        layer_norm, first_norm + ffn_out, gain_two.astype(f32), shift_two.astype(f32)
    )
    layer_out = (second_norm * row_keep).astype(bf16)
    grad_second_in, grad_gain_two, grad_shift_two = second_pull(cotangent.astype(f32) * row_keep)
    grad_ffn = grad_second_in.astype(bf16)
    grad_hidden = mm(grad_ffn, full_down, ((1,), (1,)))
    grad_pre = (grad_hidden * gelu_slope).astype(bf16)
    grad_first = grad_second_in + mm(grad_pre, full_in, ((1,), (0,)))
    term_in = mm(grad_pre, first_low, ((0,), (0,))).astype(bf16)
    term_down = mm(hidden_low, grad_ffn, ((0,), (0,))).astype(bf16)
    grad_first_in, grad_gain_one, grad_shift_one = first_pull(grad_first)
    grad_attn = grad_first_in.astype(bf16)
    grad_mixed = mm(grad_attn, full_out, ((1,), (1,))).astype(bf16)
    terms = [
        term_down,
        term_in,
        mm(mixed_rows, grad_attn, ((0,), (0,))).astype(bf16),
    ]
    zero = jnp.zeros((width,), f32)
    vec = jnp.stack(
        [
            zero,
            zero,
            jnp.sum(grad_attn, axis=0, dtype=f32),
            jnp.sum(grad_ffn, axis=0, dtype=f32),
            grad_gain_one,
            grad_shift_one,
            grad_gain_two,
            grad_shift_two,
        ]
    )
    vec = jnp.concatenate([vec, jnp.sum(grad_pre, axis=0, dtype=f32).reshape(-1, width)], axis=0)
    vec = jnp.pad(vec, ((0, -vec.shape[0] % 8), (0, 0)))
    sums, vectors, every, grad_tokens = attend_and_reduce(
        dp_n,
        [t.reshape(2, 2, -1, width) for t in terms],
        [query_rows, key_rows, value_rows, grad_mixed],
        [full_query, full_key, full_value],
        log_total,
        row_keep,
        resid_low.T,
        grad_first_in,
        vec,
        time_embed.astype(f32).reshape(-1, 128),
    )
    time_rows, time_grads = every.reshape(2, -1, width).astype(bf16)
    own_columns = lax.dynamic_slice_in_dim(time_rows, seq_rank * rows, rows, 1)
    grad_w_time = mm(own_columns, time_grads, ((0,), (0,)))
    grad_b_time = jnp.sum(time_grads, axis=0, dtype=f32)
    grad_b_in = vectors[8 : 8 + b_in.shape[0] // width].reshape(-1)
    sums = sums.astype(f32)
    down_rows, in_rows = (t.shape[0] // 4 for t in terms[:2])
    ends = [0, down_rows, down_rows + in_rows]
    ends += [ends[-1] + rows * i for i in range(1, 5)]
    share_down, share_in, share_out, share_q, share_k, share_v = (
        sums[lo:hi] for lo, hi in zip(ends[:-1], ends[1:])
    )
    return (
        layer_out,
        grad_tokens,
        share_q,
        share_k,
        share_v,
        share_out,
        grad_w_time,
        share_in,
        share_down,
        vectors[0],
        vectors[1],
        vectors[2],
        grad_b_time,
        grad_b_in,
        vectors[3],
        vectors[4],
        vectors[5],
        vectors[6],
        vectors[7],
    )


def solution(mesh):
    in_specs = (
        P(("dp", "seq"), None),
        P(("dp", "seq"), None),
        P("dp"),
        P(("dp", "seq"), None),
        P("seq", None),
        P("seq", None),
        P("seq", None),
        P("seq", None),
        P("seq", None),
        P("seq", None),
        P("seq", None),
        P(),
        P(),
        P(),
        P(),
        P(),
        P(),
        P(),
        P(),
        P(),
        P(),
    )
    out_specs = (
        P(("dp", "seq"), None),
        P(("dp", "seq"), None),
        P("seq", None),
        P("seq", None),
        P("seq", None),
        P("seq", None),
        P("seq", None),
        P("seq", None),
        P("seq", None),
        P(),
        P(),
        P(),
        P(),
        P(),
        P(),
        P(),
        P(),
        P(),
        P(),
    )
    return jax.shard_map(functools.partial(local, mesh.shape["dp"]), mesh=mesh, in_specs=in_specs, out_specs=out_specs, check_vma=False)
```

```python
import functools

import jax
import jax.numpy as jnp
from jax import lax
from jax.experimental import pallas as pl
from jax.experimental.pallas import tpu as pltpu
from jax.sharding import PartitionSpec as P

HEAD_DIM = 64
BLOCK = 25
MESH = pl.DeviceIdType.MESH


norm_eps = 1e-05
neg_large = -1e30


def layer_norm(values, gain, shift):
    center = values - jnp.mean(values, axis=-1, keepdims=True)
    spread = lax.rsqrt(jnp.mean(center * center, axis=-1, keepdims=True) + norm_eps)
    return center * spread * gain + shift


def gelu_parts(values):
    half = 0.5 + 0.5 * lax.erf(values * 0.5**0.5)
    density = jnp.exp(-0.5 * values * values) * (0.5 / jnp.pi) ** 0.5
    return values * half, half + values * density


def _forward_kernel(sizes, *refs):
    n = len(sizes)
    given, (tokens, embed, rows_in, bias_in, keep) = refs[:n], refs[n : n + 5]
    outs = refs[n + 5 : 2 * n + 5]
    (resid_out, query_out, key_out, value_out, mixed_out, pre_out, hidden_out, slope_out, ffn_out, log_total) = refs[
        2 * n + 5 : 2 * n + 15
    ]
    full = refs[2 * n + 15 : 3 * n + 15]
    act, pre, first_low, hidden, slope, total = refs[3 * n + 15 : 3 * n + 21]
    load_sem, save_sem, act_sem, c_send, c_recv, y_send, y_recv, x_send, x_recv, f_send, f_recv, g_send, g_recv = refs[
        3 * n + 21 :
    ]
    f32, bf16 = jnp.float32, jnp.bfloat16
    w_time, w_query, w_key, w_value, w_out, w_in, w_down = full
    slots, width = tokens.shape
    pair = 2 * HEAD_DIM
    scale = HEAD_DIM**-0.5
    dp, me = lax.axis_index("dp"), lax.axis_index("seq")
    half = lax.rem(dp, 2)

    def home(a, shard):
        return full[a].at[pl.ds(pl.multiple_of(shard * sizes[a], sizes[a]), sizes[a]), :]

    loads = [pltpu.make_async_copy(given[a], home(a, me), load_sem.at[a]) for a in range(n)]
    for load in loads:
        load.start()
    core, across, side = (dp, me ^ 1), (dp, me ^ 2), (dp ^ 1, me)
    barrier = pltpu.get_barrier_semaphore()
    for peer in (core, across, side):
        pl.semaphore_signal(barrier, inc=1, device_id=peer, device_id_type=MESH)
    pl.semaphore_wait(barrier, 3)

    def remote(src, send, recv, peer):
        return pltpu.make_async_remote_copy(
            src_ref=src, dst_ref=src, send_sem=send, recv_sem=recv, device_id=peer, device_id_type=MESH
        )

    chunks, of = [], [[] for _ in sizes]
    for a, rows in enumerate(sizes):
        step = min(rows // 2, 128)
        for off in range(0, rows // 2, step):
            of[a].append(len(chunks))
            chunks.append((a, rows, off, step))

    def region(j, shard, part):
        a, rows, off, step = chunks[j]
        start = pl.multiple_of(shard * rows + part * (rows // 2) + off, 16)
        return full[a].at[pl.ds(start, step), :]

    saves = []

    def crossing(j):
        return remote(region(j, me, half), y_send.at[j], y_recv.at[j], across)

    def core_copy(a):
        return remote(home(a, me), c_send.at[a], c_recv.at[a], core)

    def sideways(j):
        return remote(region(j, me ^ 2, half), x_send.at[j], x_recv.at[j], side)

    def first_half(j):
        return remote(region(j, me ^ 2, half), f_send.at[j], f_recv.at[j], core)

    def second_half(j):
        return remote(region(j, me ^ 2, 1 - half), g_send.at[j], g_recv.at[j], core)

    for j, (a, rows, off, _) in enumerate(chunks):
        if off == 0:
            loads[a].wait()
            core_copy(a).start()
        crossing(j).start()

    def step(j):
        crossing(j).wait_recv()
        sideways(j).start()
        first_half(j).start()

    def turn(j):
        sideways(j).wait_recv()
        second_half(j).start()

    def arrived(j):
        first_half(j).wait_recv()
        second_half(j).wait_recv()

    def save(src, dst, sem):
        copy = pltpu.make_async_copy(src, dst, sem)
        copy.start()
        saves.append(copy)

    def complete(a):
        for j in of[a]:
            arrived(j)
        core_copy(a).wait_recv()
        save(full[a], outs[a], save_sem.at[a])

    def dot(a, b, dims):
        return lax.dot_general(a, b, (dims, ((), ())), preferred_element_type=f32)

    def bias(i):
        return rows_in[i : i + 1, :]

    tile = 256

    def tiles(extent, size, body):
        def run(i, carry):
            body(pl.ds(pl.multiple_of(i * size, size), size))
            return carry

        lax.fori_loop(0, extent // size, run, 0)

    def project(weight, i, row):
        def body(cols):
            value = dot(act[0], weight[:, cols], ((1,), (0,)))
            if row is not None:
                value += rows_in[row : row + 1, cols]
            act[i, :, cols] = value.astype(bf16)

        tiles(width, tile, body)
        save(act.at[i], (resid_out, query_out, key_out, value_out)[i], act_sem.at[i])

    step(0)
    step(1)
    turn(0)
    complete(0)
    time_proj = dot(embed[...], w_time[...], ((1,), (0,)))[0:1] + bias(0)

    def enter(r):
        value = tokens[r, :].astype(f32) + time_proj
        pre[r, :] = value
        act[0, r, :] = value.astype(bf16)

    tiles(slots, 64, enter)
    save(act.at[0], resid_out, act_sem.at[0])
    for j, (weight, row) in enumerate(((w_query, 1), (w_key, None), (w_value, 2))):
        step(j + 2)
        turn(j + 1)
        complete(j + 1)
        project(weight, j + 1, row)

    first = lax.broadcasted_iota(jnp.int32, (1, pair), 1) < HEAD_DIM

    def head_pair(p):
        cols = pl.ds(pl.multiple_of(p * pair, pair), pair)
        q2, k2, v2 = (act[i, :, cols] for i in (1, 2, 3))
        kept = keep[...] > 0
        found = []
        for h in range(2):
            mask = jnp.where(first == (h == 0), scale, 0.0)
            scores = jnp.where(kept, dot(k2, q2 * mask.astype(bf16), ((1,), (1,))), neg_large)
            top = jnp.max(scores, axis=0, keepdims=True)
            weights = jnp.exp(scores - top)
            norm = jnp.sum(weights, axis=0, keepdims=True)
            soft = (weights * (1.0 / norm)).astype(bf16)
            log_total[pl.ds(2 * p + h, 1), :] = top + jnp.log(norm)
            found.append(dot(v2, soft, ((0,), (0,))))
        mixed = jnp.concatenate([found[0][:HEAD_DIM], found[1][HEAD_DIM:]], axis=0)
        act[4, :, cols] = mixed.T.astype(bf16)

    beside = {0: (None, 4), 1: (5, None), 3: (6, 5), 5: (7, 6), 7: (8, 7)}

    def attend(p, carry):
        for at, (enters, turns) in beside.items():

            @pl.when(p == at)
            def _():
                if enters is not None:
                    step(enters)
                if turns is not None:
                    turn(turns)

        head_pair(p)
        return carry

    lax.fori_loop(0, width // pair, attend, 0)
    save(act.at[4], mixed_out, act_sem.at[4])
    complete(4)

    def attn_out(cols):
        pre[:, cols] += dot(act[4], w_out[:, cols], ((1,), (0,))) + rows_in[3:4, cols]

    tiles(width, tile, attn_out)
    step(9)
    turn(8)
    save(pre, pre_out, act_sem.at[5])

    def norm_rows(r):
        first_low[r, :] = layer_norm(pre[r, :], bias(4), bias(5)).astype(bf16)

    tiles(slots, 32, norm_rows)

    def feed_up(start, size):
        rows = pl.ds(pl.multiple_of(start, size), size)
        value = dot(first_low[...], w_in[rows, :], ((1,), (1,))) + bias_in[:, rows]
        up, lean = gelu_parts(value)
        hidden[:, rows] = up.astype(bf16)
        slope[:, rows] = lean.astype(bf16)

    share = sizes[5]

    def up_shard(shard):
        def run(i, carry):
            feed_up(shard * share + i * tile, tile)
            return carry

        lax.fori_loop(0, share // tile, run, 0)

    def down_shards(shards, opening):
        def body(cols):
            value = rows_in[6:7, cols] if opening else total[:, cols]
            for shard in shards:
                rows = pl.ds(pl.multiple_of(shard * share, share), share)
                value = value + dot(hidden[:, rows], w_down[rows, cols], ((1,), (0,)))
            total[:, cols] = value

        tiles(width, tile, body)

    def up_arrived(which):
        def run(i, carry):
            shard = (me ^ 2) ^ lax.rem(i, 2)
            feed_up(shard * share + lax.div(i, 2) * (share // 2) + which * tile, tile)
            return carry

        lax.fori_loop(0, 4, run, 0)

    up_shard(me)
    step(10)
    turn(9)
    core_copy(5).wait_recv()
    up_shard(me ^ 1)
    step(11)
    turn(10)
    core_copy(6).wait_recv()
    down_shards((me, me ^ 1), True)
    for j in (5, 6):
        arrived(j)
    up_arrived(0)
    step(12)
    turn(11)
    for j in (7, 8):
        arrived(j)
    save(w_in, outs[5], save_sem.at[5])
    up_arrived(1)
    turn(12)
    save(hidden, hidden_out, act_sem.at[6])
    save(slope, slope_out, act_sem.at[7])
    for j in of[6]:
        arrived(j)
    save(w_down, outs[6], save_sem.at[6])
    down_shards((me ^ 2, me ^ 3), False)
    save(total, ffn_out, act_sem.at[8])
    for copy in saves:
        copy.wait()
    for a in range(n):
        core_copy(a).wait_send()
    for j in range(len(chunks)):
        for copy in (crossing, sideways, first_half, second_half):
            copy(j).wait_send()


def gather_and_forward(arrays, tokens, embed, rows_in, bias_in, keep):
    sizes = tuple(a.shape[0] for a in arrays)
    n = len(arrays)
    m = sum(max(1, r // 256) for r in sizes)
    slots, width = tokens.shape
    units = 4 * sizes[5]
    bf16, f32 = jnp.bfloat16, jnp.float32
    dma, vmem = pltpu.SemaphoreType.DMA, pltpu.VMEM
    anywhere, inside = pl.BlockSpec(memory_space=pl.ANY), pl.BlockSpec(memory_space=pltpu.VMEM)
    wide = jax.ShapeDtypeStruct((slots, width), bf16)
    return pl.pallas_call(
        functools.partial(_forward_kernel, sizes),
        out_shape=[jax.ShapeDtypeStruct((4 * a.shape[0], a.shape[1]), a.dtype) for a in arrays]
        + [wide] * 5
        + [jax.ShapeDtypeStruct((slots, width), f32)]
        + [jax.ShapeDtypeStruct((slots, units), bf16)] * 2
        + [jax.ShapeDtypeStruct((slots, width), f32), jax.ShapeDtypeStruct((width // HEAD_DIM, slots), f32)],
        in_specs=[anywhere] * n + [inside] * 5,
        out_specs=[anywhere] * (n + 9) + [inside],
        scratch_shapes=[vmem((4 * a.shape[0], a.shape[1]), a.dtype) for a in arrays]
        + [
            vmem((5, slots, width), bf16),
            vmem((slots, width), f32),
            vmem((slots, width), bf16),
            vmem((slots, units), bf16),
            vmem((slots, units), bf16),
            vmem((slots, width), f32),
        ]
        + [dma((n,)), dma((n,)), dma((9,))]
        + [dma((n,))] * 2
        + [dma((m,))] * 8,
        compiler_params=pltpu.CompilerParams(
            collective_id=0, has_side_effects=True, vmem_limit_bytes=66_000_000
        ),
        name="gather_and_forward",
    )(*arrays, tokens, embed, rows_in, bias_in, keep)


def _row_loop(rows, step, body):
    def run(i, carry):
        body(pl.ds(pl.multiple_of(i * step, step), step))
        return carry

    lax.fori_loop(0, rows // step, run, 0)


def _backward_kernel(dp_n, slab, lag, *refs):
    (hidden, slope, w_down, w_in, second, first_in, query, key, value, mixed, w_out, w_query, w_key, w_value) = refs[:14]
    (grad_ffn_in, first_low_in, resid_in, log_total, keep, gain, vec, embed) = refs[14:22]
    out, vec_out, rec_out, grad_tokens = refs[22:26]
    (own, core_in, y_in, x_in, z_in, act, grads, weights, pieces, chunk_w, acc, before) = refs[26:38]
    (time_sum, v_own, v_core, v_y, v_x, v_z, v_sum) = refs[38:45]
    (piece_sem, act_sem, w_sem, f_sem, c_s, c_r, y_s, y_r, x_s, x_r, z_s, z_r, zg_s, zg_r, xg_s, xg_r, out_sem) = refs[45:62]
    vs, vr, ws, wr = refs[62:]
    f32, bf16 = jnp.float32, jnp.bfloat16
    count = out.shape[0] // slab
    nz = dp_n // 2
    scale = HEAD_DIM**-0.5
    slots, width = query.shape
    pair = 2 * HEAD_DIM
    pairs = width // pair
    share = w_in.shape[0] // 4
    tile = width // 4
    groups = share // tile
    fine = slab <= tile
    subs = tile // slab if fine else 1
    part = min(slab, tile)
    dp, me = lax.axis_index("dp"), lax.axis_index("seq")
    x, z, y, c = lax.rem(dp, 2), lax.div(dp, 2), lax.div(me, 2), lax.rem(me, 2)
    core, across, side = (dp, me ^ 1), (dp, me ^ 2), (dp ^ 1, me)
    others = [(lax.rem(z + o, nz) * 2 + x, me) for o in range(1, nz)]

    def shard_of(i):
        return lax.rem(i, 2) * 2 + lax.rem(1 - c + lax.div(i, 2), 2)

    def chunk_loads(u):
        start = pl.multiple_of(shard_of(lax.rem(u, 4)) * share + lax.div(u, 4) * tile, tile)
        rows, slot = pl.ds(start, tile), lax.rem(u, 2)
        return [
            pltpu.make_async_copy(hidden.at[:, rows], pieces.at[slot, 0], piece_sem.at[slot, 0]),
            pltpu.make_async_copy(slope.at[:, rows], pieces.at[slot, 1], piece_sem.at[slot, 1]),
            pltpu.make_async_copy(w_down.at[rows, :], chunk_w.at[slot, 0], piece_sem.at[slot, 2]),
            pltpu.make_async_copy(w_in.at[rows, :], chunk_w.at[slot, 1], piece_sem.at[slot, 3]),
        ]

    act_loads = [
        pltpu.make_async_copy(src, act.at[i], act_sem.at[i]) for i, src in enumerate((query, key, value, mixed))
    ]
    w_loads = [
        pltpu.make_async_copy(src, weights.at[i % 2], w_sem.at[i])
        for i, src in enumerate((w_out, w_query, w_key, w_value))
    ]
    grad_ffn, first_low, resid_low = act.at[2], grads.at[1], act.at[3]
    f_loads = [
        pltpu.make_async_copy(src, dst, f_sem.at[i])
        for i, (src, dst) in enumerate(
            ((grad_ffn_in, grad_ffn), (first_low_in, first_low), (second, acc), (first_in, before), (resid_in, resid_low))
        )
    ]
    for load in f_loads[:1] + chunk_loads(0) + f_loads[1:4] + [act_loads[3], w_loads[0], w_loads[1]]:
        load.start()
    barrier = pltpu.get_barrier_semaphore()
    for peer in [core, across, side] + others:
        pl.semaphore_signal(barrier, inc=1, device_id=peer, device_id_type=MESH)
    pl.semaphore_wait(barrier, 3 + len(others))

    def remote(src, dst, send, recv, peer):
        return pltpu.make_async_remote_copy(
            src_ref=src, dst_ref=dst, send_sem=send, recv_sem=recv, device_id=peer, device_id_type=MESH
        )

    hs = slab // 2
    ps = hs // nz
    rs = min(ps, 32)
    given = 2 * share

    def slab_of(mat, group, sub):
        if fine:
            return (group * 2 * subs + mat * subs if mat is not None else group * subs + given // slab) + sub, 0
        if mat is not None:
            return mat, pl.multiple_of(group * tile, tile)
        return given // slab, pl.multiple_of(group * tile, tile)

    def deliver(mat, group, lane, p, mine, value):
        @pl.when(jnp.logical_not(mine))
        def _():
            act[lane, pl.ds(pl.multiple_of(p * tile, tile), tile), :] = value
            for sub in range(subs):
                k, at = slab_of(mat, group, sub)
                src = act.at[lane, pl.ds(pl.multiple_of(p * tile + sub * part, part), part), :]
                remote(src, core_in.at[k, p, pl.ds(at, part), :], c_s.at[k], c_r.at[k], core).start()

        @pl.when(mine)
        def _():
            for sub in range(subs):
                k, at = slab_of(mat, group, sub)
                own[k, p, pl.ds(at, part)] = value[sub * part : (sub + 1) * part]

    def sent(mat, group):
        for sub in range(subs):
            k, at = slab_of(mat, group, sub)
            rows = core_in.at[k, :, pl.ds(at, part), :]
            remote(rows, rows, c_s.at[k], c_r.at[k], core).wait_send()

    def core_copy(k):
        return remote(core_in.at[k], core_in.at[k], c_s.at[k], c_r.at[k], core)

    def y_copy(k):
        return remote(own.at[k, 1 - y], y_in.at[k], y_s.at[k], y_r.at[k], across)

    def x_copy(k):
        give = pl.ds(pl.multiple_of((1 - x) * hs, 16), hs)
        return remote(own.at[k, y, give], x_in.at[k], x_s.at[k], x_r.at[k], side)

    def z_copy(k, o):
        piece = pl.ds(pl.multiple_of(x * hs + lax.rem(z + o, nz) * ps, 16), ps)
        return remote(own.at[k, y, piece], z_in.at[k, o], z_s.at[k, o], z_r.at[k, o], others[o - 1])

    def zg_copy(k, o):
        mine = own.at[k, 1 - y, pl.ds(pl.multiple_of(x * hs + z * ps, 16), ps)]
        return remote(mine, mine, zg_s.at[k, o], zg_r.at[k, o], others[o - 1])

    def xg_copy(k):
        mine = own.at[k, 1 - y, pl.ds(pl.multiple_of(x * hs, 16), hs)]
        return remote(mine, mine, xg_s.at[k], xg_r.at[k], side)

    def out_copy(k):
        start = k * slab
        if fine:
            mat, rest = lax.rem(lax.div(k, subs), 2), lax.div(k, 2 * subs) * tile + lax.rem(k, subs) * slab
            start = jnp.where(k < given // slab, mat * share + rest, start)
        rows = pl.ds(pl.multiple_of(start, slab), slab)
        return pltpu.make_async_copy(own.at[k, 1 - y], out.at[rows, :], out_sem.at[k])

    def stage_core(k):
        core_copy(k).wait_recv()

        def add(r):
            for p in range(2):
                own[k, p, r] = (own[k, p, r].astype(f32) + core_in[k, p, r].astype(f32)).astype(bf16)

        _row_loop(slab, 16, add)
        y_copy(k).start()

    def stage_y(k):
        y_copy(k).wait()

        def add(r):
            own[k, y, r] = (own[k, y, r].astype(f32) + y_in[k, r].astype(f32)).astype(bf16)

        _row_loop(slab, 32, add)
        x_copy(k).start()

    def stage_x(k):
        x_copy(k).wait_recv()

        def add(r):
            at = pl.ds(pl.multiple_of(x * hs + r.start, 16), r.size)
            own[k, y, at] = (own[k, y, at].astype(f32) + x_in[k, r].astype(f32)).astype(bf16)

        _row_loop(hs, rs, add)
        for o in range(1, nz):
            z_copy(k, o).start()

    def stage_z(k):
        for o in range(1, nz):
            z_copy(k, o).wait_recv()

        def add(r):
            at = pl.ds(pl.multiple_of(x * hs + z * ps + r.start, 16), r.size)
            total = own[k, y, at].astype(f32)
            for o in range(1, nz):
                total += z_in[k, o, r].astype(f32)
            own[k, 1 - y, at] = total.astype(bf16)

        _row_loop(ps, rs, add)
        for o in range(1, nz):
            zg_copy(k, o).start()

    def stage_zg(k):
        for o in range(1, nz):
            zg_copy(k, o).wait_recv()
        xg_copy(k).start()

    def stage_xg(k):
        xg_copy(k).wait_recv()
        out_copy(k).start()

    def dot(a, b, dims):
        return lax.dot_general(a, b, (dims, ((), ())), preferred_element_type=f32)

    def head_pair(p):
        cols = pl.ds(pl.multiple_of(p * pair, pair), pair)
        q2, k2, v2, g2 = (act[i, :, cols] for i in range(4))
        first = lax.broadcasted_iota(jnp.int32, (1, pair), 1) < HEAD_DIM
        kept = keep[...] > 0
        found = []
        for h in range(2):
            mask = jnp.where(first == (h == 0), 1.0, 0.0)
            q_h = q2 * (mask * scale).astype(bf16)
            g_h = g2 * mask.astype(bf16)
            scores = dot(k2, q_h, ((1,), (1,)))
            soft = jnp.where(kept, jnp.exp(scores - log_total[pl.ds(2 * p + h, 1), :]), 0.0)
            grad_soft = dot(v2, g_h, ((1,), (1,)))
            inner = jnp.sum(soft * grad_soft, axis=0, keepdims=True)
            grad_scores = (soft * (grad_soft - inner)).astype(bf16)
            found.append(
                (
                    dot(k2, grad_scores, ((0,), (0,))),
                    dot(grad_scores, q2, ((1,), (0,))),
                    dot(soft.astype(bf16), g2, ((1,), (0,))),
                )
            )
        q_t = jnp.concatenate([found[0][0][:HEAD_DIM], found[1][0][HEAD_DIM:]], axis=0)
        grad_q = (q_t.T * scale).astype(bf16)
        grad_k = (jnp.where(first, found[0][1], found[1][1]) * scale).astype(bf16)
        grad_v = jnp.where(first, found[0][2], found[1][2]).astype(bf16)
        grads[0, :, cols] = grad_q
        grads[1, :, cols] = grad_k
        grads[2, :, cols] = grad_v
        v_own[0:1, cols] = jnp.sum(grad_q.astype(f32), axis=0, keepdims=True)
        v_own[1:2, cols] = jnp.sum(grad_v.astype(f32), axis=0, keepdims=True)

    def feed_chunk(u):
        group, i, slot = lax.div(u, 4), lax.rem(u, 4), lax.rem(u, 2)

        @pl.when((i == 0) & (group > 0))
        def _():
            sent(0, group - 1)
            sent(1, group - 1)

        for load in chunk_loads(u):
            load.wait()

        @pl.when(u == 0)
        def _():
            for load in f_loads[:3]:
                load.wait()

        @pl.when(u + 1 < 4 * groups)
        def _():
            for load in chunk_loads(u + 1):
                load.start()

        mine, p, shard = i >= 2, lax.rem(i, 2), shard_of(i)
        grad_hidden = dot(grad_ffn[...], chunk_w[slot, 0], ((1,), (1,)))
        grad_pre = (grad_hidden * pieces[slot, 1].astype(f32)).astype(bf16)
        cols = pl.ds(pl.multiple_of(group * tile, tile), tile)
        v_own[pl.ds(8 + shard, 1), cols] = jnp.sum(grad_pre.astype(f32), axis=0, keepdims=True)
        deliver(0, group, 0, p, mine, dot(pieces[slot, 0], grad_ffn[...], ((0,), (0,))).astype(bf16))
        deliver(1, group, 1, p, mine, dot(grad_pre, first_low[...], ((0,), (0,))).astype(bf16))

        acc[...] += dot(grad_pre, chunk_w[slot, 1], ((1,), (0,)))

    def norm_backward():
        sent(0, groups - 1)
        sent(1, groups - 1)
        for load in act_loads[:3]:
            load.start()
        f_loads[3].wait()
        v_own[2:3, :] = jnp.zeros((1, width), f32)
        v_own[4:6, :] = jnp.zeros((2, width), f32)

        def rows_of(r):
            grad, value = acc[r, :], before[r, :]
            center = value - jnp.mean(value, axis=-1, keepdims=True)
            spread = lax.rsqrt(jnp.mean(center * center, axis=-1, keepdims=True) + norm_eps)
            xhat = center * spread
            scaled = grad * gain[...]
            inner = scaled - jnp.mean(scaled, axis=-1, keepdims=True)
            result = spread * (inner - xhat * jnp.mean(scaled * xhat, axis=-1, keepdims=True))
            low = result.astype(bf16)
            acc[r, :] = result
            grads[2, r, :] = low
            v_own[2:3, :] += jnp.sum(low.astype(f32), axis=0, keepdims=True)
            v_own[4:5, :] += jnp.sum(grad * xhat, axis=0, keepdims=True)
            v_own[5:6, :] += jnp.sum(grad, axis=0, keepdims=True)

        _row_loop(slots, 32, rows_of)

    def term(m, left, right):
        def run(i, carry):
            rows = pl.ds(pl.multiple_of(shard_of(i) * tile, tile), tile)
            value = dot(left[:, rows], right[...], ((0,), (0,))).astype(bf16)
            deliver(None, m, m - 1 if not isinstance(m, int) or m else 0, lax.rem(i, 2), i >= 2, value)
            return carry

        lax.fori_loop(0, 4, run, 0)

    def out_backward():
        act_loads[3].wait()
        w_loads[0].wait()
        deliver_lane = grads.at[0]

        def run(i, carry):
            rows = pl.ds(pl.multiple_of(shard_of(i) * tile, tile), tile)
            value = dot(act[3, :, rows], grads[2], ((0,), (0,))).astype(bf16)
            p = lax.rem(i, 2)

            @pl.when(i < 2)
            def _():
                deliver_lane[pl.ds(pl.multiple_of(p * tile, tile), tile), :] = value
                for sub in range(subs):
                    k, at = slab_of(None, 0, sub)
                    src = deliver_lane.at[pl.ds(pl.multiple_of(p * tile + sub * part, part), part), :]
                    remote(src, core_in.at[k, p, pl.ds(at, part), :], c_s.at[k], c_r.at[k], core).start()

            @pl.when(i >= 2)
            def _():
                for sub in range(subs):
                    k, at = slab_of(None, 0, sub)
                    own[k, p, pl.ds(at, part)] = value[sub * part : (sub + 1) * part]

            return carry

        lax.fori_loop(0, 4, run, 0)

        def mix(r):
            act[3, r, :] = dot(grads[2, r, :], weights[0], ((1,), (1,))).astype(bf16)

        _row_loop(slots, 128, mix)
        w_loads[2].start()
        sent(None, 0)

    def resid_part(m):
        w_loads[m + 1].wait()

        def rows_of(r):
            value = acc[r, :] + dot(grads[m, r, :], weights[(m + 1) % 2], ((1,), (1,)))
            if m < 2:
                acc[r, :] = value
            else:
                grad_tokens[r, :] = value.astype(bf16)
                time_sum[...] += jnp.sum(value, axis=0, keepdims=True)

        _row_loop(slots, 128, rows_of)
        if m == 0:
            w_loads[3].start()

    v_half = v_core.shape[0]
    v_mine = pl.ds(pl.multiple_of(c * v_half, v_half), v_half)
    v_given = pl.ds(pl.multiple_of((1 - c) * v_half, v_half), v_half)

    def v_copy(i):
        peers = [core, across, side] + others + [core]
        if i == 0:
            src, dst = v_own.at[v_given], v_core
        elif i == 2 + nz:
            src = dst = vec_out.at[v_mine]
        else:
            src, dst = v_sum.at[min(i, 3) - 1], v_z.at[i - 2] if i > 2 else (v_y, v_x)[i - 1]
        return remote(src, dst, vs.at[i], vr.at[i], peers[i])

    def v_stage(i):
        if i == 0:
            v_copy(0).start()
        elif i <= 3:
            v_copy(i - 1).wait_recv()
            before = v_own[v_mine] if i == 1 else v_sum[i - 2]
            v_sum[i - 1] = before + (v_core, v_y, v_x)[i - 1][...]
            for j in range(i, i + 1 if i < 3 else 2 + nz):
                v_copy(j).start()
        elif i == 4:
            total = v_sum[2]
            for o in range(1, nz):
                v_copy(2 + o).wait_recv()
                total = total + v_z[o]
            vec_out[v_mine] = total
            v_copy(2 + nz).start()
        else:
            v_copy(2 + nz).wait_recv()

    def w_copy(q, i):
        peers = [across, side] + others + [core]
        if i == 0:
            part = rec_out.at[q, dp, y, c]
        elif i == 1:
            part = rec_out.at[q, dp, :, c]
        elif i < 1 + nz:
            part = rec_out.at[q, pl.ds(z * 2, 2), :, c]
        else:
            part = rec_out.at[q, :, :, c]
        return remote(part, part, ws.at[q, i], wr.at[q, i], peers[i])

    def w_stage(q, i):
        if i == 0:
            if q == 0:
                rec_out[0, dp, y, c] = embed[...]
            else:
                rounded = time_sum[...].astype(bf16).astype(f32)
                lanes = embed.shape[-1]
                for j in range(width // lanes):
                    rec_out[1, dp, y, c, j : j + 1, :] = rounded[:, j * lanes : (j + 1) * lanes]
            w_copy(q, 0).start()
        elif i < 3:
            w_copy(q, i - 1).wait_recv()
            for j in range(i, i + 1 if i == 1 else 1 + nz):
                w_copy(q, j).start()
        elif i == 3:
            for o in range(1, nz):
                w_copy(q, 1 + o).wait_recv()
            w_copy(q, 1 + nz).start()
        else:
            w_copy(q, 1 + nz).wait_recv()

    stages = [stage_y, stage_x, stage_z, stage_zg, stage_xg]
    feed = 4 * groups
    per = 2 * subs
    terms_at = feed + 4
    base = 4 if fine else terms_at + 3
    small = [(feed + 4 + at, functools.partial(v_stage, i)) for i, at in enumerate((0, 1, 4, 6, 8, 9))]
    for q, first in ((0, 2), (1, terms_at + 6)):
        small += [(first + at, functools.partial(w_stage, q, i)) for i, at in enumerate((0, 3, 5, 7, 8))]
    ticks = max([base + count + lag * (len(stages) - 1)] + [at + 1 for at, _ in small])
    v_own[...] = vec[...]
    time_sum[...] = jnp.zeros_like(time_sum)

    def cores(start, stop):
        def run(k, carry):
            stage_core(k)
            return carry

        lax.fori_loop(start, stop, run, 0)

    def tick(t, carry):
        @pl.when(t < feed)
        def _():
            feed_chunk(t)

        @pl.when(t == feed)
        def _():
            norm_backward()

        @pl.when(t == feed + 1)
        def _():
            out_backward()
            for load in act_loads[:3]:
                load.wait()

        @pl.when((t > feed) & (t < terms_at))
        def _():
            done = 3 * (t - feed - 1)

            def run(p, carry):
                head_pair(p)
                return carry

            lax.fori_loop(done, jnp.minimum(done + 3, pairs), run, 0)

        @pl.when((t >= terms_at) & (t < terms_at + 3))
        def _():
            m = t - terms_at

            @pl.when(m == 0)
            def _():
                f_loads[4].start()
                f_loads[4].wait()

            term(m + 1, resid_low, grads.at[m])

        for m in range(3):

            @pl.when(t == terms_at + 3 + m)
            def _():
                resid_part(m)

        if fine:

            @pl.when((t < feed) & (lax.rem(t, 4) == 3))
            def _():
                start = lax.div(t, 4) * per
                cores(start, start + per)

            @pl.when((t == feed + 1) | ((t >= terms_at) & (t < terms_at + 3)))
            def _():
                start = given // slab + jnp.maximum(t - terms_at + 1, 0) * subs
                cores(start, start + subs)

        else:

            @pl.when(t == terms_at + 2)
            def _():
                cores(0, count)

        for d, stage in enumerate(stages):
            k = t - base - d * lag

            @pl.when((k >= 0) & (k < count))
            def _():
                stage(k)

        for at, run in small:
            pl.when(t == at)(run)

        return carry

    lax.fori_loop(0, ticks, tick, 0)
    for m in range(3):
        sent(None, m + 1)

    def finish(k, carry):
        x_copy(k).wait_send()
        for o in range(1, nz):
            z_copy(k, o).wait_send()
            zg_copy(k, o).wait_send()
        xg_copy(k).wait_send()
        out_copy(k).wait()
        return carry

    lax.fori_loop(0, count, finish, 0)
    for i in range(3 + nz):
        v_copy(i).wait_send()
    for i in range(2 + nz):
        for q in range(2):
            w_copy(q, i).wait_send()


def backward_and_reduce(dp_n, streams, inside_args):
    slots, units = streams[0].shape
    vec, embed = inside_args[-2:]
    width = vec.shape[1]
    tile = width // 4
    rows = 2 * units // 4 + 4 * tile
    slab = max(128, 16 * dp_n)
    count, nz = rows // slab, dp_n // 2
    bf16, f32 = jnp.bfloat16, jnp.float32
    dma, vmem = pltpu.SemaphoreType.DMA, pltpu.VMEM
    v_shape = vec.shape
    half_shape = (v_shape[0] // 2, width)
    anywhere, inside = pl.BlockSpec(memory_space=pl.ANY), pl.BlockSpec(memory_space=pltpu.VMEM)
    return pl.pallas_call(
        functools.partial(_backward_kernel, dp_n, slab, 1),
        out_shape=[
            jax.ShapeDtypeStruct((rows, width), bf16),
            jax.ShapeDtypeStruct(v_shape, f32),
            jax.ShapeDtypeStruct((2, dp_n, 2, 2) + embed.shape, f32),
            jax.ShapeDtypeStruct((slots, width), bf16),
        ],
        in_specs=[anywhere] * len(streams) + [inside] * len(inside_args),
        out_specs=[anywhere, inside, inside, inside],
        scratch_shapes=[
            vmem((count, 2, slab, width), bf16),
            vmem((count, 2, slab, width), bf16),
            vmem((count, slab, width), bf16),
            vmem((count, slab // 2, width), bf16),
            vmem((count, nz, slab // 2 // nz, width), bf16),
            vmem((4, slots, width), bf16),
            vmem((3, slots, width), bf16),
            vmem((2, width, width), bf16),
            vmem((2, 2, slots, tile), bf16),
            vmem((2, 2, tile, width), bf16),
            vmem((slots, width), f32),
            vmem((slots, width), f32),
            vmem((1, width), f32),
            vmem(v_shape, f32),
            vmem(half_shape, f32),
            vmem(half_shape, f32),
            vmem(half_shape, f32),
            vmem((nz,) + half_shape, f32),
            vmem((3,) + half_shape, f32),
        ]
        + [dma((2, 4)), dma((4,)), dma((4,)), dma((5,))]
        + [dma((count,))] * 6
        + [dma((count, nz))] * 4
        + [dma((count,))] * 3
        + [dma((3 + nz,))] * 2
        + [dma((2, 2 + nz))] * 2,
        compiler_params=pltpu.CompilerParams(collective_id=1, has_side_effects=True, vmem_limit_bytes=67_043_328),
        name="backward_and_reduce",
    )(*streams, *inside_args)


def local(
    dp_n,
    tokens,
    time_embed,
    lengths,
    cotangent,
    w_query,
    w_key,
    w_value,
    w_out,
    w_time,
    w_in,
    w_down,
    b_query,
    b_value,
    b_out,
    b_time,
    b_in,
    b_down,
    gain_one,
    shift_one,
    gain_two,
    shift_two,
):
    f32, bf16 = jnp.float32, jnp.bfloat16
    seq_rank = lax.axis_index("seq")
    item_count = time_embed.shape[0]
    token_count = tokens.shape[0]
    slot_count = token_count // item_count
    width = tokens.shape[1]
    rows = w_time.shape[0]

    def mm(a, b, dims):
        return lax.dot_general(a, b, (dims, ((), ())), preferred_element_type=f32)

    own_lengths = lax.dynamic_slice_in_dim(lengths, seq_rank * item_count, item_count, 0)
    slot_index = lax.broadcasted_iota(jnp.int32, (item_count, slot_count), 1)
    own_valid = slot_index < own_lengths[:, None] + BLOCK
    row_keep = own_valid.reshape(token_count, 1).astype(f32)
    rows_in = jnp.stack([b_time, b_query, b_value, b_out, gain_one, shift_one, b_down, b_down]).astype(f32)
    (
        _,
        full_query,
        full_key,
        full_value,
        full_out,
        full_in,
        full_down,
        resid_low,
        query_rows,
        key_rows,
        value_rows,
        mixed_rows,
        first_in,
        hidden_low,
        gelu_slope,
        ffn_out,
        log_total,
    ) = gather_and_forward(
        [w_time, w_query, w_key, w_value, w_out, w_in, w_down],
        tokens,
        jnp.broadcast_to(time_embed, (16, width)),
        rows_in,
        b_in.astype(f32).reshape(1, -1),
        row_keep,
    )
    first_norm = layer_norm(first_in, gain_one.astype(f32), shift_one.astype(f32))
    first_low = first_norm.astype(bf16)
    second_norm, second_pull = jax.vjp(
        layer_norm, first_norm + ffn_out, gain_two.astype(f32), shift_two.astype(f32)
    )
    layer_out = (second_norm * row_keep).astype(bf16)
    grad_second_in, grad_gain_two, grad_shift_two = second_pull(cotangent.astype(f32) * row_keep)
    grad_ffn = grad_second_in.astype(bf16)
    zero = jnp.zeros((1, width), f32)
    vec = jnp.concatenate(
        [
            zero,
            zero,
            zero,
            jnp.sum(grad_ffn, axis=0, dtype=f32, keepdims=True),
            zero,
            zero,
            grad_gain_two[None],
            grad_shift_two[None],
            jnp.zeros((-(-b_in.shape[0] // width) // 8 * 8 + 8, width), f32),
        ]
    )
    sums, vectors, every, grad_tokens = backward_and_reduce(
        dp_n,
        [
            hidden_low,
            gelu_slope,
            full_down,
            full_in,
            grad_second_in,
            first_in,
            query_rows,
            key_rows,
            value_rows,
            mixed_rows,
            full_out,
            full_query,
            full_key,
            full_value,
            grad_ffn,
            first_low,
            resid_low,
        ],
        [
            log_total,
            row_keep,
            gain_one.astype(f32).reshape(1, -1),
            vec,
            time_embed.astype(f32).reshape(-1, 128),
        ],
    )
    time_rows, time_grads = every.reshape(2, -1, width).astype(bf16)
    own_columns = lax.dynamic_slice_in_dim(time_rows, seq_rank * rows, rows, 1)
    grad_w_time = mm(own_columns, time_grads, ((0,), (0,)))
    grad_b_time = jnp.sum(time_grads, axis=0, dtype=f32)
    grad_b_in = vectors[8 : 8 + b_in.shape[0] // width].reshape(-1)
    sums = sums.astype(f32)
    down_rows = in_rows = w_in.shape[0]
    ends = [0, down_rows, down_rows + in_rows]
    ends += [ends[-1] + rows * i for i in range(1, 5)]
    share_down, share_in, share_out, share_q, share_k, share_v = (
        sums[lo:hi] for lo, hi in zip(ends[:-1], ends[1:])
    )
    return (
        layer_out,
        grad_tokens,
        share_q,
        share_k,
        share_v,
        share_out,
        grad_w_time,
        share_in,
        share_down,
        vectors[0],
        vectors[1],
        vectors[2],
        grad_b_time,
        grad_b_in,
        vectors[3],
        vectors[4],
        vectors[5],
        vectors[6],
        vectors[7],
    )


def solution(mesh):
    in_specs = (
        P(("dp", "seq"), None),
        P(("dp", "seq"), None),
        P("dp"),
        P(("dp", "seq"), None),
        P("seq", None),
        P("seq", None),
        P("seq", None),
        P("seq", None),
        P("seq", None),
        P("seq", None),
        P("seq", None),
        P(),
        P(),
        P(),
        P(),
        P(),
        P(),
        P(),
        P(),
        P(),
        P(),
    )
    out_specs = (
        P(("dp", "seq"), None),
        P(("dp", "seq"), None),
        P("seq", None),
        P("seq", None),
        P("seq", None),
        P("seq", None),
        P("seq", None),
        P("seq", None),
        P("seq", None),
        P(),
        P(),
        P(),
        P(),
        P(),
        P(),
        P(),
        P(),
        P(),
        P(),
    )
    return jax.shard_map(functools.partial(local, mesh.shape["dp"]), mesh=mesh, in_specs=in_specs, out_specs=out_specs, check_vma=False)
```

```python
import functools

import jax
import jax.numpy as jnp
from jax import lax
from jax.experimental import pallas as pl
from jax.experimental.pallas import tpu as pltpu
from jax.sharding import PartitionSpec as P

HEAD_DIM = 64
BLOCK = 25
MESH = pl.DeviceIdType.MESH


norm_eps = 1e-05
neg_large = -1e30


def layer_norm(values, gain, shift):
    center = values - jnp.mean(values, axis=-1, keepdims=True)
    spread = lax.rsqrt(jnp.mean(center * center, axis=-1, keepdims=True) + norm_eps)
    return center * spread * gain + shift


def gelu_parts(values):
    half = 0.5 + 0.5 * lax.erf(values * 0.5**0.5)
    density = jnp.exp(-0.5 * values * values) * (0.5 / jnp.pi) ** 0.5
    return values * half, half + values * density


def _forward_kernel(sizes, *refs):
    n = len(sizes)
    given, (tokens, embed, cotangent, lengths) = refs[:n], refs[n : n + 4]
    biases, refs = refs[n + 4 : n + 14], refs[n + 14 :]
    outs = refs[:n]
    (resid_out, query_out, key_out, value_out, mixed_out, pre_out, hidden_out, slope_out, second_out) = refs[n : n + 9]
    grad_out, first_out, log_total, layer_out, vec = refs[n + 9 : n + 14]
    full = refs[n + 14 : 2 * n + 14]
    act, pre, first_low, hidden, slope, total, rows_in, bias_in = refs[2 * n + 14 : 2 * n + 22]
    load_sem, save_sem, act_sem, c_send, c_recv, y_send, y_recv, x_send, x_recv, f_send, f_recv, g_send, g_recv = refs[
        2 * n + 22 :
    ]
    f32, bf16 = jnp.float32, jnp.bfloat16
    w_time, w_query, w_key, w_value, w_out, w_in, w_down = full
    slots, width = tokens.shape
    pair = 2 * HEAD_DIM
    scale = HEAD_DIM**-0.5
    dp, me = lax.axis_index("dp"), lax.axis_index("seq")
    half = lax.rem(dp, 2)

    def home(a, shard):
        return full[a].at[pl.ds(pl.multiple_of(shard * sizes[a], sizes[a]), sizes[a]), :]

    loads = [pltpu.make_async_copy(given[a], home(a, me), load_sem.at[a]) for a in range(n)]
    for load in loads:
        load.start()
    core, across, side = (dp, me ^ 1), (dp, me ^ 2), (dp ^ 1, me)
    barrier = pltpu.get_barrier_semaphore()
    for peer in (core, across, side):
        pl.semaphore_signal(barrier, inc=1, device_id=peer, device_id_type=MESH)
    pl.semaphore_wait(barrier, 3)

    def remote(src, send, recv, peer):
        return pltpu.make_async_remote_copy(
            src_ref=src, dst_ref=src, send_sem=send, recv_sem=recv, device_id=peer, device_id_type=MESH
        )

    chunks, of = [], [[] for _ in sizes]
    for a, rows in enumerate(sizes):
        step = min(rows // 2, 128)
        for off in range(0, rows // 2, step):
            of[a].append(len(chunks))
            chunks.append((a, rows, off, step))

    def region(j, shard, part):
        a, rows, off, step = chunks[j]
        start = pl.multiple_of(shard * rows + part * (rows // 2) + off, 16)
        return full[a].at[pl.ds(start, step), :]

    saves = []

    def crossing(j):
        return remote(region(j, me, half), y_send.at[j], y_recv.at[j], across)

    def core_copy(a):
        return remote(home(a, me), c_send.at[a], c_recv.at[a], core)

    def sideways(j):
        return remote(region(j, me ^ 2, half), x_send.at[j], x_recv.at[j], side)

    def first_half(j):
        return remote(region(j, me ^ 2, half), f_send.at[j], f_recv.at[j], core)

    def second_half(j):
        return remote(region(j, me ^ 2, 1 - half), g_send.at[j], g_recv.at[j], core)

    for j, (a, rows, off, _) in enumerate(chunks):
        if off == 0:
            loads[a].wait()
            core_copy(a).start()
        crossing(j).start()

    def step(j):
        crossing(j).wait_recv()
        sideways(j).start()
        first_half(j).start()

    def turn(j):
        sideways(j).wait_recv()
        second_half(j).start()

    def arrived(j):
        first_half(j).wait_recv()
        second_half(j).wait_recv()

    def save(src, dst, sem):
        copy = pltpu.make_async_copy(src, dst, sem)
        copy.start()
        saves.append(copy)

    def complete(a):
        for j in of[a]:
            arrived(j)
        core_copy(a).wait_recv()
        save(full[a], outs[a], save_sem.at[a])

    def dot(a, b, dims):
        return lax.dot_general(a, b, (dims, ((), ())), preferred_element_type=f32)

    for i, ref in enumerate(biases[:9]):
        rows_in[i : i + 1, :] = ref[...].astype(f32).reshape(1, width)
    bias_in[...] = biases[9][...].astype(f32).reshape(bias_in.shape)
    bound = lengths[me] + BLOCK

    def bias(i):
        return rows_in[i : i + 1, :]

    tile = 256

    def tiles(extent, size, body):
        def run(i, carry):
            body(pl.ds(pl.multiple_of(i * size, size), size))
            return carry

        lax.fori_loop(0, extent // size, run, 0)

    def project(weight, i, row):
        def body(cols):
            value = dot(act[0], weight[:, cols], ((1,), (0,)))
            if row is not None:
                value += rows_in[row : row + 1, cols]
            act[i, :, cols] = value.astype(bf16)

        tiles(width, tile, body)
        save(act.at[i], (resid_out, query_out, key_out, value_out)[i], act_sem.at[i])

    step(0)
    step(1)
    turn(0)
    complete(0)
    wide = jnp.broadcast_to(embed[...].astype(f32), (16, width)).astype(bf16)
    time_proj = dot(wide, w_time[...], ((1,), (0,)))[0:1] + bias(0)

    def enter(r):
        value = tokens[r, :].astype(f32) + time_proj
        pre[r, :] = value
        act[0, r, :] = value.astype(bf16)

    tiles(slots, 64, enter)
    pltpu.make_async_copy(act.at[0], resid_out, act_sem.at[0]).start()
    for j, (weight, row) in enumerate(((w_query, 1), (w_key, None), (w_value, 2))):
        step(j + 2)
        turn(j + 1)
        complete(j + 1)
        project(weight, j + 1, row)

    first = lax.broadcasted_iota(jnp.int32, (1, pair), 1) < HEAD_DIM

    def head_pair(p):
        cols = pl.ds(pl.multiple_of(p * pair, pair), pair)
        q2, k2, v2 = (act[i, :, cols] for i in (1, 2, 3))
        kept = lax.broadcasted_iota(jnp.int32, (slots, 1), 0) < bound
        found = []
        for h in range(2):
            mask = jnp.where(first == (h == 0), scale, 0.0)
            scores = jnp.where(kept, dot(k2, q2 * mask.astype(bf16), ((1,), (1,))), neg_large)
            top = jnp.max(scores, axis=0, keepdims=True)
            weights = jnp.exp(scores - top)
            norm = jnp.sum(weights, axis=0, keepdims=True)
            soft = (weights * (1.0 / norm)).astype(bf16)
            log_total[pl.ds(2 * p + h, 1), :] = top + jnp.log(norm)
            found.append(dot(v2, soft, ((0,), (0,))))
        mixed = jnp.concatenate([found[0][:HEAD_DIM], found[1][HEAD_DIM:]], axis=0)
        act[4, :, cols] = mixed.T.astype(bf16)

    beside = {0: (None, 4), 1: (5, None), 3: (6, 5), 5: (7, 6), 7: (8, 7)}

    def attend(p, carry):
        for at, (enters, turns) in beside.items():

            @pl.when(p == at)
            def _():
                if enters is not None:
                    step(enters)
                if turns is not None:
                    turn(turns)

        head_pair(p)
        return carry

    lax.fori_loop(0, width // pair, attend, 0)
    save(act.at[4], mixed_out, act_sem.at[4])
    complete(4)

    def attn_out(cols):
        pre[:, cols] += dot(act[4], w_out[:, cols], ((1,), (0,))) + rows_in[3:4, cols]

    tiles(width, tile, attn_out)
    step(9)
    turn(8)
    save(pre, pre_out, act_sem.at[5])

    def norm_rows(r):
        first_low[r, :] = layer_norm(pre[r, :], bias(4), bias(5)).astype(bf16)

    tiles(slots, 32, norm_rows)
    save(first_low, first_out, act_sem.at[10])

    def feed_up(start, size):
        rows = pl.ds(pl.multiple_of(start, size), size)
        value = dot(first_low[...], w_in[rows, :], ((1,), (1,))) + bias_in[:, rows]
        up, lean = gelu_parts(value)
        hidden[:, rows] = up.astype(bf16)
        slope[:, rows] = lean.astype(bf16)

    share = sizes[5]

    def up_shard(shard):
        def run(i, carry):
            feed_up(shard * share + i * tile, tile)
            return carry

        lax.fori_loop(0, share // tile, run, 0)

    def down_shards(shards, opening):
        def body(cols):
            value = rows_in[6:7, cols] if opening else total[:, cols]
            for shard in shards:
                rows = pl.ds(pl.multiple_of(shard * share, share), share)
                value = value + dot(hidden[:, rows], w_down[rows, cols], ((1,), (0,)))
            total[:, cols] = value

        tiles(width, tile, body)

    def up_arrived(which):
        def run(i, carry):
            shard = (me ^ 2) ^ lax.rem(i, 2)
            feed_up(shard * share + lax.div(i, 2) * (share // 2) + which * tile, tile)
            return carry

        lax.fori_loop(0, 4, run, 0)

    up_shard(me)
    step(10)
    turn(9)
    core_copy(5).wait_recv()
    up_shard(me ^ 1)
    step(11)
    turn(10)
    core_copy(6).wait_recv()
    down_shards((me, me ^ 1), True)
    for j in (5, 6):
        arrived(j)
    up_arrived(0)
    step(12)
    turn(11)
    for j in (7, 8):
        arrived(j)
    save(w_in, outs[5], save_sem.at[5])
    up_arrived(1)
    turn(12)
    save(hidden, hidden_out, act_sem.at[6])
    save(slope, slope_out, act_sem.at[7])
    for j in of[6]:
        arrived(j)
    save(w_down, outs[6], save_sem.at[6])
    down_shards((me ^ 2, me ^ 3), False)
    pltpu.make_async_copy(act.at[0], resid_out, act_sem.at[0]).wait()
    vec[...] = jnp.zeros_like(vec)

    def second_rows(r):
        first_norm = layer_norm(pre[r, :], bias(4), bias(5))
        value = first_norm + total[r, :]
        center = value - jnp.mean(value, axis=-1, keepdims=True)
        spread = lax.rsqrt(jnp.mean(center * center, axis=-1, keepdims=True) + norm_eps)
        xhat = center * spread
        rows = r.start + lax.broadcasted_iota(jnp.int32, (r.size, 1), 0)
        valid = jnp.where(rows < bound, 1.0, 0.0)
        layer_out[r, :] = ((xhat * bias(7) + bias(8)) * valid).astype(bf16)
        grad = cotangent[r, :].astype(f32) * valid
        scaled = grad * bias(7)
        inner = scaled - jnp.mean(scaled, axis=-1, keepdims=True)
        result = spread * (inner - xhat * jnp.mean(scaled * xhat, axis=-1, keepdims=True))
        low = result.astype(bf16)
        total[r, :] = result
        act[0, r, :] = low
        vec[3:4, :] += jnp.sum(low.astype(f32), axis=0, keepdims=True)
        vec[6:7, :] += jnp.sum(grad * xhat, axis=0, keepdims=True)
        vec[7:8, :] += jnp.sum(grad, axis=0, keepdims=True)

    tiles(slots, 32, second_rows)
    save(total, second_out, act_sem.at[8])
    save(act.at[0], grad_out, act_sem.at[9])
    for copy in saves:
        copy.wait()
    for a in range(n):
        core_copy(a).wait_send()
    for j in range(len(chunks)):
        for copy in (crossing, sideways, first_half, second_half):
            copy(j).wait_send()


def gather_and_forward(arrays, tokens, embed, cotangent, lengths, biases):
    sizes = tuple(a.shape[0] for a in arrays)
    n = len(arrays)
    m = sum(max(1, r // 256) for r in sizes)
    slots, width = tokens.shape
    units = 4 * sizes[5]
    bf16, f32 = jnp.bfloat16, jnp.float32
    dma, vmem = pltpu.SemaphoreType.DMA, pltpu.VMEM
    anywhere, inside = pl.BlockSpec(memory_space=pl.ANY), pl.BlockSpec(memory_space=pltpu.VMEM)
    wide = jax.ShapeDtypeStruct((slots, width), bf16)
    wide_f32 = jax.ShapeDtypeStruct((slots, width), f32)
    return pl.pallas_call(
        functools.partial(_forward_kernel, sizes),
        out_shape=[jax.ShapeDtypeStruct((4 * a.shape[0], a.shape[1]), a.dtype) for a in arrays]
        + [wide] * 5
        + [wide_f32]
        + [jax.ShapeDtypeStruct((slots, units), bf16)] * 2
        + [wide_f32, wide, wide]
        + [
            jax.ShapeDtypeStruct((width // HEAD_DIM, slots), f32),
            wide,
            jax.ShapeDtypeStruct((8 + units // width + -units // width % 8, width), f32),
        ],
        in_specs=[anywhere] * n
        + [inside] * 3
        + [pl.BlockSpec(memory_space=pltpu.SMEM)]
        + [inside] * len(biases),
        out_specs=[anywhere] * (n + 11) + [inside] * 3,
        scratch_shapes=[vmem((4 * a.shape[0], a.shape[1]), a.dtype) for a in arrays]
        + [
            vmem((5, slots, width), bf16),
            vmem((slots, width), f32),
            vmem((slots, width), bf16),
            vmem((slots, units), bf16),
            vmem((slots, units), bf16),
            vmem((slots, width), f32),
            vmem((16, width), f32),
            vmem((1, units), f32),
        ]
        + [dma((n,)), dma((n,)), dma((11,))]
        + [dma((n,))] * 2
        + [dma((m,))] * 8,
        compiler_params=pltpu.CompilerParams(
            collective_id=0, has_side_effects=True, vmem_limit_bytes=66_000_000
        ),
        name="gather_and_forward",
    )(*arrays, tokens, embed, cotangent, lengths, *biases)


def _row_loop(rows, step, body):
    def run(i, carry):
        body(pl.ds(pl.multiple_of(i * step, step), step))
        return carry

    lax.fori_loop(0, rows // step, run, 0)


def _backward_kernel(dp_n, slab, lag, *refs):
    (hidden, slope, w_down, w_in, second, first_in, query, key, value, mixed, w_out, w_query, w_key, w_value) = refs[:14]
    (grad_ffn_in, first_low_in, resid_in, log_total, gain_in, vec, embed, lengths) = refs[14:22]
    out, vec_out, rec_out, grad_tokens = refs[22:26]
    (own, core_in, y_in, x_in, z_in, act, grads, weights, pieces, chunk_w, acc, before) = refs[26:38]
    (time_sum, v_own, v_core, v_y, v_x, v_z, v_sum) = refs[38:45]
    (piece_sem, act_sem, w_sem, f_sem, c_s, c_r, y_s, y_r, x_s, x_r, z_s, z_r, zg_s, zg_r, xg_s, xg_r, out_sem) = refs[45:62]
    vs, vr, ws, wr = refs[62:]
    f32, bf16 = jnp.float32, jnp.bfloat16
    count = out.shape[0] // slab
    nz = dp_n // 2
    scale = HEAD_DIM**-0.5
    slots, width = query.shape
    pair = 2 * HEAD_DIM
    pairs = width // pair
    share = w_in.shape[0] // 4
    tile = width // 4
    groups = share // tile
    fine = slab <= tile
    subs = tile // slab if fine else 1
    part = min(slab, tile)
    dp, me = lax.axis_index("dp"), lax.axis_index("seq")
    x, z, y, c = lax.rem(dp, 2), lax.div(dp, 2), lax.div(me, 2), lax.rem(me, 2)
    core, across, side = (dp, me ^ 1), (dp, me ^ 2), (dp ^ 1, me)
    others = [(lax.rem(z + o, nz) * 2 + x, me) for o in range(1, nz)]

    def shard_of(i):
        return lax.rem(i, 2) * 2 + lax.rem(1 - c + lax.div(i, 2), 2)

    def chunk_loads(u):
        start = pl.multiple_of(shard_of(lax.rem(u, 4)) * share + lax.div(u, 4) * tile, tile)
        rows, slot = pl.ds(start, tile), lax.rem(u, 2)
        return [
            pltpu.make_async_copy(hidden.at[:, rows], pieces.at[slot, 0], piece_sem.at[slot, 0]),
            pltpu.make_async_copy(slope.at[:, rows], pieces.at[slot, 1], piece_sem.at[slot, 1]),
            pltpu.make_async_copy(w_down.at[rows, :], chunk_w.at[slot, 0], piece_sem.at[slot, 2]),
            pltpu.make_async_copy(w_in.at[rows, :], chunk_w.at[slot, 1], piece_sem.at[slot, 3]),
        ]

    act_loads = [
        pltpu.make_async_copy(src, act.at[i], act_sem.at[i]) for i, src in enumerate((query, key, value, mixed))
    ]
    w_loads = [
        pltpu.make_async_copy(src, weights.at[i % 2], w_sem.at[i])
        for i, src in enumerate((w_out, w_query, w_key, w_value))
    ]
    grad_ffn, first_low, resid_low = act.at[2], grads.at[1], act.at[3]
    f_loads = [
        pltpu.make_async_copy(src, dst, f_sem.at[i])
        for i, (src, dst) in enumerate(
            ((grad_ffn_in, grad_ffn), (first_low_in, first_low), (second, acc), (first_in, before), (resid_in, resid_low))
        )
    ]
    for load in f_loads[:1] + chunk_loads(0) + f_loads[1:4] + [act_loads[3], w_loads[0], w_loads[1]]:
        load.start()
    barrier = pltpu.get_barrier_semaphore()
    for peer in [core, across, side] + others:
        pl.semaphore_signal(barrier, inc=1, device_id=peer, device_id_type=MESH)
    pl.semaphore_wait(barrier, 3 + len(others))

    def remote(src, dst, send, recv, peer):
        return pltpu.make_async_remote_copy(
            src_ref=src, dst_ref=dst, send_sem=send, recv_sem=recv, device_id=peer, device_id_type=MESH
        )

    hs = slab // 2
    ps = hs // nz
    rs = min(ps, 32)
    given = 2 * share

    def slab_of(mat, group, sub):
        if fine:
            return (group * 2 * subs + mat * subs if mat is not None else group * subs + given // slab) + sub, 0
        if mat is not None:
            return mat, pl.multiple_of(group * tile, tile)
        return given // slab, pl.multiple_of(group * tile, tile)

    def deliver(mat, group, lane, p, mine, value):
        @pl.when(jnp.logical_not(mine))
        def _():
            act[lane, pl.ds(pl.multiple_of(p * tile, tile), tile), :] = value
            for sub in range(subs):
                k, at = slab_of(mat, group, sub)
                src = act.at[lane, pl.ds(pl.multiple_of(p * tile + sub * part, part), part), :]
                remote(src, core_in.at[k, p, pl.ds(at, part), :], c_s.at[k], c_r.at[k], core).start()

        @pl.when(mine)
        def _():
            for sub in range(subs):
                k, at = slab_of(mat, group, sub)
                own[k, p, pl.ds(at, part)] = value[sub * part : (sub + 1) * part]

    def sent(mat, group):
        for sub in range(subs):
            k, at = slab_of(mat, group, sub)
            rows = core_in.at[k, :, pl.ds(at, part), :]
            remote(rows, rows, c_s.at[k], c_r.at[k], core).wait_send()

    def core_copy(k):
        return remote(core_in.at[k], core_in.at[k], c_s.at[k], c_r.at[k], core)

    def y_copy(k):
        return remote(own.at[k, 1 - y], y_in.at[k], y_s.at[k], y_r.at[k], across)

    def x_copy(k):
        give = pl.ds(pl.multiple_of((1 - x) * hs, 16), hs)
        return remote(own.at[k, y, give], x_in.at[k], x_s.at[k], x_r.at[k], side)

    def z_copy(k, o):
        piece = pl.ds(pl.multiple_of(x * hs + lax.rem(z + o, nz) * ps, 16), ps)
        return remote(own.at[k, y, piece], z_in.at[k, o], z_s.at[k, o], z_r.at[k, o], others[o - 1])

    def zg_copy(k, o):
        mine = own.at[k, 1 - y, pl.ds(pl.multiple_of(x * hs + z * ps, 16), ps)]
        return remote(mine, mine, zg_s.at[k, o], zg_r.at[k, o], others[o - 1])

    def xg_copy(k):
        mine = own.at[k, 1 - y, pl.ds(pl.multiple_of(x * hs, 16), hs)]
        return remote(mine, mine, xg_s.at[k], xg_r.at[k], side)

    def out_copy(k):
        start = k * slab
        if fine:
            mat, rest = lax.rem(lax.div(k, subs), 2), lax.div(k, 2 * subs) * tile + lax.rem(k, subs) * slab
            start = jnp.where(k < given // slab, mat * share + rest, start)
        rows = pl.ds(pl.multiple_of(start, slab), slab)
        return pltpu.make_async_copy(own.at[k, 1 - y], out.at[rows, :], out_sem.at[k])

    def stage_core(k):
        core_copy(k).wait_recv()

        def add(r):
            for p in range(2):
                own[k, p, r] = (own[k, p, r].astype(f32) + core_in[k, p, r].astype(f32)).astype(bf16)

        _row_loop(slab, 16, add)
        y_copy(k).start()

    def stage_y(k):
        y_copy(k).wait()

        def add(r):
            own[k, y, r] = (own[k, y, r].astype(f32) + y_in[k, r].astype(f32)).astype(bf16)

        _row_loop(slab, 32, add)
        x_copy(k).start()

    def stage_x(k):
        x_copy(k).wait_recv()

        def add(r):
            at = pl.ds(pl.multiple_of(x * hs + r.start, 16), r.size)
            own[k, y, at] = (own[k, y, at].astype(f32) + x_in[k, r].astype(f32)).astype(bf16)

        _row_loop(hs, rs, add)
        for o in range(1, nz):
            z_copy(k, o).start()

    def stage_z(k):
        for o in range(1, nz):
            z_copy(k, o).wait_recv()

        def add(r):
            at = pl.ds(pl.multiple_of(x * hs + z * ps + r.start, 16), r.size)
            total = own[k, y, at].astype(f32)
            for o in range(1, nz):
                total += z_in[k, o, r].astype(f32)
            own[k, 1 - y, at] = total.astype(bf16)

        _row_loop(ps, rs, add)
        for o in range(1, nz):
            zg_copy(k, o).start()

    def stage_zg(k):
        for o in range(1, nz):
            zg_copy(k, o).wait_recv()
        xg_copy(k).start()

    def stage_xg(k):
        xg_copy(k).wait_recv()
        out_copy(k).start()

    def dot(a, b, dims):
        return lax.dot_general(a, b, (dims, ((), ())), preferred_element_type=f32)

    def head_pair(p):
        cols = pl.ds(pl.multiple_of(p * pair, pair), pair)
        q2, k2, v2, g2 = (act[i, :, cols] for i in range(4))
        first = lax.broadcasted_iota(jnp.int32, (1, pair), 1) < HEAD_DIM
        kept = lax.broadcasted_iota(jnp.int32, (slots, 1), 0) < bound
        found = []
        for h in range(2):
            mask = jnp.where(first == (h == 0), 1.0, 0.0)
            q_h = q2 * (mask * scale).astype(bf16)
            g_h = g2 * mask.astype(bf16)
            scores = dot(k2, q_h, ((1,), (1,)))
            soft = jnp.where(kept, jnp.exp(scores - log_total[pl.ds(2 * p + h, 1), :]), 0.0)
            grad_soft = dot(v2, g_h, ((1,), (1,)))
            inner = jnp.sum(soft * grad_soft, axis=0, keepdims=True)
            grad_scores = (soft * (grad_soft - inner)).astype(bf16)
            found.append(
                (
                    dot(k2, grad_scores, ((0,), (0,))),
                    dot(grad_scores, q2, ((1,), (0,))),
                    dot(soft.astype(bf16), g2, ((1,), (0,))),
                )
            )
        q_t = jnp.concatenate([found[0][0][:HEAD_DIM], found[1][0][HEAD_DIM:]], axis=0)
        grad_q = (q_t.T * scale).astype(bf16)
        grad_k = (jnp.where(first, found[0][1], found[1][1]) * scale).astype(bf16)
        grad_v = jnp.where(first, found[0][2], found[1][2]).astype(bf16)
        grads[0, :, cols] = grad_q
        grads[1, :, cols] = grad_k
        grads[2, :, cols] = grad_v
        v_own[0:1, cols] = jnp.sum(grad_q.astype(f32), axis=0, keepdims=True)
        v_own[1:2, cols] = jnp.sum(grad_v.astype(f32), axis=0, keepdims=True)

    def feed_chunk(u):
        group, i, slot = lax.div(u, 4), lax.rem(u, 4), lax.rem(u, 2)

        @pl.when((i == 0) & (group > 0))
        def _():
            sent(0, group - 1)
            sent(1, group - 1)

        for load in chunk_loads(u):
            load.wait()

        @pl.when(u == 0)
        def _():
            for load in f_loads[:3]:
                load.wait()

        @pl.when(u + 1 < 4 * groups)
        def _():
            for load in chunk_loads(u + 1):
                load.start()

        mine, p, shard = i >= 2, lax.rem(i, 2), shard_of(i)
        grad_hidden = dot(grad_ffn[...], chunk_w[slot, 0], ((1,), (1,)))
        grad_pre = (grad_hidden * pieces[slot, 1].astype(f32)).astype(bf16)
        cols = pl.ds(pl.multiple_of(group * tile, tile), tile)
        v_own[pl.ds(8 + shard, 1), cols] = jnp.sum(grad_pre.astype(f32), axis=0, keepdims=True)
        deliver(0, group, 0, p, mine, dot(pieces[slot, 0], grad_ffn[...], ((0,), (0,))).astype(bf16))
        deliver(1, group, 1, p, mine, dot(grad_pre, first_low[...], ((0,), (0,))).astype(bf16))

        acc[...] += dot(grad_pre, chunk_w[slot, 1], ((1,), (0,)))

    def norm_backward():
        sent(0, groups - 1)
        sent(1, groups - 1)
        for load in act_loads[:3]:
            load.start()
        f_loads[3].wait()
        v_own[2:3, :] = jnp.zeros((1, width), f32)
        v_own[4:6, :] = jnp.zeros((2, width), f32)

        def rows_of(r):
            grad, value = acc[r, :], before[r, :]
            center = value - jnp.mean(value, axis=-1, keepdims=True)
            spread = lax.rsqrt(jnp.mean(center * center, axis=-1, keepdims=True) + norm_eps)
            xhat = center * spread
            scaled = grad * gain_in[...].astype(f32).reshape(1, width)
            inner = scaled - jnp.mean(scaled, axis=-1, keepdims=True)
            result = spread * (inner - xhat * jnp.mean(scaled * xhat, axis=-1, keepdims=True))
            low = result.astype(bf16)
            acc[r, :] = result
            grads[2, r, :] = low
            v_own[2:3, :] += jnp.sum(low.astype(f32), axis=0, keepdims=True)
            v_own[4:5, :] += jnp.sum(grad * xhat, axis=0, keepdims=True)
            v_own[5:6, :] += jnp.sum(grad, axis=0, keepdims=True)

        _row_loop(slots, 32, rows_of)

    def term(m, left, right):
        def run(i, carry):
            rows = pl.ds(pl.multiple_of(shard_of(i) * tile, tile), tile)
            value = dot(left[:, rows], right[...], ((0,), (0,))).astype(bf16)
            deliver(None, m, m - 1 if not isinstance(m, int) or m else 0, lax.rem(i, 2), i >= 2, value)
            return carry

        lax.fori_loop(0, 4, run, 0)

    def out_backward():
        act_loads[3].wait()
        w_loads[0].wait()
        deliver_lane = grads.at[0]

        def run(i, carry):
            rows = pl.ds(pl.multiple_of(shard_of(i) * tile, tile), tile)
            value = dot(act[3, :, rows], grads[2], ((0,), (0,))).astype(bf16)
            p = lax.rem(i, 2)

            @pl.when(i < 2)
            def _():
                deliver_lane[pl.ds(pl.multiple_of(p * tile, tile), tile), :] = value
                for sub in range(subs):
                    k, at = slab_of(None, 0, sub)
                    src = deliver_lane.at[pl.ds(pl.multiple_of(p * tile + sub * part, part), part), :]
                    remote(src, core_in.at[k, p, pl.ds(at, part), :], c_s.at[k], c_r.at[k], core).start()

            @pl.when(i >= 2)
            def _():
                for sub in range(subs):
                    k, at = slab_of(None, 0, sub)
                    own[k, p, pl.ds(at, part)] = value[sub * part : (sub + 1) * part]

            return carry

        lax.fori_loop(0, 4, run, 0)

        def mix(r):
            act[3, r, :] = dot(grads[2, r, :], weights[0], ((1,), (1,))).astype(bf16)

        _row_loop(slots, 128, mix)
        w_loads[2].start()
        sent(None, 0)

    def resid_part(m):
        w_loads[m + 1].wait()

        def rows_of(r):
            value = acc[r, :] + dot(grads[m, r, :], weights[(m + 1) % 2], ((1,), (1,)))
            if m < 2:
                acc[r, :] = value
            else:
                grad_tokens[r, :] = value.astype(bf16)
                time_sum[...] += jnp.sum(value, axis=0, keepdims=True)

        _row_loop(slots, 128, rows_of)
        if m == 0:
            w_loads[3].start()

    v_half = v_core.shape[0]
    v_mine = pl.ds(pl.multiple_of(c * v_half, v_half), v_half)
    v_given = pl.ds(pl.multiple_of((1 - c) * v_half, v_half), v_half)

    def v_copy(i):
        peers = [core, across, side] + others + [core]
        if i == 0:
            src, dst = v_own.at[v_given], v_core
        elif i == 2 + nz:
            src = dst = vec_out.at[v_mine]
        else:
            src, dst = v_sum.at[min(i, 3) - 1], v_z.at[i - 2] if i > 2 else (v_y, v_x)[i - 1]
        return remote(src, dst, vs.at[i], vr.at[i], peers[i])

    def v_stage(i):
        if i == 0:
            v_copy(0).start()
        elif i <= 3:
            v_copy(i - 1).wait_recv()
            before = v_own[v_mine] if i == 1 else v_sum[i - 2]
            v_sum[i - 1] = before + (v_core, v_y, v_x)[i - 1][...]
            for j in range(i, i + 1 if i < 3 else 2 + nz):
                v_copy(j).start()
        elif i == 4:
            total = v_sum[2]
            for o in range(1, nz):
                v_copy(2 + o).wait_recv()
                total = total + v_z[o]
            vec_out[v_mine] = total
            v_copy(2 + nz).start()
        else:
            v_copy(2 + nz).wait_recv()

    def w_copy(q, i):
        peers = [across, side] + others + [core]
        if i == 0:
            part = rec_out.at[q, dp, y, c]
        elif i == 1:
            part = rec_out.at[q, dp, :, c]
        elif i < 1 + nz:
            part = rec_out.at[q, pl.ds(z * 2, 2), :, c]
        else:
            part = rec_out.at[q, :, :, c]
        return remote(part, part, ws.at[q, i], wr.at[q, i], peers[i])

    def w_stage(q, i):
        if i == 0:
            if q == 0:
                value = embed[...].astype(f32)
            else:
                value = time_sum[...].astype(bf16).astype(f32)
            lanes = rec_out.shape[-1]
            for j in range(width // lanes):
                rec_out[q, dp, y, c, j : j + 1, :] = value[:, j * lanes : (j + 1) * lanes]
            w_copy(q, 0).start()
        elif i < 3:
            w_copy(q, i - 1).wait_recv()
            for j in range(i, i + 1 if i == 1 else 1 + nz):
                w_copy(q, j).start()
        elif i == 3:
            for o in range(1, nz):
                w_copy(q, 1 + o).wait_recv()
            w_copy(q, 1 + nz).start()
        else:
            w_copy(q, 1 + nz).wait_recv()

    stages = [stage_y, stage_x, stage_z, stage_zg, stage_xg]
    feed = 4 * groups
    per = 2 * subs
    terms_at = feed + 4
    base = 4 if fine else terms_at + 3
    small = [(feed + 4 + at, functools.partial(v_stage, i)) for i, at in enumerate((0, 1, 4, 6, 8, 9))]
    for q, first in ((0, 2), (1, terms_at + 6)):
        small += [(first + at, functools.partial(w_stage, q, i)) for i, at in enumerate((0, 3, 5, 7, 8))]
    ticks = max([base + count + lag * (len(stages) - 1)] + [at + 1 for at, _ in small])
    bound = lengths[me] + BLOCK
    v_own[...] = vec[...]
    time_sum[...] = jnp.zeros_like(time_sum)

    def cores(start, stop):
        def run(k, carry):
            stage_core(k)
            return carry

        lax.fori_loop(start, stop, run, 0)

    def tick(t, carry):
        @pl.when(t < feed)
        def _():
            feed_chunk(t)

        @pl.when(t == feed)
        def _():
            norm_backward()

        @pl.when(t == feed + 1)
        def _():
            out_backward()
            for load in act_loads[:3]:
                load.wait()

        @pl.when((t > feed) & (t < terms_at))
        def _():
            done = 3 * (t - feed - 1)

            def run(p, carry):
                head_pair(p)
                return carry

            lax.fori_loop(done, jnp.minimum(done + 3, pairs), run, 0)

        @pl.when((t >= terms_at) & (t < terms_at + 3))
        def _():
            m = t - terms_at

            @pl.when(m == 0)
            def _():
                f_loads[4].start()
                f_loads[4].wait()

            term(m + 1, resid_low, grads.at[m])

        for m in range(3):

            @pl.when(t == terms_at + 3 + m)
            def _():
                resid_part(m)

        if fine:

            @pl.when((t < feed) & (lax.rem(t, 4) == 3))
            def _():
                start = lax.div(t, 4) * per
                cores(start, start + per)

            @pl.when((t == feed + 1) | ((t >= terms_at) & (t < terms_at + 3)))
            def _():
                start = given // slab + jnp.maximum(t - terms_at + 1, 0) * subs
                cores(start, start + subs)

        else:

            @pl.when(t == terms_at + 2)
            def _():
                cores(0, count)

        for d, stage in enumerate(stages):
            k = t - base - d * lag

            @pl.when((k >= 0) & (k < count))
            def _():
                stage(k)

        for at, run in small:
            pl.when(t == at)(run)

        return carry

    lax.fori_loop(0, ticks, tick, 0)
    for m in range(3):
        sent(None, m + 1)

    def finish(k, carry):
        x_copy(k).wait_send()
        for o in range(1, nz):
            z_copy(k, o).wait_send()
            zg_copy(k, o).wait_send()
        xg_copy(k).wait_send()
        out_copy(k).wait()
        return carry

    lax.fori_loop(0, count, finish, 0)
    for i in range(3 + nz):
        v_copy(i).wait_send()
    for i in range(2 + nz):
        for q in range(2):
            w_copy(q, i).wait_send()


def backward_and_reduce(dp_n, streams, inside_args):
    slots, units = streams[0].shape
    vec, embed = inside_args[-3:-1]
    width = vec.shape[1]
    tile = width // 4
    rows = 2 * units // 4 + 4 * tile
    slab = max(128, 16 * dp_n)
    count, nz = rows // slab, dp_n // 2
    bf16, f32 = jnp.bfloat16, jnp.float32
    dma, vmem = pltpu.SemaphoreType.DMA, pltpu.VMEM
    v_shape = vec.shape
    half_shape = (v_shape[0] // 2, width)
    anywhere, inside = pl.BlockSpec(memory_space=pl.ANY), pl.BlockSpec(memory_space=pltpu.VMEM)
    return pl.pallas_call(
        functools.partial(_backward_kernel, dp_n, slab, 1),
        out_shape=[
            jax.ShapeDtypeStruct((rows, width), bf16),
            jax.ShapeDtypeStruct(v_shape, f32),
            jax.ShapeDtypeStruct((2, dp_n, 2, 2, width // 128, 128), f32),
            jax.ShapeDtypeStruct((slots, width), bf16),
        ],
        in_specs=[anywhere] * len(streams)
        + [inside] * (len(inside_args) - 1)
        + [pl.BlockSpec(memory_space=pltpu.SMEM)],
        out_specs=[anywhere, inside, inside, inside],
        scratch_shapes=[
            vmem((count, 2, slab, width), bf16),
            vmem((count, 2, slab, width), bf16),
            vmem((count, slab, width), bf16),
            vmem((count, slab // 2, width), bf16),
            vmem((count, nz, slab // 2 // nz, width), bf16),
            vmem((4, slots, width), bf16),
            vmem((3, slots, width), bf16),
            vmem((2, width, width), bf16),
            vmem((2, 2, slots, tile), bf16),
            vmem((2, 2, tile, width), bf16),
            vmem((slots, width), f32),
            vmem((slots, width), f32),
            vmem((1, width), f32),
            vmem(v_shape, f32),
            vmem(half_shape, f32),
            vmem(half_shape, f32),
            vmem(half_shape, f32),
            vmem((nz,) + half_shape, f32),
            vmem((3,) + half_shape, f32),
        ]
        + [dma((2, 4)), dma((4,)), dma((4,)), dma((5,))]
        + [dma((count,))] * 6
        + [dma((count, nz))] * 4
        + [dma((count,))] * 3
        + [dma((3 + nz,))] * 2
        + [dma((2, 2 + nz))] * 2,
        compiler_params=pltpu.CompilerParams(collective_id=1, has_side_effects=True, vmem_limit_bytes=67_043_328),
        name="backward_and_reduce",
    )(*streams, *inside_args)


def _widen_kernel(plan, sums, *refs):
    outs, (low, high, load_sem, save_sem) = refs[: len(plan)], refs[len(plan) :]
    step = low.shape[1]
    blocks = [(out, off) for out, rows in zip(outs, plan) for off in range(0, rows, step)]

    def load(i):
        return pltpu.make_async_copy(sums.at[pl.ds(i * step, step), :], low.at[i % 4], load_sem.at[i % 4])

    def save(i):
        out, off = blocks[i]
        return pltpu.make_async_copy(high.at[i % 4], out.at[pl.ds(off, step), :], save_sem.at[i % 4])

    for i in range(min(3, len(blocks))):
        load(i).start()
    for i in range(len(blocks)):
        load(i).wait()
        if i + 3 < len(blocks):
            load(i + 3).start()
        if i >= 4:
            save(i - 4).wait()

        def widen(r):
            high[i % 4, r] = low[i % 4, r].astype(jnp.float32)

        _row_loop(step, 64, widen)
        save(i).start()
    for i in range(max(0, len(blocks) - 4), len(blocks)):
        save(i).wait()


def widen(sums, plan):
    width = sums.shape[1]
    step = 256
    anywhere = pl.BlockSpec(memory_space=pl.ANY)
    return pl.pallas_call(
        functools.partial(_widen_kernel, plan),
        out_shape=[jax.ShapeDtypeStruct((rows, width), jnp.float32) for rows in plan],
        in_specs=[anywhere],
        out_specs=[anywhere] * len(plan),
        scratch_shapes=[
            pltpu.VMEM((4, step, width), jnp.bfloat16),
            pltpu.VMEM((4, step, width), jnp.float32),
            pltpu.SemaphoreType.DMA((4,)),
            pltpu.SemaphoreType.DMA((4,)),
        ],
        compiler_params=pltpu.CompilerParams(vmem_limit_bytes=64 << 20),
        name="widen",
    )(sums)


def local(
    dp_n,
    tokens,
    time_embed,
    lengths,
    cotangent,
    w_query,
    w_key,
    w_value,
    w_out,
    w_time,
    w_in,
    w_down,
    b_query,
    b_value,
    b_out,
    b_time,
    b_in,
    b_down,
    gain_one,
    shift_one,
    gain_two,
    shift_two,
):
    f32, bf16 = jnp.float32, jnp.bfloat16
    seq_rank = lax.axis_index("seq")
    width = tokens.shape[1]
    rows = w_time.shape[0]

    def mm(a, b, dims):
        return lax.dot_general(a, b, (dims, ((), ())), preferred_element_type=f32)

    (
        _,
        full_query,
        full_key,
        full_value,
        full_out,
        full_in,
        full_down,
        resid_low,
        query_rows,
        key_rows,
        value_rows,
        mixed_rows,
        first_in,
        hidden_low,
        gelu_slope,
        grad_second_in,
        grad_ffn,
        first_low,
        log_total,
        layer_out,
        vec,
    ) = gather_and_forward(
        [w_time, w_query, w_key, w_value, w_out, w_in, w_down],
        tokens,
        time_embed,
        cotangent,
        lengths,
        [b_time, b_query, b_value, b_out, gain_one, shift_one, b_down, gain_two, shift_two, b_in],
    )
    sums, vectors, every, grad_tokens = backward_and_reduce(
        dp_n,
        [
            hidden_low,
            gelu_slope,
            full_down,
            full_in,
            grad_second_in,
            first_in,
            query_rows,
            key_rows,
            value_rows,
            mixed_rows,
            full_out,
            full_query,
            full_key,
            full_value,
            grad_ffn,
            first_low,
            resid_low,
        ],
        [log_total, gain_one, vec, time_embed, lengths],
    )
    time_rows, time_grads = every.reshape(2, -1, width).astype(bf16)
    own_columns = lax.dynamic_slice_in_dim(time_rows, seq_rank * rows, rows, 1)
    grad_w_time = mm(own_columns, time_grads, ((0,), (0,)))
    grad_b_time = jnp.sum(time_grads, axis=0, dtype=f32)
    grad_b_in = vectors[8 : 8 + b_in.shape[0] // width].reshape(-1)
    share_down, share_in, share_out, share_q, share_k, share_v = widen(
        sums, (w_in.shape[0], w_in.shape[0]) + (rows,) * 4
    )
    return (
        layer_out,
        grad_tokens,
        share_q,
        share_k,
        share_v,
        share_out,
        grad_w_time,
        share_in,
        share_down,
        vectors[0],
        vectors[1],
        vectors[2],
        grad_b_time,
        grad_b_in,
        vectors[3],
        vectors[4],
        vectors[5],
        vectors[6],
        vectors[7],
    )


def solution(mesh):
    in_specs = (
        P(("dp", "seq"), None),
        P(("dp", "seq"), None),
        P("dp"),
        P(("dp", "seq"), None),
        P("seq", None),
        P("seq", None),
        P("seq", None),
        P("seq", None),
        P("seq", None),
        P("seq", None),
        P("seq", None),
        P(),
        P(),
        P(),
        P(),
        P(),
        P(),
        P(),
        P(),
        P(),
        P(),
    )
    out_specs = (
        P(("dp", "seq"), None),
        P(("dp", "seq"), None),
        P("seq", None),
        P("seq", None),
        P("seq", None),
        P("seq", None),
        P("seq", None),
        P("seq", None),
        P("seq", None),
        P(),
        P(),
        P(),
        P(),
        P(),
        P(),
        P(),
        P(),
        P(),
        P(),
    )
    return jax.shard_map(functools.partial(local, mesh.shape["dp"]), mesh=mesh, in_specs=in_specs, out_specs=out_specs, check_vma=False)
```

```python
import functools

import jax
import jax.numpy as jnp
from jax import lax
from jax.experimental import pallas as pl
from jax.experimental.pallas import tpu as pltpu
from jax.sharding import PartitionSpec as P

HEAD_DIM = 64
BLOCK = 25
MESH = pl.DeviceIdType.MESH


norm_eps = 1e-05
neg_large = -1e30


def layer_norm(values, gain, shift):
    center = values - jnp.mean(values, axis=-1, keepdims=True)
    spread = lax.rsqrt(jnp.mean(center * center, axis=-1, keepdims=True) + norm_eps)
    return center * spread * gain + shift


def gelu_parts(values):
    half = 0.5 + 0.5 * lax.erf(values * 0.5**0.5)
    density = jnp.exp(-0.5 * values * values) * (0.5 / jnp.pi) ** 0.5
    return values * half, half + values * density


def _forward_kernel(sizes, *refs):
    n = len(sizes)
    given, (tokens, embed, cotangent, lengths) = refs[:n], refs[n : n + 4]
    biases, refs = refs[n + 4 : n + 14], refs[n + 14 :]
    outs = refs[:n]
    (resid_out, query_out, key_out, value_out, mixed_out, pre_out, hidden_out, slope_out, second_out) = refs[n : n + 9]
    grad_out, first_out, log_total, layer_out, vec = refs[n + 9 : n + 14]
    full = refs[n + 14 : 2 * n + 14]
    act, pre, first_low, hidden, slope, total, rows_in, bias_in = refs[2 * n + 14 : 2 * n + 22]
    load_sem, save_sem, act_sem, c_send, c_recv, y_send, y_recv, x_send, x_recv, f_send, f_recv, g_send, g_recv = refs[
        2 * n + 22 :
    ]
    f32, bf16 = jnp.float32, jnp.bfloat16
    w_time, w_query, w_key, w_value, w_out, w_in, w_down = full
    slots, width = tokens.shape
    pair = 2 * HEAD_DIM
    scale = HEAD_DIM**-0.5
    dp, me = lax.axis_index("dp"), lax.axis_index("seq")
    half = lax.rem(dp, 2)

    def home(a, shard):
        return full[a].at[pl.ds(pl.multiple_of(shard * sizes[a], sizes[a]), sizes[a]), :]

    loads = [pltpu.make_async_copy(given[a], home(a, me), load_sem.at[a]) for a in range(n)]
    for load in loads:
        load.start()
    core, across, side = (dp, me ^ 1), (dp, me ^ 2), (dp ^ 1, me)
    barrier = pltpu.get_barrier_semaphore()
    for peer in (core, across, side):
        pl.semaphore_signal(barrier, inc=1, device_id=peer, device_id_type=MESH)
    pl.semaphore_wait(barrier, 3)

    def remote(src, send, recv, peer):
        return pltpu.make_async_remote_copy(
            src_ref=src, dst_ref=src, send_sem=send, recv_sem=recv, device_id=peer, device_id_type=MESH
        )

    chunks, of = [], [[] for _ in sizes]
    for a, rows in enumerate(sizes):
        step = min(rows // 2, 128)
        for off in range(0, rows // 2, step):
            of[a].append(len(chunks))
            chunks.append((a, rows, off, step))

    def region(j, shard, part):
        a, rows, off, step = chunks[j]
        start = pl.multiple_of(shard * rows + part * (rows // 2) + off, 16)
        return full[a].at[pl.ds(start, step), :]

    saves = []

    def crossing(j):
        return remote(region(j, me, half), y_send.at[j], y_recv.at[j], across)

    def core_copy(a):
        return remote(home(a, me), c_send.at[a], c_recv.at[a], core)

    def sideways(j):
        return remote(region(j, me ^ 2, half), x_send.at[j], x_recv.at[j], side)

    def first_half(j):
        return remote(region(j, me ^ 2, half), f_send.at[j], f_recv.at[j], core)

    def second_half(j):
        return remote(region(j, me ^ 2, 1 - half), g_send.at[j], g_recv.at[j], core)

    for j, (a, rows, off, _) in enumerate(chunks):
        if off == 0:
            loads[a].wait()
            core_copy(a).start()
        crossing(j).start()

    def step(j):
        crossing(j).wait_recv()
        sideways(j).start()
        first_half(j).start()

    def turn(j):
        sideways(j).wait_recv()
        second_half(j).start()

    def arrived(j):
        first_half(j).wait_recv()
        second_half(j).wait_recv()

    def save(src, dst, sem):
        copy = pltpu.make_async_copy(src, dst, sem)
        copy.start()
        saves.append(copy)

    def complete(a):
        for j in of[a]:
            arrived(j)
        core_copy(a).wait_recv()
        save(full[a], outs[a], save_sem.at[a])

    def dot(a, b, dims):
        return lax.dot_general(a, b, (dims, ((), ())), preferred_element_type=f32)

    for i, ref in enumerate(biases[:9]):
        rows_in[i : i + 1, :] = ref[...].astype(f32).reshape(1, width)
    bias_in[...] = biases[9][...].astype(f32).reshape(bias_in.shape)
    bound = lengths[me] + BLOCK

    def bias(i):
        return rows_in[i : i + 1, :]

    tile = 256

    def tiles(extent, size, body):
        def run(i, carry):
            body(pl.ds(pl.multiple_of(i * size, size), size))
            return carry

        lax.fori_loop(0, extent // size, run, 0)

    def project(weight, i, row):
        def body(cols):
            value = dot(act[0], weight[:, cols], ((1,), (0,)))
            if row is not None:
                value += rows_in[row : row + 1, cols]
            act[i, :, cols] = value.astype(bf16)

        tiles(width, tile, body)
        save(act.at[i], (resid_out, query_out, key_out, value_out)[i], act_sem.at[i])

    step(0)
    step(1)
    turn(0)
    complete(0)
    wide = jnp.broadcast_to(embed[...].astype(f32), (16, width)).astype(bf16)
    time_proj = dot(wide, w_time[...], ((1,), (0,)))[0:1] + bias(0)

    def enter(r):
        value = tokens[r, :].astype(f32) + time_proj
        pre[r, :] = value
        act[0, r, :] = value.astype(bf16)

    tiles(slots, 64, enter)
    pltpu.make_async_copy(act.at[0], resid_out, act_sem.at[0]).start()
    for j, (weight, row) in enumerate(((w_query, 1), (w_key, None), (w_value, 2))):
        step(j + 2)
        turn(j + 1)
        complete(j + 1)
        project(weight, j + 1, row)

    first = lax.broadcasted_iota(jnp.int32, (1, pair), 1) < HEAD_DIM

    def head_pair(p):
        cols = pl.ds(pl.multiple_of(p * pair, pair), pair)
        q2, k2, v2 = (act[i, :, cols] for i in (1, 2, 3))
        kept = lax.broadcasted_iota(jnp.int32, (slots, 1), 0) < bound
        found = []
        for h in range(2):
            mask = jnp.where(first == (h == 0), scale, 0.0)
            scores = jnp.where(kept, dot(k2, q2 * mask.astype(bf16), ((1,), (1,))), neg_large)
            top = jnp.max(scores, axis=0, keepdims=True)
            weights = jnp.exp(scores - top)
            norm = jnp.sum(weights, axis=0, keepdims=True)
            soft = (weights * (1.0 / norm)).astype(bf16)
            log_total[pl.ds(2 * p + h, 1), :] = top + jnp.log(norm)
            found.append(dot(v2, soft, ((0,), (0,))))
        mixed = jnp.concatenate([found[0][:HEAD_DIM], found[1][HEAD_DIM:]], axis=0)
        act[4, :, cols] = mixed.T.astype(bf16)

    beside = {0: (None, 4), 1: (5, None), 3: (6, 5), 5: (7, 6), 7: (8, 7)}

    def attend(p, carry):
        for at, (enters, turns) in beside.items():

            @pl.when(p == at)
            def _():
                if enters is not None:
                    step(enters)
                if turns is not None:
                    turn(turns)

        head_pair(p)
        return carry

    lax.fori_loop(0, width // pair, attend, 0)
    save(act.at[4], mixed_out, act_sem.at[4])
    complete(4)

    def attn_out(cols):
        pre[:, cols] += dot(act[4], w_out[:, cols], ((1,), (0,))) + rows_in[3:4, cols]

    tiles(width, tile, attn_out)
    step(9)
    turn(8)
    save(pre, pre_out, act_sem.at[5])

    def norm_rows(r):
        first_low[r, :] = layer_norm(pre[r, :], bias(4), bias(5)).astype(bf16)

    tiles(slots, 32, norm_rows)
    save(first_low, first_out, act_sem.at[10])

    def feed_up(start, size):
        rows = pl.ds(pl.multiple_of(start, size), size)
        value = dot(first_low[...], w_in[rows, :], ((1,), (1,))) + bias_in[:, rows]
        up, lean = gelu_parts(value)
        hidden[:, rows] = up.astype(bf16)
        slope[:, rows] = lean.astype(bf16)

    share = sizes[5]

    def up_shard(shard):
        def run(i, carry):
            feed_up(shard * share + i * tile, tile)
            return carry

        lax.fori_loop(0, share // tile, run, 0)

    def down_shards(shards, opening):
        def body(cols):
            value = rows_in[6:7, cols] if opening else total[:, cols]
            for shard in shards:
                rows = pl.ds(pl.multiple_of(shard * share, share), share)
                value = value + dot(hidden[:, rows], w_down[rows, cols], ((1,), (0,)))
            total[:, cols] = value

        tiles(width, tile, body)

    def up_arrived(which):
        def run(i, carry):
            shard = (me ^ 2) ^ lax.rem(i, 2)
            feed_up(shard * share + lax.div(i, 2) * (share // 2) + which * tile, tile)
            return carry

        lax.fori_loop(0, 4, run, 0)

    up_shard(me)
    step(10)
    turn(9)
    core_copy(5).wait_recv()
    up_shard(me ^ 1)
    step(11)
    turn(10)
    core_copy(6).wait_recv()
    down_shards((me, me ^ 1), True)
    for j in (5, 6):
        arrived(j)
    up_arrived(0)
    step(12)
    turn(11)
    for j in (7, 8):
        arrived(j)
    save(w_in, outs[5], save_sem.at[5])
    up_arrived(1)
    turn(12)
    save(hidden, hidden_out, act_sem.at[6])
    save(slope, slope_out, act_sem.at[7])
    for j in of[6]:
        arrived(j)
    save(w_down, outs[6], save_sem.at[6])
    down_shards((me ^ 2, me ^ 3), False)
    pltpu.make_async_copy(act.at[0], resid_out, act_sem.at[0]).wait()
    vec[...] = jnp.zeros_like(vec)

    def second_rows(r):
        first_norm = layer_norm(pre[r, :], bias(4), bias(5))
        value = first_norm + total[r, :]
        center = value - jnp.mean(value, axis=-1, keepdims=True)
        spread = lax.rsqrt(jnp.mean(center * center, axis=-1, keepdims=True) + norm_eps)
        xhat = center * spread
        rows = r.start + lax.broadcasted_iota(jnp.int32, (r.size, 1), 0)
        valid = jnp.where(rows < bound, 1.0, 0.0)
        layer_out[r, :] = ((xhat * bias(7) + bias(8)) * valid).astype(bf16)
        grad = cotangent[r, :].astype(f32) * valid
        scaled = grad * bias(7)
        inner = scaled - jnp.mean(scaled, axis=-1, keepdims=True)
        result = spread * (inner - xhat * jnp.mean(scaled * xhat, axis=-1, keepdims=True))
        low = result.astype(bf16)
        total[r, :] = result
        act[0, r, :] = low
        vec[3:4, :] += jnp.sum(low.astype(f32), axis=0, keepdims=True)
        vec[6:7, :] += jnp.sum(grad * xhat, axis=0, keepdims=True)
        vec[7:8, :] += jnp.sum(grad, axis=0, keepdims=True)

    tiles(slots, 32, second_rows)
    save(total, second_out, act_sem.at[8])
    save(act.at[0], grad_out, act_sem.at[9])
    for copy in saves:
        copy.wait()
    for a in range(n):
        core_copy(a).wait_send()
    for j in range(len(chunks)):
        for copy in (crossing, sideways, first_half, second_half):
            copy(j).wait_send()


def gather_and_forward(arrays, tokens, embed, cotangent, lengths, biases):
    sizes = tuple(a.shape[0] for a in arrays)
    n = len(arrays)
    m = sum(max(1, r // 256) for r in sizes)
    slots, width = tokens.shape
    units = 4 * sizes[5]
    bf16, f32 = jnp.bfloat16, jnp.float32
    dma, vmem = pltpu.SemaphoreType.DMA, pltpu.VMEM
    anywhere, inside = pl.BlockSpec(memory_space=pl.ANY), pl.BlockSpec(memory_space=pltpu.VMEM)
    wide = jax.ShapeDtypeStruct((slots, width), bf16)
    wide_f32 = jax.ShapeDtypeStruct((slots, width), f32)
    return pl.pallas_call(
        functools.partial(_forward_kernel, sizes),
        out_shape=[jax.ShapeDtypeStruct((4 * a.shape[0], a.shape[1]), a.dtype) for a in arrays]
        + [wide] * 5
        + [wide_f32]
        + [jax.ShapeDtypeStruct((slots, units), bf16)] * 2
        + [wide_f32, wide, wide]
        + [
            jax.ShapeDtypeStruct((width // HEAD_DIM, slots), f32),
            wide,
            jax.ShapeDtypeStruct((8 + units // width + -units // width % 8, width), f32),
        ],
        in_specs=[anywhere] * n
        + [inside] * 3
        + [pl.BlockSpec(memory_space=pltpu.SMEM)]
        + [inside] * len(biases),
        out_specs=[anywhere] * (n + 11) + [inside] * 3,
        scratch_shapes=[vmem((4 * a.shape[0], a.shape[1]), a.dtype) for a in arrays]
        + [
            vmem((5, slots, width), bf16),
            vmem((slots, width), f32),
            vmem((slots, width), bf16),
            vmem((slots, units), bf16),
            vmem((slots, units), bf16),
            vmem((slots, width), f32),
            vmem((16, width), f32),
            vmem((1, units), f32),
        ]
        + [dma((n,)), dma((n,)), dma((11,))]
        + [dma((n,))] * 2
        + [dma((m,))] * 8,
        compiler_params=pltpu.CompilerParams(
            collective_id=0, has_side_effects=True, vmem_limit_bytes=66_000_000
        ),
        name="gather_and_forward",
    )(*arrays, tokens, embed, cotangent, lengths, *biases)


def _row_loop(rows, step, body):
    def run(i, carry):
        body(pl.ds(pl.multiple_of(i * step, step), step))
        return carry

    lax.fori_loop(0, rows // step, run, 0)


def _backward_kernel(dp_n, slab, lag, *refs):
    (hidden, slope, w_down, w_in, second, first_in, query, key, value, mixed, w_out, w_query, w_key, w_value) = refs[:14]
    (grad_ffn_in, first_low_in, resid_in, log_total, gain_in, vec, embed, lengths) = refs[14:22]
    out, vec_out, rec_out, grad_tokens = refs[22:26]
    (own, core_in, y_in, x_in, z_in, act, grads, weights, pieces, chunk_w, acc, before) = refs[26:38]
    (time_sum, v_own, v_core, v_y, v_x, v_z, v_sum) = refs[38:45]
    (piece_sem, act_sem, w_sem, f_sem, c_s, c_r, y_s, y_r, x_s, x_r, z_s, z_r, zg_s, zg_r, xg_s, xg_r, out_sem) = refs[45:62]
    vs, vr, ws, wr = refs[62:]
    f32, bf16 = jnp.float32, jnp.bfloat16
    count = out.shape[0] // slab
    nz = dp_n // 2
    scale = HEAD_DIM**-0.5
    slots, width = query.shape
    pair = 2 * HEAD_DIM
    pairs = width // pair
    share = w_in.shape[0] // 4
    tile = width // 4
    groups = share // tile
    fine = slab <= tile
    subs = tile // slab if fine else 1
    part = min(slab, tile)
    dp, me = lax.axis_index("dp"), lax.axis_index("seq")
    x, z, y, c = lax.rem(dp, 2), lax.div(dp, 2), lax.div(me, 2), lax.rem(me, 2)
    core, across, side = (dp, me ^ 1), (dp, me ^ 2), (dp ^ 1, me)
    others = [(lax.rem(z + o, nz) * 2 + x, me) for o in range(1, nz)]

    def shard_of(i):
        return lax.rem(i, 2) * 2 + lax.rem(1 - c + lax.div(i, 2), 2)

    def chunk_loads(u):
        start = pl.multiple_of(shard_of(lax.rem(u, 4)) * share + lax.div(u, 4) * tile, tile)
        rows, slot = pl.ds(start, tile), lax.rem(u, 2)
        return [
            pltpu.make_async_copy(hidden.at[:, rows], pieces.at[slot, 0], piece_sem.at[slot, 0]),
            pltpu.make_async_copy(slope.at[:, rows], pieces.at[slot, 1], piece_sem.at[slot, 1]),
            pltpu.make_async_copy(w_down.at[rows, :], chunk_w.at[slot, 0], piece_sem.at[slot, 2]),
            pltpu.make_async_copy(w_in.at[rows, :], chunk_w.at[slot, 1], piece_sem.at[slot, 3]),
        ]

    act_loads = [
        pltpu.make_async_copy(src, act.at[i], act_sem.at[i]) for i, src in enumerate((query, key, value, mixed))
    ]
    w_loads = [
        pltpu.make_async_copy(src, weights.at[i % 2], w_sem.at[i])
        for i, src in enumerate((w_out, w_query, w_key, w_value))
    ]
    grad_ffn, first_low, resid_low = act.at[2], grads.at[1], act.at[3]
    f_loads = [
        pltpu.make_async_copy(src, dst, f_sem.at[i])
        for i, (src, dst) in enumerate(
            ((grad_ffn_in, grad_ffn), (first_low_in, first_low), (second, acc), (first_in, before), (resid_in, resid_low))
        )
    ]
    for load in f_loads[:1] + chunk_loads(0) + f_loads[1:4] + [act_loads[3], w_loads[0], w_loads[1]]:
        load.start()
    barrier = pltpu.get_barrier_semaphore()
    for peer in [core, across, side] + others:
        pl.semaphore_signal(barrier, inc=1, device_id=peer, device_id_type=MESH)
    pl.semaphore_wait(barrier, 3 + len(others))

    def remote(src, dst, send, recv, peer):
        return pltpu.make_async_remote_copy(
            src_ref=src, dst_ref=dst, send_sem=send, recv_sem=recv, device_id=peer, device_id_type=MESH
        )

    hs = slab // 2
    ps = hs // nz
    rs = min(ps, 32)
    given = 2 * share

    def slab_of(mat, group, sub):
        if fine:
            return (group * 2 * subs + mat * subs if mat is not None else group * subs + given // slab) + sub, 0
        if mat is not None:
            return mat, pl.multiple_of(group * tile, tile)
        return given // slab, pl.multiple_of(group * tile, tile)

    def deliver(mat, group, lane, p, mine, value):
        @pl.when(jnp.logical_not(mine))
        def _():
            act[lane, pl.ds(pl.multiple_of(p * tile, tile), tile), :] = value
            for sub in range(subs):
                k, at = slab_of(mat, group, sub)
                src = act.at[lane, pl.ds(pl.multiple_of(p * tile + sub * part, part), part), :]
                remote(src, core_in.at[k, p, pl.ds(at, part), :], c_s.at[k], c_r.at[k], core).start()

        @pl.when(mine)
        def _():
            for sub in range(subs):
                k, at = slab_of(mat, group, sub)
                own[k, p, pl.ds(at, part)] = value[sub * part : (sub + 1) * part]

    def sent(mat, group):
        for sub in range(subs):
            k, at = slab_of(mat, group, sub)
            rows = core_in.at[k, :, pl.ds(at, part), :]
            remote(rows, rows, c_s.at[k], c_r.at[k], core).wait_send()

    def core_copy(k):
        return remote(core_in.at[k], core_in.at[k], c_s.at[k], c_r.at[k], core)

    def y_copy(k):
        return remote(own.at[k, 1 - y], y_in.at[k], y_s.at[k], y_r.at[k], across)

    def x_copy(k):
        give = pl.ds(pl.multiple_of((1 - x) * hs, 16), hs)
        return remote(own.at[k, y, give], x_in.at[k], x_s.at[k], x_r.at[k], side)

    hops = [1 << i for i in range(nz.bit_length() - 1)]

    def z_rows(i, bit):
        start = x * hs
        for j, d in enumerate(hops[: i + 1]):
            half = hs >> (j + 1)
            start += (bit if j == i else lax.rem(lax.div(z, d), 2)) * half
        return pl.ds(pl.multiple_of(start, 16), hs >> (i + 1))

    def z_bit(i):
        return lax.rem(lax.div(z, hops[i]), 2)

    def z_peer(i):
        return ((z ^ hops[i]) * 2 + x, me)

    def z_land(k, i):
        return z_in.at[k, pl.ds(hs - (hs >> i), hs >> (i + 1))]

    def z_copy(k, i):
        return remote(own.at[k, y, z_rows(i, 1 - z_bit(i))], z_land(k, i), z_s.at[k, i], z_r.at[k, i], z_peer(i))

    def zg_copy(k, i):
        mine = own.at[k, 1 - y, z_rows(i, z_bit(i))]
        return remote(mine, mine, zg_s.at[k, i], zg_r.at[k, i], z_peer(i))

    def xg_copy(k):
        mine = own.at[k, 1 - y, pl.ds(pl.multiple_of(x * hs, 16), hs)]
        return remote(mine, mine, xg_s.at[k], xg_r.at[k], side)

    def out_copy(k):
        start = k * slab
        if fine:
            mat, rest = lax.rem(lax.div(k, subs), 2), lax.div(k, 2 * subs) * tile + lax.rem(k, subs) * slab
            start = jnp.where(k < given // slab, mat * share + rest, start)
        rows = pl.ds(pl.multiple_of(start, slab), slab)
        return pltpu.make_async_copy(own.at[k, 1 - y], out.at[rows, :], out_sem.at[k])

    def stage_core(k):
        core_copy(k).wait_recv()

        def add(r):
            for p in range(2):
                own[k, p, r] = (own[k, p, r].astype(f32) + core_in[k, p, r].astype(f32)).astype(bf16)

        _row_loop(slab, 16, add)
        y_copy(k).start()

    def stage_y(k):
        y_copy(k).wait()

        def add(r):
            own[k, y, r] = (own[k, y, r].astype(f32) + y_in[k, r].astype(f32)).astype(bf16)

        _row_loop(slab, 32, add)
        x_copy(k).start()

    def stage_x(k):
        x_copy(k).wait_recv()

        def add(r):
            at = pl.ds(pl.multiple_of(x * hs + r.start, 16), r.size)
            own[k, y, at] = (own[k, y, at].astype(f32) + x_in[k, r].astype(f32)).astype(bf16)

        _row_loop(hs, rs, add)
        z_copy(k, 0).start()

    last = len(hops) - 1

    def stage_z(i, k):
        z_copy(k, i).wait_recv()
        rows = z_rows(i, z_bit(i))
        land = hs - (hs >> i)

        def add(r):
            at = pl.ds(pl.multiple_of(rows.start + r.start, 16), r.size)
            value = own[k, y, at].astype(f32) + z_in[k, pl.ds(pl.multiple_of(land + r.start, 16), r.size)].astype(f32)
            own[k, (1 - y) if i == last else y, at] = value.astype(bf16)

        _row_loop(rows.size, min(rows.size, 32), add)
        if i == last:
            zg_copy(k, i).start()
        else:
            z_copy(k, i + 1).start()

    def stage_zg(i, k):
        zg_copy(k, i).wait_recv()
        if i:
            zg_copy(k, i - 1).start()
        else:
            xg_copy(k).start()

    def stage_xg(k):
        xg_copy(k).wait_recv()
        out_copy(k).start()

    def dot(a, b, dims):
        return lax.dot_general(a, b, (dims, ((), ())), preferred_element_type=f32)

    def head_pair(p):
        cols = pl.ds(pl.multiple_of(p * pair, pair), pair)
        q2, k2, v2, g2 = (act[i, :, cols] for i in range(4))
        first = lax.broadcasted_iota(jnp.int32, (1, pair), 1) < HEAD_DIM
        kept = lax.broadcasted_iota(jnp.int32, (slots, 1), 0) < bound
        found = []
        for h in range(2):
            mask = jnp.where(first == (h == 0), 1.0, 0.0)
            q_h = q2 * (mask * scale).astype(bf16)
            g_h = g2 * mask.astype(bf16)
            scores = dot(k2, q_h, ((1,), (1,)))
            soft = jnp.where(kept, jnp.exp(scores - log_total[pl.ds(2 * p + h, 1), :]), 0.0)
            grad_soft = dot(v2, g_h, ((1,), (1,)))
            inner = jnp.sum(soft * grad_soft, axis=0, keepdims=True)
            grad_scores = (soft * (grad_soft - inner)).astype(bf16)
            found.append(
                (
                    dot(k2, grad_scores, ((0,), (0,))),
                    dot(grad_scores, q2, ((1,), (0,))),
                    dot(soft.astype(bf16), g2, ((1,), (0,))),
                )
            )
        q_t = jnp.concatenate([found[0][0][:HEAD_DIM], found[1][0][HEAD_DIM:]], axis=0)
        grad_q = (q_t.T * scale).astype(bf16)
        grad_k = (jnp.where(first, found[0][1], found[1][1]) * scale).astype(bf16)
        grad_v = jnp.where(first, found[0][2], found[1][2]).astype(bf16)
        grads[0, :, cols] = grad_q
        grads[1, :, cols] = grad_k
        grads[2, :, cols] = grad_v
        v_own[0:1, cols] = jnp.sum(grad_q.astype(f32), axis=0, keepdims=True)
        v_own[1:2, cols] = jnp.sum(grad_v.astype(f32), axis=0, keepdims=True)

    def feed_chunk(u):
        group, i, slot = lax.div(u, 4), lax.rem(u, 4), lax.rem(u, 2)

        @pl.when((i == 0) & (group > 0))
        def _():
            sent(0, group - 1)
            sent(1, group - 1)

        for load in chunk_loads(u):
            load.wait()

        @pl.when(u == 0)
        def _():
            for load in f_loads[:3]:
                load.wait()

        @pl.when(u + 1 < 4 * groups)
        def _():
            for load in chunk_loads(u + 1):
                load.start()

        mine, p, shard = i >= 2, lax.rem(i, 2), shard_of(i)
        grad_hidden = dot(grad_ffn[...], chunk_w[slot, 0], ((1,), (1,)))
        grad_pre = (grad_hidden * pieces[slot, 1].astype(f32)).astype(bf16)
        cols = pl.ds(pl.multiple_of(group * tile, tile), tile)
        v_own[pl.ds(8 + shard, 1), cols] = jnp.sum(grad_pre.astype(f32), axis=0, keepdims=True)
        deliver(0, group, 0, p, mine, dot(pieces[slot, 0], grad_ffn[...], ((0,), (0,))).astype(bf16))
        deliver(1, group, 1, p, mine, dot(grad_pre, first_low[...], ((0,), (0,))).astype(bf16))

        acc[...] += dot(grad_pre, chunk_w[slot, 1], ((1,), (0,)))

    def norm_backward():
        sent(0, groups - 1)
        sent(1, groups - 1)
        for load in act_loads[:3]:
            load.start()
        f_loads[3].wait()
        v_own[2:3, :] = jnp.zeros((1, width), f32)
        v_own[4:6, :] = jnp.zeros((2, width), f32)

        def rows_of(r):
            grad, value = acc[r, :], before[r, :]
            center = value - jnp.mean(value, axis=-1, keepdims=True)
            spread = lax.rsqrt(jnp.mean(center * center, axis=-1, keepdims=True) + norm_eps)
            xhat = center * spread
            scaled = grad * gain_in[...].astype(f32).reshape(1, width)
            inner = scaled - jnp.mean(scaled, axis=-1, keepdims=True)
            result = spread * (inner - xhat * jnp.mean(scaled * xhat, axis=-1, keepdims=True))
            low = result.astype(bf16)
            acc[r, :] = result
            grads[2, r, :] = low
            v_own[2:3, :] += jnp.sum(low.astype(f32), axis=0, keepdims=True)
            v_own[4:5, :] += jnp.sum(grad * xhat, axis=0, keepdims=True)
            v_own[5:6, :] += jnp.sum(grad, axis=0, keepdims=True)

        _row_loop(slots, 32, rows_of)

    def term(m, left, right):
        def run(i, carry):
            rows = pl.ds(pl.multiple_of(shard_of(i) * tile, tile), tile)
            value = dot(left[:, rows], right[...], ((0,), (0,))).astype(bf16)
            deliver(None, m, m - 1 if not isinstance(m, int) or m else 0, lax.rem(i, 2), i >= 2, value)
            return carry

        lax.fori_loop(0, 4, run, 0)

    def out_backward():
        act_loads[3].wait()
        w_loads[0].wait()
        deliver_lane = grads.at[0]

        def run(i, carry):
            rows = pl.ds(pl.multiple_of(shard_of(i) * tile, tile), tile)
            value = dot(act[3, :, rows], grads[2], ((0,), (0,))).astype(bf16)
            p = lax.rem(i, 2)

            @pl.when(i < 2)
            def _():
                deliver_lane[pl.ds(pl.multiple_of(p * tile, tile), tile), :] = value
                for sub in range(subs):
                    k, at = slab_of(None, 0, sub)
                    src = deliver_lane.at[pl.ds(pl.multiple_of(p * tile + sub * part, part), part), :]
                    remote(src, core_in.at[k, p, pl.ds(at, part), :], c_s.at[k], c_r.at[k], core).start()

            @pl.when(i >= 2)
            def _():
                for sub in range(subs):
                    k, at = slab_of(None, 0, sub)
                    own[k, p, pl.ds(at, part)] = value[sub * part : (sub + 1) * part]

            return carry

        lax.fori_loop(0, 4, run, 0)

        def mix(r):
            act[3, r, :] = dot(grads[2, r, :], weights[0], ((1,), (1,))).astype(bf16)

        _row_loop(slots, 128, mix)
        w_loads[2].start()
        sent(None, 0)

    def resid_part(m):
        w_loads[m + 1].wait()

        def rows_of(r):
            value = acc[r, :] + dot(grads[m, r, :], weights[(m + 1) % 2], ((1,), (1,)))
            if m < 2:
                acc[r, :] = value
            else:
                grad_tokens[r, :] = value.astype(bf16)
                time_sum[...] += jnp.sum(value, axis=0, keepdims=True)

        _row_loop(slots, 128, rows_of)
        if m == 0:
            w_loads[3].start()

    v_half = v_core.shape[0]
    v_mine = pl.ds(pl.multiple_of(c * v_half, v_half), v_half)
    v_given = pl.ds(pl.multiple_of((1 - c) * v_half, v_half), v_half)

    def v_copy(i):
        peers = [core, across, side] + others + [core]
        if i == 0:
            src, dst = v_own.at[v_given], v_core
        elif i == 2 + nz:
            src = dst = vec_out.at[v_mine]
        else:
            src, dst = v_sum.at[min(i, 3) - 1], v_z.at[i - 2] if i > 2 else (v_y, v_x)[i - 1]
        return remote(src, dst, vs.at[i], vr.at[i], peers[i])

    def v_stage(i):
        if i == 0:
            v_copy(0).start()
        elif i <= 3:
            v_copy(i - 1).wait_recv()
            before = v_own[v_mine] if i == 1 else v_sum[i - 2]
            v_sum[i - 1] = before + (v_core, v_y, v_x)[i - 1][...]
            for j in range(i, i + 1 if i < 3 else 2 + nz):
                v_copy(j).start()
        elif i == 4:
            total = v_sum[2]
            for o in range(1, nz):
                v_copy(2 + o).wait_recv()
                total = total + v_z[o]
            vec_out[v_mine] = total
            v_copy(2 + nz).start()
        else:
            v_copy(2 + nz).wait_recv()

    def w_copy(q, i):
        peers = [across, side] + others + [core]
        if i == 0:
            part = rec_out.at[q, dp, y, c]
        elif i == 1:
            part = rec_out.at[q, dp, :, c]
        elif i < 1 + nz:
            part = rec_out.at[q, pl.ds(z * 2, 2), :, c]
        else:
            part = rec_out.at[q, :, :, c]
        return remote(part, part, ws.at[q, i], wr.at[q, i], peers[i])

    def w_stage(q, i):
        if i == 0:
            if q == 0:
                value = embed[...].astype(f32)
            else:
                value = time_sum[...].astype(bf16).astype(f32)
            lanes = rec_out.shape[-1]
            for j in range(width // lanes):
                rec_out[q, dp, y, c, j : j + 1, :] = value[:, j * lanes : (j + 1) * lanes]
            w_copy(q, 0).start()
        elif i < 3:
            w_copy(q, i - 1).wait_recv()
            for j in range(i, i + 1 if i == 1 else 1 + nz):
                w_copy(q, j).start()
        elif i == 3:
            for o in range(1, nz):
                w_copy(q, 1 + o).wait_recv()
            w_copy(q, 1 + nz).start()
        else:
            w_copy(q, 1 + nz).wait_recv()

    stages = [stage_y, stage_x]
    stages += [functools.partial(stage_z, i) for i in range(len(hops))]
    stages += [functools.partial(stage_zg, i) for i in reversed(range(len(hops)))]
    stages += [stage_xg]
    feed = 4 * groups
    per = 2 * subs
    terms_at = feed + 4
    base = 4 if fine else terms_at + 3
    small = [(feed + 4 + at, functools.partial(v_stage, i)) for i, at in enumerate((0, 1, 4, 6, 8, 9))]
    for q, first in ((0, 2), (1, terms_at + 3)):
        small += [(first + at, functools.partial(w_stage, q, i)) for i, at in enumerate((0, 3, 5, 7, 8))]
    ticks = max([base + count + lag * (len(stages) - 1)] + [at + 1 for at, _ in small])
    bound = lengths[me] + BLOCK
    v_own[...] = vec[...]
    time_sum[...] = jnp.zeros_like(time_sum)

    def cores(start, stop):
        def run(k, carry):
            stage_core(k)
            return carry

        lax.fori_loop(start, stop, run, 0)

    def tick(t, carry):
        @pl.when(t < feed)
        def _():
            feed_chunk(t)

        @pl.when(t == feed)
        def _():
            norm_backward()

        @pl.when(t == feed + 1)
        def _():
            out_backward()
            for load in act_loads[:3]:
                load.wait()

        @pl.when((t > feed) & (t < terms_at))
        def _():
            done = 3 * (t - feed - 1)

            def run(p, carry):
                head_pair(p)
                return carry

            lax.fori_loop(done, jnp.minimum(done + 3, pairs), run, 0)

        @pl.when((t >= terms_at) & (t < terms_at + 3))
        def _():
            m = t - terms_at

            @pl.when(m == 0)
            def _():
                f_loads[4].start()
                f_loads[4].wait()

            term(m + 1, resid_low, grads.at[m])

        for m in range(3):

            @pl.when(t == terms_at + m)
            def _():
                resid_part(m)

        if fine:

            @pl.when((t < feed) & (lax.rem(t, 4) == 3))
            def _():
                start = lax.div(t, 4) * per
                cores(start, start + per)

            @pl.when((t == feed + 1) | ((t >= terms_at) & (t < terms_at + 3)))
            def _():
                start = given // slab + jnp.maximum(t - terms_at + 1, 0) * subs
                cores(start, start + subs)

        else:

            @pl.when(t == terms_at + 2)
            def _():
                cores(0, count)

        for d, stage in enumerate(stages):
            k = t - base - d * lag

            @pl.when((k >= 0) & (k < count))
            def _():
                stage(k)

        for at, run in small:
            pl.when(t == at)(run)

        return carry

    lax.fori_loop(0, ticks, tick, 0)
    for m in range(3):
        sent(None, m + 1)

    def finish(k, carry):
        x_copy(k).wait_send()
        for i in range(len(hops)):
            z_copy(k, i).wait_send()
            zg_copy(k, i).wait_send()
        xg_copy(k).wait_send()
        out_copy(k).wait()
        return carry

    lax.fori_loop(0, count, finish, 0)
    for i in range(3 + nz):
        v_copy(i).wait_send()
    for i in range(2 + nz):
        for q in range(2):
            w_copy(q, i).wait_send()


def backward_and_reduce(dp_n, streams, inside_args):
    slots, units = streams[0].shape
    vec, embed = inside_args[-3:-1]
    width = vec.shape[1]
    tile = width // 4
    rows = 2 * units // 4 + 4 * tile
    slab = max(128, 16 * dp_n)
    count, nz = rows // slab, dp_n // 2
    bf16, f32 = jnp.bfloat16, jnp.float32
    dma, vmem = pltpu.SemaphoreType.DMA, pltpu.VMEM
    v_shape = vec.shape
    half_shape = (v_shape[0] // 2, width)
    anywhere, inside = pl.BlockSpec(memory_space=pl.ANY), pl.BlockSpec(memory_space=pltpu.VMEM)
    return pl.pallas_call(
        functools.partial(_backward_kernel, dp_n, slab, 1),
        out_shape=[
            jax.ShapeDtypeStruct((rows, width), bf16),
            jax.ShapeDtypeStruct(v_shape, f32),
            jax.ShapeDtypeStruct((2, dp_n, 2, 2, width // 128, 128), f32),
            jax.ShapeDtypeStruct((slots, width), bf16),
        ],
        in_specs=[anywhere] * len(streams)
        + [inside] * (len(inside_args) - 1)
        + [pl.BlockSpec(memory_space=pltpu.SMEM)],
        out_specs=[anywhere, inside, inside, inside],
        scratch_shapes=[
            vmem((count, 2, slab, width), bf16),
            vmem((count, 2, slab, width), bf16),
            vmem((count, slab, width), bf16),
            vmem((count, slab // 2, width), bf16),
            vmem((count, slab // 2, width), bf16),
            vmem((4, slots, width), bf16),
            vmem((3, slots, width), bf16),
            vmem((2, width, width), bf16),
            vmem((2, 2, slots, tile), bf16),
            vmem((2, 2, tile, width), bf16),
            vmem((slots, width), f32),
            vmem((slots, width), f32),
            vmem((1, width), f32),
            vmem(v_shape, f32),
            vmem(half_shape, f32),
            vmem(half_shape, f32),
            vmem(half_shape, f32),
            vmem((nz,) + half_shape, f32),
            vmem((3,) + half_shape, f32),
        ]
        + [dma((2, 4)), dma((4,)), dma((4,)), dma((5,))]
        + [dma((count,))] * 6
        + [dma((count, max(1, nz.bit_length() - 1)))] * 4
        + [dma((count,))] * 3
        + [dma((3 + nz,))] * 2
        + [dma((2, 2 + nz))] * 2,
        compiler_params=pltpu.CompilerParams(collective_id=1, has_side_effects=True, vmem_limit_bytes=67_043_328),
        name="backward_and_reduce",
    )(*streams, *inside_args)


def _widen_kernel(plan, sums, *refs):
    outs, (low, high, load_sem, save_sem) = refs[: len(plan)], refs[len(plan) :]
    step = low.shape[1]
    blocks = [(out, off) for out, rows in zip(outs, plan) for off in range(0, rows, step)]

    def load(i):
        return pltpu.make_async_copy(sums.at[pl.ds(i * step, step), :], low.at[i % 4], load_sem.at[i % 4])

    def save(i):
        out, off = blocks[i]
        return pltpu.make_async_copy(high.at[i % 4], out.at[pl.ds(off, step), :], save_sem.at[i % 4])

    for i in range(min(3, len(blocks))):
        load(i).start()
    for i in range(len(blocks)):
        load(i).wait()
        if i + 3 < len(blocks):
            load(i + 3).start()
        if i >= 4:
            save(i - 4).wait()

        def widen(r):
            high[i % 4, r] = low[i % 4, r].astype(jnp.float32)

        _row_loop(step, 64, widen)
        save(i).start()
    for i in range(max(0, len(blocks) - 4), len(blocks)):
        save(i).wait()


def widen(sums, plan):
    width = sums.shape[1]
    step = 256
    anywhere = pl.BlockSpec(memory_space=pl.ANY)
    return pl.pallas_call(
        functools.partial(_widen_kernel, plan),
        out_shape=[jax.ShapeDtypeStruct((rows, width), jnp.float32) for rows in plan],
        in_specs=[anywhere],
        out_specs=[anywhere] * len(plan),
        scratch_shapes=[
            pltpu.VMEM((4, step, width), jnp.bfloat16),
            pltpu.VMEM((4, step, width), jnp.float32),
            pltpu.SemaphoreType.DMA((4,)),
            pltpu.SemaphoreType.DMA((4,)),
        ],
        compiler_params=pltpu.CompilerParams(vmem_limit_bytes=64 << 20),
        name="widen",
    )(sums)


def local(
    dp_n,
    tokens,
    time_embed,
    lengths,
    cotangent,
    w_query,
    w_key,
    w_value,
    w_out,
    w_time,
    w_in,
    w_down,
    b_query,
    b_value,
    b_out,
    b_time,
    b_in,
    b_down,
    gain_one,
    shift_one,
    gain_two,
    shift_two,
):
    f32, bf16 = jnp.float32, jnp.bfloat16
    seq_rank = lax.axis_index("seq")
    width = tokens.shape[1]
    rows = w_time.shape[0]

    def mm(a, b, dims):
        return lax.dot_general(a, b, (dims, ((), ())), preferred_element_type=f32)

    (
        _,
        full_query,
        full_key,
        full_value,
        full_out,
        full_in,
        full_down,
        resid_low,
        query_rows,
        key_rows,
        value_rows,
        mixed_rows,
        first_in,
        hidden_low,
        gelu_slope,
        grad_second_in,
        grad_ffn,
        first_low,
        log_total,
        layer_out,
        vec,
    ) = gather_and_forward(
        [w_time, w_query, w_key, w_value, w_out, w_in, w_down],
        tokens,
        time_embed,
        cotangent,
        lengths,
        [b_time, b_query, b_value, b_out, gain_one, shift_one, b_down, gain_two, shift_two, b_in],
    )
    sums, vectors, every, grad_tokens = backward_and_reduce(
        dp_n,
        [
            hidden_low,
            gelu_slope,
            full_down,
            full_in,
            grad_second_in,
            first_in,
            query_rows,
            key_rows,
            value_rows,
            mixed_rows,
            full_out,
            full_query,
            full_key,
            full_value,
            grad_ffn,
            first_low,
            resid_low,
        ],
        [log_total, gain_one, vec, time_embed, lengths],
    )
    time_rows, time_grads = every.reshape(2, -1, width).astype(bf16)
    own_columns = lax.dynamic_slice_in_dim(time_rows, seq_rank * rows, rows, 1)
    grad_w_time = mm(own_columns, time_grads, ((0,), (0,)))
    grad_b_time = jnp.sum(time_grads, axis=0, dtype=f32)
    grad_b_in = vectors[8 : 8 + b_in.shape[0] // width].reshape(-1)
    share_down, share_in, share_out, share_q, share_k, share_v = widen(
        sums, (w_in.shape[0], w_in.shape[0]) + (rows,) * 4
    )
    return (
        layer_out,
        grad_tokens,
        share_q,
        share_k,
        share_v,
        share_out,
        grad_w_time,
        share_in,
        share_down,
        vectors[0],
        vectors[1],
        vectors[2],
        grad_b_time,
        grad_b_in,
        vectors[3],
        vectors[4],
        vectors[5],
        vectors[6],
        vectors[7],
    )


def solution(mesh):
    in_specs = (
        P(("dp", "seq"), None),
        P(("dp", "seq"), None),
        P("dp"),
        P(("dp", "seq"), None),
        P("seq", None),
        P("seq", None),
        P("seq", None),
        P("seq", None),
        P("seq", None),
        P("seq", None),
        P("seq", None),
        P(),
        P(),
        P(),
        P(),
        P(),
        P(),
        P(),
        P(),
        P(),
        P(),
    )
    out_specs = (
        P(("dp", "seq"), None),
        P(("dp", "seq"), None),
        P("seq", None),
        P("seq", None),
        P("seq", None),
        P("seq", None),
        P("seq", None),
        P("seq", None),
        P("seq", None),
        P(),
        P(),
        P(),
        P(),
        P(),
        P(),
        P(),
        P(),
        P(),
        P(),
    )
    return jax.shard_map(functools.partial(local, mesh.shape["dp"]), mesh=mesh, in_specs=in_specs, out_specs=out_specs, check_vma=False)
```
